32 devices in a mesh: node: 4 (over y, core), cores: 8 (over z, x).
Axes of the slice: x: 2, y: 2, z: 4, core: 2. Of those that a mesh axis runs over, the one named last changes fastest.
Arguments:
- adjoint: bfloat16 [256, 2, 128, 128], P(('node', 'cores')), may hold values from -6 to 6
- saved: bfloat16 [2, 4, 256, 2, 128, 128], P(None, None, ('node', 'cores')), may hold values from -0.046875 to 0.046875
- propagators: bfloat16 [2, 4, 2, 128, 128], replicated, may hold values from -3 to 3, as said below
- coupling: bfloat16 [128, 128], replicated, may hold values from -0.5 to 0.5
- higher: int32 [256, 4], replicated, may hold values from 0 to 255, as said below
- lower: int32 [256, 4], replicated, may hold values from 0 to 255, as said below
- ladder: int32 [2, 256, 4], P(None, ('node', 'cores')), may hold values from 0 to 3
- rates: float32 [2, 4], replicated, may hold values from 0.1 to 0.4
- decay: float32 [256], P(('node', 'cores')), may hold values from 0.4 to 1
Outputs:
- adjoint_out: bfloat16 [256, 2, 128, 128], P(('node', 'cores'))
- gradient: float32 [128, 8, 2, 128], P(('node', 'cores'))
The draws below stay inside these ranges and needn't reach their ends.
Inputs may be any that keep to these rules, and one draw needn't show every extreme that they name: Density j lives on owner j // 8. Taken in the order of density then mode, the 32 higher-tier partners of one owner's densities lie on distinct owners when 8 * 4 <= 32, and else exactly 1 of them lie on each owner. The same holds for the lower-tier partners. `propagators`: A propagator substep is close to unitary.
All inputs are finite; a program needn't handle non-finite values.
Results may differ from the reference program's by a relative error of at most 0.024.
Values may be sent and summed in bfloat16 or wider, within the bound.
A program may use at most 128 MiB of HBM per device.

```python
import math
import jax
import jax.numpy as jnp

DIM = 128
MODES = 4
ADO_DEV = 8
STEPS = 2
NSUB = 4
OWNERS = 32
NA = 256


def build_partners(key):
    links = ADO_DEV * MODES
    perm_key = jax.random.fold_in(key, 11)
    local_key = jax.random.fold_in(key, 12)
    perms = jax.vmap(lambda owner_id: jax.random.permutation(jax.random.fold_in(perm_key, owner_id), OWNERS))(jnp.arange(OWNERS))
    source = perms[:, jnp.arange(links) % OWNERS]
    local = jax.random.randint(local_key, (OWNERS, links), 0, ADO_DEV)
    return (source * ADO_DEV + local).reshape(OWNERS * ADO_DEV, MODES).astype(jnp.int32)


def draw_higher(key, part):
    return build_partners(jax.random.fold_in(key, 1))


def draw_lower(key, part):
    return build_partners(jax.random.fold_in(key, 2))


def draw_propagators(key, part):
    scale = 0.4 / DIM ** 0.5
    raw = jax.random.normal(key, (STEPS, NSUB, DIM, DIM), jnp.float32) * scale
    hermit = (raw + jnp.swapaxes(raw, -1, -2)) / 2.0 ** 0.5
    square = jnp.matmul(hermit, hermit)
    cube = jnp.matmul(square, hermit)
    identity = jnp.eye(DIM, dtype=jnp.float32)
    real_part = identity - 0.5 * square
    imag_part = -hermit + cube / 6.0
    return jnp.stack([real_part, imag_part], axis=2).astype(jnp.bfloat16)


def set_ends(values, own_key, least, high):
    extent = values.shape
    index_at = [jax.random.randint(jax.random.fold_in(own_key, axis), (), 0, extent[axis]) for axis in range(len(extent))]
    values = values.at[tuple(index_at)].set(least)
    longest = extent.index(max(extent))
    index_at[longest] = (index_at[longest] + 1) % extent[longest]
    return values.at[tuple(index_at)].set(high)


def with_spikes(array, rng, source, target, parts, factor):
    def block_of(position):
        return (jnp.arange(array.shape[position]) // (array.shape[position] // parts)).reshape((-1,) + (1,) * (array.ndim - 1 - position))

    first = jax.random.permutation(rng, parts)[block_of(target)]
    other_side = (block_of(target) + parts // 2) % parts
    return jnp.where((block_of(source) == first) | (block_of(source) == other_side), factor * array, array)


def level_of(key, extent, pieces, smallest, high):
    gain = 1.0
    for position, blocks in pieces:
        draws = jax.random.uniform(jax.random.fold_in(jax.random.fold_in(key, 6), position), (blocks,), jnp.float32, smallest / len(pieces), high / len(pieces))
        gain = gain * jnp.repeat(jnp.exp(draws), extent[position] // blocks).reshape((-1,) + (1,) * (len(extent) - 1 - position))
    return gain


def centred(rng, shape, deviation, bound, pieces=(), kind=jnp.bfloat16):
    gain = level_of(rng, shape, pieces, -0.22, 0.18) if pieces else 1.0
    drawn = jax.random.normal(rng, shape, jnp.float32) * deviation * gain
    return jnp.minimum(jnp.maximum(drawn, -bound), bound).astype(kind)


def gaussian_with(own_key, shape, width, limit, pieces, heavy, kind=jnp.bfloat16):
    entries = width * jax.random.normal(own_key, shape, jnp.float32)
    if pieces:
        entries = entries * level_of(own_key, shape, pieces, -0.22, 0.18)
    return jnp.clip(with_spikes(entries, jax.random.fold_in(own_key, 3), *heavy), -limit, limit).astype(kind)


def setup_inputs(seed: int = 0) -> dict:
    key_list = jax.random.split(jax.random.key(seed), 10)
    return {
        "adjoint": centred(key_list[0], (NA, 2, DIM, DIM), 1.0, 6.0, ((0, 32),)),
        "saved": gaussian_with(key_list[1], (STEPS, NSUB, NA, 2, DIM, DIM), (1.0 / (2 * DIM * NA) ** 0.5), 0.046875, ((2, 32),), (2, 5, 32, 2.75)),
        "propagators": draw_propagators(jax.random.fold_in(key_list[9], 71), 0),
        "coupling": centred(key_list[3], (DIM, DIM), DIM ** -0.5, 0.5),
        "higher": draw_higher(jax.random.fold_in(key_list[9], 71), 0),
        "lower": draw_lower(jax.random.fold_in(key_list[9], 71), 0),
        "ladder": set_ends(jax.random.randint(key_list[6], (2, NA, MODES), 0, 4), jax.random.fold_in(key_list[6], 1), 0, 3).astype(jnp.int32),
        "rates": jnp.clip(jnp.exp(jax.random.uniform(key_list[7], (2, MODES), jnp.float32, math.log(0.1), math.log(0.4))), 0.1, 0.4),
        "decay": jnp.clip(0.4 + 0.6 * jax.random.uniform(key_list[8], (NA,), jnp.float32) ** level_of(key_list[8], (NA,), ((0, 32),), -0.2, 0.2), 0.4, 1.0),
    }


def linked_sum(state_full, link_table, weights, strengths):
    total = jnp.zeros(state_full.shape, jnp.float32)
    for mode_index in range(MODES):
        factor = weights[:, mode_index].astype(jnp.float32) * strengths[mode_index]
        total = total + factor[:, None, None, None] * state_full[link_table[:, mode_index]]
    return total


def couple_step(state, up_sum, down_sum, coupling, decay):
    plus = (up_sum + down_sum).astype(jnp.bfloat16).astype(jnp.float32)
    minus = (up_sum - down_sum).astype(jnp.bfloat16).astype(jnp.float32)
    operator = coupling.astype(jnp.float32)
    left = jnp.einsum('ab,jxbc->jxac', operator, plus)
    right = jnp.einsum('jxab,bc->jxac', minus, operator)
    kept = decay[:, None, None, None] * state.astype(jnp.float32)
    real_part = kept[:, 0] + left[:, 1] - right[:, 1]
    imag_part = kept[:, 1] - left[:, 0] + right[:, 0]
    return jnp.stack([real_part, imag_part], axis=1).astype(jnp.bfloat16)


def rotate_step(state, prop_re, prop_im):
    state_f = state.astype(jnp.float32)
    real_u = prop_re.astype(jnp.float32)
    imag_u = prop_im.astype(jnp.float32)
    times_re = jnp.einsum('jxab,bc->jxac', state_f, real_u)
    times_im = jnp.einsum('jxab,bc->jxac', state_f, imag_u)
    middle = jnp.stack([times_re[:, 0] - times_im[:, 1], times_im[:, 0] + times_re[:, 1]], axis=1)
    middle = middle.astype(jnp.bfloat16).astype(jnp.float32)
    left_re = jnp.einsum('ba,jxbc->jxac', real_u, middle)
    left_im = jnp.einsum('ba,jxbc->jxac', imag_u, middle)
    result = jnp.stack([left_re[:, 0] + left_im[:, 1], left_re[:, 1] - left_im[:, 0]], axis=1)
    return result.astype(jnp.bfloat16)


def projection(saved_block, state):
    saved_f = saved_block.astype(jnp.float32)
    state_f = state.astype(jnp.float32)
    swapped = jnp.stack([state_f[:, 1], -state_f[:, 0]], axis=1)
    real_part = jnp.einsum('jxba,jxbc->ac', saved_f, state_f)
    imag_part = jnp.einsum('jxba,jxbc->ac', saved_f, swapped)
    return jnp.stack([real_part, imag_part], axis=1)


def reference(adjoint, saved, propagators, coupling, higher, lower, ladder, rates, decay):
    state = adjoint
    columns = []
    for step_index in range(STEPS):
        state_full = state.astype(jnp.float32)
        up_sum = linked_sum(state_full, higher, ladder[0], rates[0])
        down_sum = linked_sum(state_full, lower, ladder[1], rates[1])
        state = couple_step(state, up_sum, down_sum, coupling, decay)
        for substep in range(NSUB):
            state = rotate_step(state, propagators[step_index, substep, 0], propagators[step_index, substep, 1])
            columns.append(projection(saved[step_index, substep], state))
    return state, jnp.stack(columns, axis=1)
```

```python
import functools

import jax
import jax.numpy as jnp
from jax import lax
from jax.experimental import pallas as pl
from jax.experimental.pallas import tpu as pltpu
from jax.sharding import PartitionSpec as P

MESH = pl.DeviceIdType.MESH
F32 = jnp.float32
BF16 = jnp.bfloat16


def dot(a, b):
    return jnp.dot(a, b, preferred_element_type=F32)


def kernel(
    dims,
    higher,
    lower,
    ladder,
    rates,
    decay,
    adjoint,
    saved_in,
    propagators,
    coupling,
    out,
    grad,
    right_u,
    left_u,
    hist,
    zout,
    zin,
    rout,
    rin,
    terms,
    term_stage,
    term_inbox,
    saved,
    saved_t,
    place,
    weight,
    ladders,
    near_send,
    near_recv,
    near_pass,
    near_take,
    line_send,
    line_recv,
    line_pass,
    line_take,
    z_send,
    z_recv,
    r_send,
    r_recv,
    ladder_send,
    ladder_recv,
    term_send,
    term_recv,
    local,
    *gathered,
):
    nodes, depth, width, pair, count, modes, steps, subs, dim, halves, pieces = dims
    near, line = gathered[:steps], gathered[steps:]
    cores = depth * width
    owners = nodes * cores
    tall = nodes // pair
    chips = tall * width
    rows = dim // owners
    batch = subs // halves
    piece = count // pieces
    slots = 2 * modes
    node = lax.axis_index("node")
    spot = lax.axis_index("cores")
    level = spot // width
    column = spot % width
    side = node // pair
    core = node % pair
    chip = side * width + column

    def chip_id(other):
        return ((other // width) * pair + core, level * width + other % width)

    def chip_at(offset, sign):
        far = lax.rem(side + tall + sign * (offset // width), tall)
        return far * width + lax.rem(column + width + sign * (offset % width), width)

    def mate_id(turn):
        return (side * pair + lax.rem(core + turn, pair), spot)

    def level_id(other):
        return (node, other * width + column)

    barrier = pltpu.get_barrier_semaphore()

    own = node * cores + spot

    def owner_id(offset):
        other = lax.rem(own + offset, owners)
        return (other // cores, lax.rem(other, cores))

    def greet(offset, carry):
        pl.semaphore_signal(barrier, inc=1, device_id=owner_id(offset), device_id_type=MESH)
        return carry

    lax.fori_loop(1, owners, greet, 0)
    fetch = pltpu.make_async_copy(saved_in, saved, local.at[0])
    fetch.start()

    def remote(source, target, sent, arrived, device):
        return pltpu.make_async_remote_copy(
            src_ref=source,
            dst_ref=target,
            send_sem=sent,
            recv_sem=arrived,
            device_id=device,
            device_id_type=MESH,
        )

    def near_block(step, a_chip, a_core):
        return near[step].at[pl.ds((a_chip * pair + a_core) * count, count)]

    def line_block(step, a_core, a_level):
        return line[step].at[pl.ds((a_core * depth + a_level) * count, count)]

    def near_copy(step, offset, source):
        return remote(
            source,
            near_block(step, chip, core),
            near_send.at[step, offset - 1],
            near_recv.at[step, offset - 1],
            chip_id(chip_at(offset, 1)),
        )

    def near_mate(step, a_chip, turn, source):
        return remote(
            source,
            near_block(step, a_chip, core),
            near_pass.at[step, turn - 1, a_chip],
            near_take.at[step, turn - 1, a_chip],
            mate_id(turn),
        )

    def line_copy(step, way, hop, source):
        a_level = level - (hop - 1) if way == 0 else level + (hop - 1)
        return remote(
            source,
            line_block(step, core, a_level),
            line_send.at[step, way, hop - 1],
            line_recv.at[step, way, hop - 1],
            level_id(level + 1 if way == 0 else level - 1),
        )

    def line_mate(step, a_level, turn, source):
        return remote(
            source,
            line_block(step, core, a_level),
            line_pass.at[step, turn - 1, a_level],
            line_take.at[step, turn - 1, a_level],
            mate_id(turn),
        )

    def z_copy(step, way, a_level, k):
        return remote(
            zout.at[step, a_level, pl.ds(k * piece, piece)],
            zin.at[step, way, a_level, pl.ds(k * piece, piece)],
            z_send.at[step, a_level, k],
            z_recv.at[step, way, a_level, k],
            level_id(level + 1 if way == 0 else level - 1),
        )

    def r_copy(step, offset):
        target = chip_at(offset, 1)
        return remote(
            rout.at[step, target],
            rin.at[step, offset - 1],
            r_send.at[step, offset - 1],
            r_recv.at[step, offset - 1],
            chip_id(target),
        )

    def ladder_level(other):
        return remote(
            ladder, ladders.at[level], ladder_send.at[other], ladder_recv.at[level], level_id(other)
        )

    def ladder_chip(other):
        return remote(
            ladder,
            ladders.at[depth + chip],
            ladder_send.at[depth + other],
            ladder_recv.at[depth + chip],
            chip_id(other),
        )

    def each_ladder(act):
        def one_level(other, carry):
            @pl.when(other != level)
            def _():
                act(ladder_level(other))

            return carry

        def one_chip(other, carry):
            @pl.when(other != chip)
            def _():
                act(ladder_chip(other))

            return carry

        lax.fori_loop(0, depth, one_level, 0)
        lax.fori_loop(0, chips, one_chip, 0)

    def take_ladders():
        def one_level(other, carry):
            @pl.when(other != level)
            def _():
                remote(
                    ladder,
                    ladders.at[other],
                    ladder_send.at[other],
                    ladder_recv.at[other],
                    level_id(other),
                ).wait_recv()

            return carry

        def one_chip(other, carry):
            @pl.when(other != chip)
            def _():
                remote(
                    ladder,
                    ladders.at[depth + other],
                    ladder_send.at[depth + other],
                    ladder_recv.at[depth + other],
                    chip_id(other),
                ).wait_recv()

            return carry

        lax.fori_loop(0, depth, one_level, 0)
        lax.fori_loop(0, chips, one_chip, 0)

    def tabulate():
        for way in range(2):
            for mode in range(modes):
                for j in range(count):
                    value = ladder[way, mode, j]
                    ladders[level, way, mode, j] = value
                    ladders[depth + chip, way, mode, j] = value

        def entry(at, along_z):
            index, j = at // count, at % count
            if along_z:
                target = node * cores + index * width + column
            else:
                target = ((index // width) * pair + core) * cores + level * width + index % width
            row = index if along_z else depth + index
            for way in range(2):
                for mode in range(modes):
                    link = (higher, lower)[way][mode, target * count + j]
                    source = link // count
                    a_node, a_spot = source // cores, source % cores
                    a_level, a_column = a_spot // width, a_spot % width
                    a_side, a_core = a_node // pair, a_node % pair
                    if along_z:
                        here = a_level == level
                        block = (a_side * width + a_column) * pair + a_core
                    else:
                        here = jnp.logical_and(a_side == side, a_column == column)
                        block = a_core * depth + a_level
                    value = ladders[row, way, mode, j].astype(F32) * rates[way, mode]
                    spot_at = ((row * count + j) * 2 + way) * modes + mode
                    place[spot_at] = block * count + link % count
                    weight[spot_at] = jnp.where(here, value, 0.0)

        def entry_z(at, carry):
            entry(at, True)
            return carry

        def entry_r(at, carry):
            entry(at, False)
            return carry

        lax.fori_loop(0, depth * count, entry_z, 0)
        lax.fori_loop(0, chips * count, entry_r, 0)

    def partial(blocks, row, put):
        operator = coupling[...]

        def some(pick, carry):
            plus, minus = [], []
            for i in range(2):
                sums = []
                for way in range(2):
                    total = None
                    for mode in range(modes):
                        at = ((row * count + pick * 2 + i) * 2 + way) * modes + mode
                        scale = jnp.full((16, dim), weight[at], F32).astype(BF16)
                        term = blocks[place[at]].reshape(dim // 16, 16, dim) * scale
                        total = term if total is None else total + term
                    sums.append(total.reshape(dim, dim))
                plus.append(sums[0] + sums[1])
                minus.append(sums[0] - sums[1])
            left = dot(operator, jnp.concatenate(plus, axis=1))
            right = dot(jnp.concatenate(minus, axis=0), operator)
            for i in range(2):
                value = left[:, i * dim : (i + 1) * dim] - right[i * dim : (i + 1) * dim]
                put(pick * 2 + i, value.astype(BF16))
            return carry

        lax.fori_loop(0, count // 2, some, 0)

    def prepare():
        def one(at, carry):
            step, sub = at // subs, at % subs
            u_re = propagators[step, sub, 0]
            u_im = propagators[step, sub, 1]
            right_u[at, :dim, :dim] = u_re
            right_u[at, :dim, dim:] = u_im
            right_u[at, dim:, :dim] = -u_im
            right_u[at, dim:, dim:] = u_re
            t_re = u_re.T
            t_im = u_im.T
            left_u[at, :dim, :dim] = t_re
            left_u[at, :dim, dim:] = t_im
            left_u[at, dim:, :dim] = -t_im
            left_u[at, dim:, dim:] = t_re
            return carry

        lax.fori_loop(0, steps * subs, one, 0)

    def turn_saved(sub):
        for j in range(count):
            kept = saved[steps - 1, sub, j].reshape(2 * dim, dim)
            saved_t[sub, :, 2 * dim * j : 2 * dim * (j + 1)] = kept.T

    def project(step, sub):
        total = jnp.zeros((dim, 2 * dim), F32)
        for j in range(count):
            lam_re = hist[step, sub + 1, j, 0]
            lam_im = hist[step, sub + 1, j, 1]
            both = jnp.concatenate(
                [
                    jnp.concatenate([lam_re, lam_im], axis=1),
                    jnp.concatenate([lam_im, -lam_re], axis=1),
                ],
                axis=0,
            )
            if step == steps - 1:
                kept_t = saved_t[sub, :, 2 * dim * j : 2 * dim * (j + 1)]
                total = total + dot(kept_t, both)
            else:
                kept = saved[step, sub, j].reshape(2 * dim, dim)
                total = total + lax.dot_general(
                    kept, both, (((0,), (0,)), ((), ())), preferred_element_type=F32
                )
        terms[sub % batch] = total
        if sub % batch == batch - 1:
            spread(step * halves + sub // batch)

    def spread(group):
        for target in range(owners):
            term_stage[group, target] = jnp.concatenate(
                [terms[i, target * rows : (target + 1) * rows] for i in range(batch)], axis=0
            ).astype(BF16)

        def send(offset, carry):
            pltpu.make_async_remote_copy(
                src_ref=term_stage.at[group, lax.rem(own + offset, owners)],
                dst_ref=term_inbox.at[group, offset - 1],
                send_sem=term_send.at[group],
                recv_sem=term_recv.at[group],
                device_id=owner_id(offset),
                device_id_type=MESH,
            ).start()
            return carry

        lax.fori_loop(1, owners, send, 0)

    def finish(group):
        everything = term_inbox.at[group]
        pltpu.make_async_copy(everything, everything, term_recv.at[group]).wait()
        total = term_stage[group, own].astype(F32)
        for offset in range(1, owners):
            total = total + term_inbox[group, offset - 1].astype(F32)
        for i in range(batch):
            for row in range(rows):
                for part in range(2):
                    grad[row, group * batch + i, part : part + 1, :] = total[
                        i * rows + row : i * rows + row + 1, part * dim : (part + 1) * dim
                    ]
        pltpu.make_async_copy(everything, everything, term_send.at[group]).wait()

    def rotate(step, half):
        def one(sub, carry):
            at = step * subs + sub
            mult_r = right_u[at]
            mult_l = left_u[at]
            for j in range(0, count, 2):
                rows = jnp.concatenate(
                    [
                        jnp.concatenate(
                            [hist[step, sub, j + i, 0], hist[step, sub, j + i, 1]], axis=1
                        )
                        for i in range(2)
                    ],
                    axis=0,
                )
                middle = dot(rows, mult_r).astype(BF16)
                stacked = jnp.concatenate(
                    [
                        jnp.concatenate([middle[:dim, :dim], middle[dim:, :dim]], axis=1),
                        jnp.concatenate([middle[:dim, dim:], middle[dim:, dim:]], axis=1),
                    ],
                    axis=0,
                )
                result = dot(mult_l, stacked).astype(BF16)
                for i in range(2):
                    for part in range(2):
                        hist[step, sub + 1, j + i, part] = result[
                            part * dim : (part + 1) * dim, i * dim : (i + 1) * dim
                        ]
            return carry

        lax.fori_loop(half * batch, (half + 1) * batch, one, 0)

    def join(step, state):
        def one(j, carry):
            lam = decay[j] * state[j, 0].astype(F32) + zout[step, level, j].astype(F32)
            hist[step, 0, j, 0] = lam.astype(BF16)
            total = rout[step, chip, j].astype(F32)
            for offset in range(1, chips):
                total = total + rin[step, offset - 1, j].astype(F32)
            lam = decay[j] * state[j, 1].astype(F32) - total
            hist[step, 0, j, 1] = lam.astype(BF16)
            return carry

        lax.fori_loop(0, count, one, 0)

    def arrives(way, hop):
        return level >= hop if way == 0 else level + hop < depth

    def goes_on(way, hop):
        if way == 0:
            return jnp.logical_and(level >= hop - 1, level < depth - 1)
        return jnp.logical_and(level + hop - 1 < depth, level > 0)

    def take_line(step, hop):
        for way in range(2):

            @pl.when(arrives(way, hop))
            def _(way=way):
                a_level = level - hop if way == 0 else level + hop
                block = line_block(step, core, a_level)
                remote(
                    block,
                    block,
                    line_send.at[step, way, hop - 1],
                    line_recv.at[step, way, hop - 1],
                    level_id(level),
                ).wait_recv()
                if hop + 1 < depth:

                    @pl.when(goes_on(way, hop + 1))
                    def _():
                        line_copy(step, way, hop + 1, block).start()

                for turn in range(1, pair):
                    line_mate(step, a_level, turn, block).start()

    def take_near(step):
        def one(offset, carry):
            a_chip = chip_at(offset, -1)
            block = near_block(step, a_chip, core)
            near_copy(step, offset, block).wait_recv()
            for turn in range(1, pair):
                near_mate(step, a_chip, turn, block).start()
            return carry

        lax.fori_loop(1, chips, one, 0)
        for turn in range(1, pair):

            def two(a_chip, carry, turn=turn):
                block = near_block(step, a_chip, lax.rem(core + pair - turn, pair))
                near_mate(step, a_chip, turn, block).wait_recv()
                return carry

            lax.fori_loop(0, chips, two, 0)

    def mates_line(step):
        for turn in range(1, pair):

            def two(a_level, carry, turn=turn):
                block = line_block(step, lax.rem(core + pair - turn, pair), a_level)
                line_mate(step, a_level, turn, block).wait_recv()
                return carry

            lax.fori_loop(0, depth, two, 0)

    def reduce_start(step):
        def one(i, carry):
            a_level = jnp.where(level * 2 < depth, depth - 1 - i, i)

            def put(j, value):
                zout[step, a_level, j] = value

            partial(near[step], a_level, put)

            def send(way):
                for k in range(pieces):
                    z_copy(step, way, a_level, k).start()

            pl.when(jnp.logical_and(level == 0, a_level > 0))(lambda: send(0))
            pl.when(jnp.logical_and(level == depth - 1, a_level < depth - 1))(lambda: send(1))
            return carry

        lax.fori_loop(0, depth, one, 0)

    def exchange(step):
        def one(i, carry):
            offset = lax.rem(i + 1, chips)
            target = chip_at(offset, 1)

            def put(j, value):
                rout[step, target, j] = value

            partial(line[step], depth + target, put)

            @pl.when(offset > 0)
            def _():
                r_copy(step, offset).start()

            return carry

        lax.fori_loop(0, chips, one, 0)

    def reduce_on(step):
        for ahead in range(max(depth - 2, 0), -1, -1):
            for k in range(pieces):
                for way in range(2):
                    if way == 0:
                        a_level = level + ahead
                        fits = jnp.logical_and(level > 0, a_level < depth)
                    else:
                        a_level = level - ahead
                        fits = jnp.logical_and(level < depth - 1, a_level >= 0)

                    @pl.when(fits)
                    def _(way=way, k=k, a_level=a_level):
                        z_copy(step, way, a_level, k).wait_recv()
                        for j in range(k * piece, (k + 1) * piece):
                            total = zout[step, a_level, j].astype(F32)
                            total = total + zin[step, way, a_level, j].astype(F32)
                            zout[step, a_level, j] = total.astype(BF16)
                        if ahead > 0:
                            z_copy(step, way, a_level, k).start()

    prepare()
    pl.semaphore_wait(barrier, owners - 1)
    for step in range(steps):
        state = adjoint if step == 0 else hist.at[step - 1, subs]
        re, im = state.at[:, 0], state.at[:, 1]
        for way in range(2):

            @pl.when(goes_on(way, 1))
            def _(way=way):
                line_copy(step, way, 1, re).start()

        def plane(offset, carry, step=step, im=im):
            near_copy(step, offset, im).start()
            return carry

        lax.fori_loop(1, chips, plane, 0)
        for turn in range(1, pair):
            near_mate(step, chip, turn, im).start()
            line_mate(step, level, turn, re).start()
        keep_im = pltpu.make_async_copy(im, near_block(step, chip, core), local.at[2])
        keep_re = pltpu.make_async_copy(re, line_block(step, core, level), local.at[3])
        keep_im.start()
        keep_re.start()
        if step == 0:
            each_ladder(lambda copy: copy.start())
            fetch.wait()
            for sub in range(subs):
                turn_saved(sub)
            take_ladders()
            tabulate()
        else:
            for sub in range(subs):
                project(step - 1, sub)
        if depth > 1:
            take_line(step, 1)
        keep_im.wait()
        keep_re.wait()
        take_near(step)
        if depth > 2:
            take_line(step, 2)
        reduce_start(step)
        for hop in range(3, depth):
            take_line(step, hop)
        mates_line(step)
        exchange(step)
        reduce_on(step)

        def collect(offset, carry, step=step):
            r_copy(step, offset).wait_recv()
            return carry

        lax.fori_loop(1, chips, collect, 0)
        join(step, state)
        for half in range(halves):
            rotate(step, half)
            if step == steps - 1:
                for sub in range(half * batch, (half + 1) * batch):
                    project(step, sub)
                    if sub == subs - 1:
                        result = pltpu.make_async_copy(hist.at[step, subs], out, local.at[1])
                        result.start()

        for hop in range(1, depth):
            for way in range(2):

                @pl.when(goes_on(way, hop))
                def _(way=way, hop=hop):
                    a_level = level - (hop - 1) if way == 0 else level + (hop - 1)
                    line_copy(step, way, hop, line_block(step, core, a_level)).wait_send()

        def done_chip(offset, carry, step=step):
            near_copy(step, offset, near_block(step, chip, core)).wait_send()
            r_copy(step, offset).wait_send()
            return carry

        lax.fori_loop(1, chips, done_chip, 0)
        for turn in range(1, pair):

            def done_near(a_chip, carry, step=step, turn=turn):
                near_mate(step, a_chip, turn, near_block(step, a_chip, core)).wait_send()
                return carry

            def done_line(a_level, carry, step=step, turn=turn):
                line_mate(step, a_level, turn, line_block(step, core, a_level)).wait_send()
                return carry

            lax.fori_loop(0, chips, done_near, 0)
            lax.fori_loop(0, depth, done_line, 0)

        def done_z(a_level, carry, step=step):
            @pl.when(a_level != level)
            def _():
                for k in range(pieces):
                    z_copy(step, 0, a_level, k).wait_send()

            return carry

        lax.fori_loop(0, depth, done_z, 0)

    each_ladder(lambda copy: copy.wait_send())
    result.wait()
    for group in range(steps * halves):
        finish(group)


def body(adjoint, saved, propagators, coupling, higher, lower, ladder, rates, decay):
    nodes = lax.axis_size("node")
    cores = lax.axis_size("cores")
    owners = nodes * cores
    count = adjoint.shape[0]
    modes = higher.shape[1]
    steps, subs = propagators.shape[:2]
    dim = coupling.shape[0]
    depth = 1 << (cores.bit_length() // 2)
    width = cores // depth
    pair = 2 if nodes % 2 == 0 else 1
    chips = nodes // pair * width
    pieces = 2
    rows = dim // owners
    halves = 2 if subs % 2 == 0 else 1
    batch = subs // halves
    higher, lower, ladder = higher.T, lower.T, jnp.swapaxes(ladder, 1, 2)
    smem = pl.BlockSpec(memory_space=pltpu.SMEM)
    vmem = pl.BlockSpec(memory_space=pltpu.VMEM)
    block = adjoint.shape
    hbm = pl.BlockSpec(memory_space=pl.ANY)
    hops = max(depth - 1, 1)
    others = max(chips - 1, 1)
    mates = max(pair - 1, 1)
    half = (count,) + block[2:]
    table = (depth + chips) * count * 2 * modes
    dma = pltpu.SemaphoreType.DMA
    state, grad = pl.pallas_call(
        functools.partial(kernel, (nodes, depth, width, pair, count, modes, steps, subs, dim, halves, pieces)),
        out_shape=(
            jax.ShapeDtypeStruct(block, BF16),
            jax.ShapeDtypeStruct((rows, steps * subs, 2, dim), F32),
        ),
        in_specs=[smem] * 5 + [vmem, hbm, vmem, vmem],
        out_specs=(hbm, vmem),
        scratch_shapes=[
            pltpu.VMEM((steps * subs, 2 * dim, 2 * dim), BF16),
            pltpu.VMEM((steps * subs, 2 * dim, 2 * dim), BF16),
            pltpu.VMEM((steps, subs + 1) + block, BF16),
            pltpu.VMEM((steps, depth) + half, BF16),
            pltpu.VMEM((steps, 2, depth) + half, BF16),
            pltpu.VMEM((steps, chips) + half, BF16),
            pltpu.VMEM((steps, others) + half, BF16),
            pltpu.VMEM((batch, dim, 2 * dim), F32),
            pltpu.VMEM((steps * halves, owners, batch * rows, 2 * dim), BF16),
            pltpu.VMEM((steps * halves, owners - 1, batch * rows, 2 * dim), BF16),
            pltpu.VMEM(saved.shape, BF16),
            pltpu.VMEM((subs, dim, count * 2 * dim), BF16),
            pltpu.SMEM((table,), jnp.int32),
            pltpu.SMEM((table,), F32),
            pltpu.SMEM((depth + chips, 2, modes, count), jnp.int32),
            dma((steps, others)),
            dma((steps, others)),
            dma((steps, mates, chips)),
            dma((steps, mates, chips)),
            dma((steps, 2, hops)),
            dma((steps, 2, hops)),
            dma((steps, mates, depth)),
            dma((steps, mates, depth)),
            dma((steps, depth, pieces)),
            dma((steps, 2, depth, pieces)),
            dma((steps, others)),
            dma((steps, others)),
            dma((depth + chips,)),
            dma((depth + chips,)),
            dma((steps * halves,)),
            dma((steps * halves,)),
            dma((4,)),
            *[pltpu.VMEM((chips * pair * count, dim, dim), BF16)] * steps,
            *[pltpu.VMEM((depth * pair * count, dim, dim), BF16)] * steps,
        ],
        compiler_params=pltpu.CompilerParams(
            collective_id=0, has_side_effects=True, vmem_limit_bytes=63_000_000
        ),
    )(higher, lower, ladder, rates, decay, adjoint, saved, propagators, coupling)
    return state, grad


def solution(mesh):
    return jax.shard_map(
        body,
        mesh=mesh,
        in_specs=(
            P(("node", "cores"), None, None, None),
            P(None, None, ("node", "cores"), None, None, None),
            P(),
            P(),
            P(),
            P(),
            P(None, ("node", "cores"), None),
            P(),
            P(("node", "cores")),
        ),
        out_specs=(P(("node", "cores"), None, None, None), P(("node", "cores"), None, None, None)),
        check_vma=False,
    )
```

```python
import functools

import jax
import jax.numpy as jnp
from jax import lax
from jax.experimental import pallas as pl
from jax.experimental.pallas import tpu as pltpu
from jax.sharding import PartitionSpec as P

MESH = pl.DeviceIdType.MESH
F32 = jnp.float32
BF16 = jnp.bfloat16


def dot(a, b):
    return jnp.dot(a, b, preferred_element_type=F32)


def kernel(
    dims,
    higher,
    lower,
    ladder,
    rates,
    decay,
    adjoint,
    saved_in,
    propagators,
    coupling,
    out,
    grad,
    right_u,
    left_u,
    hist,
    zout,
    zin,
    rout,
    row_in,
    col_in,
    row_end,
    col_end,
    terms,
    term_stage,
    term_inbox,
    saved,
    saved_t,
    place,
    weight,
    home,
    inside,
    ladders,
    near_send,
    near_recv,
    near_pass,
    near_take,
    line_send,
    line_recv,
    line_pass,
    line_take,
    z_send,
    z_recv,
    row_send,
    row_recv,
    col_send,
    col_recv,
    row_last,
    row_done,
    col_last,
    col_done,
    ladder_send,
    ladder_recv,
    term_send,
    term_recv,
    local,
    *gathered,
):
    nodes, depth, width, pair, count, modes, steps, subs, dim, halves, pieces = dims
    near, line = gathered[:steps], gathered[steps:]
    cores = depth * width
    owners = nodes * cores
    tall = nodes // pair
    chips = tall * width
    rows = dim // owners
    batch = subs // halves
    piece = count // pieces
    slots = 2 * modes
    node = lax.axis_index("node")
    spot = lax.axis_index("cores")
    level = spot // width
    column = spot % width
    side = node // pair
    core = node % pair
    chip = side * width + column

    def split(value, size):
        if size & (size - 1) == 0:
            return value >> (size.bit_length() - 1), value & (size - 1)
        return lax.div(value, size), lax.rem(value, size)

    def chip_id(other):
        return ((other // width) * pair + core, level * width + other % width)

    def chip_at(up, right):
        return lax.rem(side + up + tall, tall) * width + lax.rem(column + right + width, width)

    def mate_id(turn):
        return (side * pair + lax.rem(core + turn, pair), spot)

    def level_id(other):
        return (node, other * width + column)

    barrier = pltpu.get_barrier_semaphore()

    own = node * cores + spot

    def owner_id(offset):
        other = lax.rem(own + offset, owners)
        return (other // cores, lax.rem(other, cores))

    def greet(offset, carry):
        pl.semaphore_signal(barrier, inc=1, device_id=owner_id(offset), device_id_type=MESH)
        return carry

    lax.fori_loop(1, owners, greet, 0)
    fetch = pltpu.make_async_copy(saved_in, saved, local.at[0])
    fetch.start()

    def remote(source, target, sent, arrived, device):
        return pltpu.make_async_remote_copy(
            src_ref=source,
            dst_ref=target,
            send_sem=sent,
            recv_sem=arrived,
            device_id=device,
            device_id_type=MESH,
        )

    def part(k):
        return pl.ds(k * piece, piece)

    def near_block(step, a_chip, a_core, k):
        return near[step].at[pl.ds((a_chip * pair + a_core) * count + k * piece, piece)]

    def line_block(step, a_core, a_level, k):
        return line[step].at[pl.ds((a_core * depth + a_level) * count + k * piece, piece)]

    def near_copy(step, up, right, k, source, a_chip, target):
        at = up * width + right - 1
        return remote(
            source,
            near_block(step, a_chip, core, k),
            near_send.at[step, at, k],
            near_recv.at[step, at, k],
            chip_id(target),
        )

    def near_got(step, up, right, k):
        a_chip = chip_at(-up, -right)
        block = near_block(step, a_chip, core, k)
        near_copy(step, up, right, k, block, a_chip, a_chip).wait_recv()
        for turn in range(1, pair):
            near_mate(step, a_chip, turn, k, block).start()
        return block, a_chip

    def near_mate(step, a_chip, turn, k, source):
        return remote(
            source,
            near_block(step, a_chip, core, k),
            near_pass.at[step, turn - 1, a_chip, k],
            near_take.at[step, turn - 1, a_chip, k],
            mate_id(turn),
        )

    def line_copy(step, way, hop, k, source):
        a_level = level - (hop - 1) if way == 0 else level + (hop - 1)
        return remote(
            source,
            line_block(step, core, a_level, k),
            line_send.at[step, way, hop - 1, k],
            line_recv.at[step, way, hop - 1, k],
            level_id(level + 1 if way == 0 else level - 1),
        )

    def line_mate(step, a_level, turn, k, source):
        return remote(
            source,
            line_block(step, core, a_level, k),
            line_pass.at[step, turn - 1, a_level, k],
            line_take.at[step, turn - 1, a_level, k],
            mate_id(turn),
        )

    def z_copy(step, way, a_level, k):
        return remote(
            zout.at[step, a_level, pl.ds(k * piece, piece)],
            zin.at[step, way, a_level, pl.ds(k * piece, piece)],
            z_send.at[step, a_level, k],
            z_recv.at[step, way, a_level, k],
            level_id(level + 1 if way == 0 else level - 1),
        )

    def row_copy(step, up, right):
        return remote(
            rout.at[step, chip_at(up, right), part(0)],
            row_in.at[step, right - 1, up],
            row_send.at[step, right - 1, up],
            row_recv.at[step, right - 1, up],
            chip_id(chip_at(0, right)),
        )

    def col_copy(step, up, right):
        return remote(
            rout.at[step, chip_at(up, right), part(1)],
            col_in.at[step, up - 1, right],
            col_send.at[step, up - 1, right],
            col_recv.at[step, up - 1, right],
            chip_id(chip_at(up, 0)),
        )

    def col_final(step, up):
        return remote(
            rout.at[step, chip_at(up, 0), part(0)],
            col_end.at[step, up - 1],
            col_last.at[step, up - 1],
            col_done.at[step, up - 1],
            chip_id(chip_at(up, 0)),
        )

    def row_final(step, right):
        return remote(
            rout.at[step, chip_at(0, right), part(1)],
            row_end.at[step, right - 1],
            row_last.at[step, right - 1],
            row_done.at[step, right - 1],
            chip_id(chip_at(0, right)),
        )

    def ladder_level(other):
        return remote(
            ladder, ladders.at[level], ladder_send.at[other], ladder_recv.at[level], level_id(other)
        )

    def ladder_chip(other):
        return remote(
            ladder,
            ladders.at[depth + chip],
            ladder_send.at[depth + other],
            ladder_recv.at[depth + chip],
            chip_id(other),
        )

    def each_ladder(act):
        def one_level(other, carry):
            @pl.when(other != level)
            def _():
                act(ladder_level(other))

            return carry

        def one_chip(other, carry):
            @pl.when(other != chip)
            def _():
                act(ladder_chip(other))

            return carry

        lax.fori_loop(0, depth, one_level, 0)
        lax.fori_loop(0, chips, one_chip, 0)

    def take_ladders():
        def one_level(other, carry):
            @pl.when(other != level)
            def _():
                remote(
                    ladder,
                    ladders.at[other],
                    ladder_send.at[other],
                    ladder_recv.at[other],
                    level_id(other),
                ).wait_recv()

            return carry

        def one_chip(other, carry):
            @pl.when(other != chip)
            def _():
                remote(
                    ladder,
                    ladders.at[depth + other],
                    ladder_send.at[depth + other],
                    ladder_recv.at[depth + other],
                    chip_id(other),
                ).wait_recv()

            return carry

        lax.fori_loop(0, depth, one_level, 0)
        lax.fori_loop(0, chips, one_chip, 0)

    def tabulate():
        for way in range(2):
            for mode in range(modes):
                for j in range(count):
                    value = ladder[way, mode, j]
                    ladders[level, way, mode, j] = value
                    ladders[depth + chip, way, mode, j] = value

        def locate(owner, carry):
            a_node, a_spot = split(owner, cores)
            a_level, a_column = split(a_spot, width)
            a_side, a_core = split(a_node, pair)
            home[0, owner] = ((a_side * width + a_column) * pair + a_core) * count
            home[1, owner] = (a_core * depth + a_level) * count
            inside[0, owner] = jnp.where(a_level == level, 1.0, 0.0)
            beside = jnp.logical_and(a_side == side, a_column == column)
            inside[1, owner] = jnp.where(beside, 1.0, 0.0)
            return carry

        lax.fori_loop(0, owners, locate, 0)

        def entry(at, along_z):
            index, j = split(at, count)
            if along_z:
                target, kind, row = node * cores + index * width + column, 0, index
            else:
                a_side, a_column = split(index, width)
                target = (a_side * pair + core) * cores + level * width + a_column
                kind, row = 1, depth + index
            for way in range(2):
                for mode in range(modes):
                    source, member = split((higher, lower)[way][mode, target * count + j], count)
                    value = ladders[row, way, mode, j].astype(F32) * rates[way, mode]
                    slot = (row * count + j) * slots + way * modes + mode
                    place[slot] = home[kind, source] + member
                    weight[slot] = inside[kind, source] * value

        def entry_z(at, carry):
            entry(at, True)
            return carry

        def entry_r(at, carry):
            entry(at, False)
            return carry

        lax.fori_loop(0, depth * count, entry_z, 0)
        lax.fori_loop(0, chips * count, entry_r, 0)

    def partial(blocks, row, put):
        operator = coupling[...]

        def some(pick, carry):
            plus, minus = [], []
            for i in range(2):
                sums = []
                for way in range(2):
                    total = None
                    for mode in range(modes):
                        at = (row * count + pick * 2 + i) * slots + way * modes + mode
                        scale = jnp.full((16, dim), weight[at], F32).astype(BF16)
                        term = blocks[place[at]].reshape(dim // 16, 16, dim) * scale
                        total = term if total is None else total + term
                    sums.append(total.reshape(dim, dim))
                plus.append(sums[0] + sums[1])
                minus.append(sums[0] - sums[1])
            left = dot(operator, jnp.concatenate(plus, axis=1))
            right = dot(jnp.concatenate(minus, axis=0), operator)
            for i in range(2):
                value = left[:, i * dim : (i + 1) * dim] - right[i * dim : (i + 1) * dim]
                put(pick * 2 + i, value.astype(BF16))
            return carry

        lax.fori_loop(0, count // 2, some, 0)

    def prepare():
        def one(at, carry):
            step, sub = at // subs, at % subs
            u_re = propagators[step, sub, 0]
            u_im = propagators[step, sub, 1]
            right_u[at, :dim, :dim] = u_re
            right_u[at, :dim, dim:] = u_im
            right_u[at, dim:, :dim] = -u_im
            right_u[at, dim:, dim:] = u_re
            t_re = u_re.T
            t_im = u_im.T
            left_u[at, :dim, :dim] = t_re
            left_u[at, :dim, dim:] = t_im
            left_u[at, dim:, :dim] = -t_im
            left_u[at, dim:, dim:] = t_re
            return carry

        lax.fori_loop(0, steps * subs, one, 0)

    def turn_saved(sub):
        for j in range(count):
            kept = saved[steps - 1, sub, j].reshape(2 * dim, dim)
            saved_t[sub, :, 2 * dim * j : 2 * dim * (j + 1)] = kept.T

    def project(step, sub):
        total = jnp.zeros((dim, 2 * dim), F32)
        for j in range(count):
            lam_re = hist[step, sub + 1, j, 0]
            lam_im = hist[step, sub + 1, j, 1]
            both = jnp.concatenate(
                [
                    jnp.concatenate([lam_re, lam_im], axis=1),
                    jnp.concatenate([lam_im, -lam_re], axis=1),
                ],
                axis=0,
            )
            if step == steps - 1:
                kept_t = saved_t[sub, :, 2 * dim * j : 2 * dim * (j + 1)]
                total = total + dot(kept_t, both)
            else:
                kept = saved[step, sub, j].reshape(2 * dim, dim)
                total = total + lax.dot_general(
                    kept, both, (((0,), (0,)), ((), ())), preferred_element_type=F32
                )
        terms[sub % batch] = total
        if sub % batch == batch - 1:
            spread(step * halves + sub // batch)

    def spread(group):
        for target in range(owners):
            term_stage[group, target] = jnp.concatenate(
                [terms[i, target * rows : (target + 1) * rows] for i in range(batch)], axis=0
            ).astype(BF16)

        def send(offset, carry):
            pltpu.make_async_remote_copy(
                src_ref=term_stage.at[group, lax.rem(own + offset, owners)],
                dst_ref=term_inbox.at[group, offset - 1],
                send_sem=term_send.at[group],
                recv_sem=term_recv.at[group],
                device_id=owner_id(offset),
                device_id_type=MESH,
            ).start()
            return carry

        lax.fori_loop(1, owners, send, 0)

    def finish(group):
        everything = term_inbox.at[group]
        pltpu.make_async_copy(everything, everything, term_recv.at[group]).wait()
        total = term_stage[group, own].astype(F32)
        for offset in range(1, owners):
            total = total + term_inbox[group, offset - 1].astype(F32)
        for i in range(batch):
            for row in range(rows):
                for part in range(2):
                    grad[row, group * batch + i, part : part + 1, :] = total[
                        i * rows + row : i * rows + row + 1, part * dim : (part + 1) * dim
                    ]
        pltpu.make_async_copy(everything, everything, term_send.at[group]).wait()

    def rotate(step, half):
        def one(sub, carry):
            at = step * subs + sub
            mult_r = right_u[at]
            mult_l = left_u[at]
            for j in range(0, count, 2):
                rows = jnp.concatenate(
                    [
                        jnp.concatenate(
                            [hist[step, sub, j + i, 0], hist[step, sub, j + i, 1]], axis=1
                        )
                        for i in range(2)
                    ],
                    axis=0,
                )
                middle = dot(rows, mult_r).astype(BF16)
                stacked = jnp.concatenate(
                    [
                        jnp.concatenate([middle[:dim, :dim], middle[dim:, :dim]], axis=1),
                        jnp.concatenate([middle[:dim, dim:], middle[dim:, dim:]], axis=1),
                    ],
                    axis=0,
                )
                result = dot(mult_l, stacked).astype(BF16)
                for i in range(2):
                    for part in range(2):
                        hist[step, sub + 1, j + i, part] = result[
                            part * dim : (part + 1) * dim, i * dim : (i + 1) * dim
                        ]
            return carry

        lax.fori_loop(half * batch, (half + 1) * batch, one, 0)

    def join(step, state):
        def one(j, carry):
            lam = decay[j] * state[j, 0].astype(F32) + zout[step, level, j].astype(F32)
            hist[step, 0, j, 0] = lam.astype(BF16)
            total = rout[step, chip, j].astype(F32)
            lam = decay[j] * state[j, 1].astype(F32) - total
            hist[step, 0, j, 1] = lam.astype(BF16)
            return carry

        lax.fori_loop(0, count, one, 0)

    def fold(target, sources):
        for j in range(piece):
            total = target[j].astype(F32)
            for source in sources:
                total = total + source[j].astype(F32)
            target[j] = total.astype(BF16)

    def arrives(way, hop):
        return level >= hop if way == 0 else level + hop < depth

    def goes_on(way, hop):
        if way == 0:
            return jnp.logical_and(level >= hop - 1, level < depth - 1)
        return jnp.logical_and(level + hop - 1 < depth, level > 0)

    def take_line(step, hop, k):
        for way in range(2):

            @pl.when(arrives(way, hop))
            def _(way=way):
                a_level = level - hop if way == 0 else level + hop
                block = line_block(step, core, a_level, k)
                remote(
                    block,
                    block,
                    line_send.at[step, way, hop - 1, k],
                    line_recv.at[step, way, hop - 1, k],
                    level_id(level),
                ).wait_recv()
                if hop + 1 < depth:

                    @pl.when(goes_on(way, hop + 1))
                    def _():
                        line_copy(step, way, hop + 1, k, block).start()

                for turn in range(1, pair):
                    line_mate(step, a_level, turn, k, block).start()

    def each(lo, hi, act):
        def one(i, carry):
            act(i)
            return carry

        lax.fori_loop(lo, hi, one, 0)

    def take_first(step):
        def along(right):
            block, a_chip = near_got(step, 0, right, 0)
            each(
                1,
                tall,
                lambda up: near_copy(
                    step, up, right, 0, block, a_chip, chip_at(up, 0)
                ).start(),
            )

        def across(up):
            block, a_chip = near_got(step, up, 0, 1)
            each(
                1,
                width,
                lambda right: near_copy(
                    step, up, right, 1, block, a_chip, chip_at(0, right)
                ).start(),
            )

        each(1, width, along)
        each(1, tall, across)

    def take_second(step):
        each(1, width, lambda right: near_got(step, 0, right, 1) and None)
        each(1, tall, lambda up: near_got(step, up, 0, 0) and None)

    def take_far(step):
        def one(up):
            def two(right):
                for k in range(pieces):
                    near_got(step, up, right, k)

            each(1, width, two)

        each(1, tall, one)
        for turn in range(1, pair):

            def two(a_chip, turn=turn):
                for k in range(pieces):
                    block = near_block(step, a_chip, lax.rem(core + pair - turn, pair), k)
                    near_mate(step, a_chip, turn, k, block).wait_recv()

            each(0, chips, two)

    def mates_line(step):
        for turn in range(1, pair):

            def two(a_level, turn=turn):
                for k in range(pieces):
                    block = line_block(step, lax.rem(core + pair - turn, pair), a_level, k)
                    line_mate(step, a_level, turn, k, block).wait_recv()

            each(0, depth, two)

    def reduce_start(step, lo, hi):
        def one(i, carry):
            a_level = jnp.where(level * 2 < depth, depth - 1 - i, i)

            def put(j, value):
                zout[step, a_level, j] = value

            partial(near[step], a_level, put)

            def send(way):
                for k in range(pieces):
                    z_copy(step, way, a_level, k).start()

            pl.when(jnp.logical_and(level == 0, a_level > 0))(lambda: send(0))
            pl.when(jnp.logical_and(level == depth - 1, a_level < depth - 1))(lambda: send(1))
            return carry

        lax.fori_loop(lo, hi, one, 0)

    def exchange(step):
        def one(i):
            up, right = split(chips - 1 - i, width)
            target = chip_at(up, right)

            def put(j, value):
                rout[step, target, j] = value

            partial(line[step], depth + target, put)

            @pl.when(right > 0)
            def _():
                row_copy(step, up, right).start()

            @pl.when(up > 0)
            def _():
                col_copy(step, up, right).start()

        each(0, chips, one)

    def exchange_on(step):
        def column(up):
            target = chip_at(up, 0)
            each(1, width, lambda right: row_copy(step, up, right).wait_recv())
            fold(
                rout.at[step, target, part(0)],
                [row_in.at[step, right - 1, up] for right in range(1, width)],
            )
            col_final(step, up).start()

        def line_of(right):
            target = chip_at(0, right)
            each(1, tall, lambda up: col_copy(step, up, right).wait_recv())
            fold(
                rout.at[step, target, part(1)],
                [col_in.at[step, up - 1, right] for up in range(1, tall)],
            )
            row_final(step, right).start()

        each(1, tall, column)
        each(1, width, line_of)

    def exchange_end(step):
        each(1, width, lambda right: row_copy(step, 0, right).wait_recv())
        each(1, tall, lambda up: col_copy(step, up, 0).wait_recv())
        each(1, tall, lambda up: col_final(step, up).wait_recv())
        each(1, width, lambda right: row_final(step, right).wait_recv())
        fold(
            rout.at[step, chip, part(0)],
            [row_in.at[step, right - 1, 0] for right in range(1, width)]
            + [col_end.at[step, up - 1] for up in range(1, tall)],
        )
        fold(
            rout.at[step, chip, part(1)],
            [col_in.at[step, up - 1, 0] for up in range(1, tall)]
            + [row_end.at[step, right - 1] for right in range(1, width)],
        )

    def reduce_on(step):
        for ahead in range(max(depth - 2, 0), -1, -1):
            for k in range(pieces):
                for way in range(2):
                    if way == 0:
                        a_level = level + ahead
                        fits = jnp.logical_and(level > 0, a_level < depth)
                    else:
                        a_level = level - ahead
                        fits = jnp.logical_and(level < depth - 1, a_level >= 0)

                    @pl.when(fits)
                    def _(way=way, k=k, a_level=a_level):
                        z_copy(step, way, a_level, k).wait_recv()
                        for j in range(k * piece, (k + 1) * piece):
                            total = zout[step, a_level, j].astype(F32)
                            total = total + zin[step, way, a_level, j].astype(F32)
                            zout[step, a_level, j] = total.astype(BF16)
                        if ahead > 0:
                            z_copy(step, way, a_level, k).start()

    prepare()
    pl.semaphore_wait(barrier, owners - 1)
    for step in range(steps):
        state = adjoint if step == 0 else hist.at[step - 1, subs]
        for k in range(pieces):
            for way in range(2):

                @pl.when(goes_on(way, 1))
                def _(way=way, k=k):
                    line_copy(step, way, 1, k, state.at[part(k), 0]).start()

        def first(right, k, step=step, state=state):
            near_copy(step, 0, right, k, state.at[part(k), 1], chip, chip_at(0, right)).start()

        def other(up, k, step=step, state=state):
            near_copy(step, up, 0, k, state.at[part(k), 1], chip, chip_at(up, 0)).start()

        each(1, width, lambda right: first(right, 0))
        each(1, tall, lambda up: other(up, 1))
        each(1, width, lambda right: first(right, 1))
        each(1, tall, lambda up: other(up, 0))
        for k in range(pieces):
            for turn in range(1, pair):
                near_mate(step, chip, turn, k, state.at[part(k), 1]).start()
                line_mate(step, level, turn, k, state.at[part(k), 0]).start()
        keep_im = pltpu.make_async_copy(
            state.at[:, 1], near[step].at[pl.ds((chip * pair + core) * count, count)], local.at[2]
        )
        keep_re = pltpu.make_async_copy(
            state.at[:, 0], line[step].at[pl.ds((core * depth + level) * count, count)], local.at[3]
        )
        keep_im.start()
        keep_re.start()
        if step == 0:
            each_ladder(lambda copy: copy.start())
            fetch.wait()
            for sub in range(subs):
                turn_saved(sub)
            take_ladders()
            tabulate()
        else:
            for sub in range(subs):
                project(step - 1, sub)
        if depth > 1:
            take_line(step, 1, 0)
        take_first(step)
        for k in range(1, pieces):
            if depth > 1:
                take_line(step, 1, k)
        take_second(step)
        keep_im.wait()
        keep_re.wait()
        take_far(step)
        reduce_start(step, 0, 1)
        if depth > 2:
            for k in range(pieces):
                take_line(step, 2, k)
        reduce_start(step, 1, depth)
        for hop in range(3, depth):
            for k in range(pieces):
                take_line(step, hop, k)
        mates_line(step)
        exchange(step)
        reduce_on(step)
        exchange_on(step)
        exchange_end(step)
        join(step, state)
        for half in range(halves):
            rotate(step, half)
            if step == steps - 1:
                for sub in range(half * batch, (half + 1) * batch):
                    project(step, sub)
                    if sub == subs - 1:
                        result = pltpu.make_async_copy(hist.at[step, subs], out, local.at[1])
                        result.start()

        for hop in range(1, depth):
            for k in range(pieces):
                for way in range(2):

                    @pl.when(goes_on(way, hop))
                    def _(way=way, hop=hop, k=k):
                        a_level = level - (hop - 1) if way == 0 else level + (hop - 1)
                        block = line_block(step, core, a_level, k)
                        line_copy(step, way, hop, k, block).wait_send()

        def done_near(up, right, step=step):
            for k in range(pieces):
                block = near_block(step, chip, core, k)
                near_copy(step, up, right, k, block, chip, chip).wait_send()

        def done_chip(at, step=step):
            up, right = split(at, width)
            done_near(up, right)

            @pl.when(right > 0)
            def _():
                row_copy(step, up, right).wait_send()

            @pl.when(up > 0)
            def _():
                col_copy(step, up, right).wait_send()

        each(1, chips, done_chip)
        each(1, tall, lambda up: col_final(step, up).wait_send())
        each(1, width, lambda right: row_final(step, right).wait_send())
        for turn in range(1, pair):

            def sent_near(a_chip, step=step, turn=turn):
                for k in range(pieces):
                    block = near_block(step, a_chip, core, k)
                    near_mate(step, a_chip, turn, k, block).wait_send()

            def sent_line(a_level, step=step, turn=turn):
                for k in range(pieces):
                    block = line_block(step, core, a_level, k)
                    line_mate(step, a_level, turn, k, block).wait_send()

            each(0, chips, sent_near)
            each(0, depth, sent_line)

        def done_z(a_level, carry, step=step):
            @pl.when(a_level != level)
            def _():
                for k in range(pieces):
                    z_copy(step, 0, a_level, k).wait_send()

            return carry

        lax.fori_loop(0, depth, done_z, 0)

    each_ladder(lambda copy: copy.wait_send())
    result.wait()
    for group in range(steps * halves):
        finish(group)


def body(adjoint, saved, propagators, coupling, higher, lower, ladder, rates, decay):
    nodes = lax.axis_size("node")
    cores = lax.axis_size("cores")
    owners = nodes * cores
    count = adjoint.shape[0]
    modes = higher.shape[1]
    steps, subs = propagators.shape[:2]
    dim = coupling.shape[0]
    depth = 1 << (cores.bit_length() // 2)
    width = cores // depth
    pair = 2 if nodes % 2 == 0 else 1
    chips = nodes // pair * width
    pieces = 2
    rows = dim // owners
    halves = 2 if subs % 2 == 0 else 1
    batch = subs // halves
    higher, lower, ladder = higher.T, lower.T, jnp.swapaxes(ladder, 1, 2)
    smem = pl.BlockSpec(memory_space=pltpu.SMEM)
    vmem = pl.BlockSpec(memory_space=pltpu.VMEM)
    block = adjoint.shape
    hbm = pl.BlockSpec(memory_space=pl.ANY)
    hops = max(depth - 1, 1)
    others = max(chips - 1, 1)
    mates = max(pair - 1, 1)
    half = (count,) + block[2:]
    bit = (count // pieces,) + block[2:]
    tall = nodes // pair
    table = (depth + chips) * count * 2 * modes
    dma = pltpu.SemaphoreType.DMA
    state, grad = pl.pallas_call(
        functools.partial(kernel, (nodes, depth, width, pair, count, modes, steps, subs, dim, halves, pieces)),
        out_shape=(
            jax.ShapeDtypeStruct(block, BF16),
            jax.ShapeDtypeStruct((rows, steps * subs, 2, dim), F32),
        ),
        in_specs=[smem] * 5 + [vmem, hbm, vmem, vmem],
        out_specs=(hbm, vmem),
        scratch_shapes=[
            pltpu.VMEM((steps * subs, 2 * dim, 2 * dim), BF16),
            pltpu.VMEM((steps * subs, 2 * dim, 2 * dim), BF16),
            pltpu.VMEM((steps, subs + 1) + block, BF16),
            pltpu.VMEM((steps, depth) + half, BF16),
            pltpu.VMEM((steps, 2, depth) + half, BF16),
            pltpu.VMEM((steps, chips) + half, BF16),
            pltpu.VMEM((steps, max(width - 1, 1), tall) + bit, BF16),
            pltpu.VMEM((steps, max(tall - 1, 1), width) + bit, BF16),
            pltpu.VMEM((steps, max(width - 1, 1)) + bit, BF16),
            pltpu.VMEM((steps, max(tall - 1, 1)) + bit, BF16),
            pltpu.VMEM((batch, dim, 2 * dim), F32),
            pltpu.VMEM((steps * halves, owners, batch * rows, 2 * dim), BF16),
            pltpu.VMEM((steps * halves, owners - 1, batch * rows, 2 * dim), BF16),
            pltpu.VMEM(saved.shape, BF16),
            pltpu.VMEM((subs, dim, count * 2 * dim), BF16),
            pltpu.SMEM((table,), jnp.int32),
            pltpu.SMEM((table,), F32),
            pltpu.SMEM((2, owners), jnp.int32),
            pltpu.SMEM((2, owners), F32),
            pltpu.SMEM((depth + chips, 2, modes, count), jnp.int32),
            dma((steps, others, pieces)),
            dma((steps, others, pieces)),
            dma((steps, mates, chips, pieces)),
            dma((steps, mates, chips, pieces)),
            dma((steps, 2, hops, pieces)),
            dma((steps, 2, hops, pieces)),
            dma((steps, mates, depth, pieces)),
            dma((steps, mates, depth, pieces)),
            dma((steps, depth, pieces)),
            dma((steps, 2, depth, pieces)),
            dma((steps, max(width - 1, 1), tall)),
            dma((steps, max(width - 1, 1), tall)),
            dma((steps, max(tall - 1, 1), width)),
            dma((steps, max(tall - 1, 1), width)),
            dma((steps, max(width - 1, 1))),
            dma((steps, max(width - 1, 1))),
            dma((steps, max(tall - 1, 1))),
            dma((steps, max(tall - 1, 1))),
            dma((depth + chips,)),
            dma((depth + chips,)),
            dma((steps * halves,)),
            dma((steps * halves,)),
            dma((4,)),
            *[pltpu.VMEM((chips * pair * count, dim, dim), BF16)] * steps,
            *[pltpu.VMEM((depth * pair * count, dim, dim), BF16)] * steps,
        ],
        compiler_params=pltpu.CompilerParams(
            collective_id=0, has_side_effects=True, vmem_limit_bytes=63_000_000
        ),
    )(higher, lower, ladder, rates, decay, adjoint, saved, propagators, coupling)
    return state, grad


def solution(mesh):
    return jax.shard_map(
        body,
        mesh=mesh,
        in_specs=(
            P(("node", "cores"), None, None, None),
            P(None, None, ("node", "cores"), None, None, None),
            P(),
            P(),
            P(),
            P(),
            P(None, ("node", "cores"), None),
            P(),
            P(("node", "cores")),
        ),
        out_specs=(P(("node", "cores"), None, None, None), P(("node", "cores"), None, None, None)),
        check_vma=False,
    )
```

```python
import functools

import jax
import jax.numpy as jnp
from jax import lax
from jax.experimental import pallas as pl
from jax.experimental.pallas import tpu as pltpu
from jax.sharding import PartitionSpec as P

MESH = pl.DeviceIdType.MESH
F32 = jnp.float32
BF16 = jnp.bfloat16


def dot(a, b):
    return jnp.dot(a, b, preferred_element_type=F32)


def kernel(
    dims,
    higher,
    lower,
    ladder,
    rates,
    decay,
    adjoint,
    saved_in,
    propagators,
    coupling,
    out,
    grad,
    right_u,
    left_u,
    hist,
    zout,
    zin,
    rout,
    row_in,
    col_in,
    row_end,
    col_end,
    terms,
    term_stage,
    term_inbox,
    saved,
    saved_t,
    place,
    weight,
    home,
    inside,
    ladders,
    near_send,
    near_recv,
    near_pass,
    near_take,
    line_send,
    line_recv,
    line_pass,
    line_take,
    z_send,
    z_recv,
    row_send,
    row_recv,
    col_send,
    col_recv,
    row_last,
    row_done,
    col_last,
    col_done,
    ladder_send,
    ladder_recv,
    term_send,
    term_recv,
    local,
    *gathered,
):
    nodes, depth, width, pair, count, modes, steps, subs, dim, halves, pieces = dims
    near, line = gathered[:steps], gathered[steps:]
    cores = depth * width
    owners = nodes * cores
    tall = nodes // pair
    chips = tall * width
    rows = dim // owners
    batch = subs // halves
    piece = count // pieces
    slots = 2 * modes
    node = lax.axis_index("node")
    spot = lax.axis_index("cores")
    level = spot // width
    column = spot % width
    side = node // pair
    core = node % pair
    chip = side * width + column

    def split(value, size):
        if size & (size - 1) == 0:
            return value >> (size.bit_length() - 1), value & (size - 1)
        return lax.div(value, size), lax.rem(value, size)

    def chip_id(other):
        return ((other // width) * pair + core, level * width + other % width)

    def chip_at(up, right):
        return lax.rem(side + up + tall, tall) * width + lax.rem(column + right + width, width)

    def mate_id(turn):
        return (side * pair + lax.rem(core + turn, pair), spot)

    def level_id(other):
        return (node, other * width + column)

    barrier = pltpu.get_barrier_semaphore()

    own = node * cores + spot

    def owner_id(offset):
        other = lax.rem(own + offset, owners)
        return (other // cores, lax.rem(other, cores))

    def greet(offset, carry):
        pl.semaphore_signal(barrier, inc=1, device_id=owner_id(offset), device_id_type=MESH)
        return carry

    lax.fori_loop(1, owners, greet, 0)
    fetch = pltpu.make_async_copy(saved_in, saved, local.at[0])
    fetch.start()

    def remote(source, target, sent, arrived, device):
        return pltpu.make_async_remote_copy(
            src_ref=source,
            dst_ref=target,
            send_sem=sent,
            recv_sem=arrived,
            device_id=device,
            device_id_type=MESH,
        )

    def part(k):
        return pl.ds(k * piece, piece)

    def near_block(step, a_chip, a_core, k):
        return near[step].at[pl.ds((a_chip * pair + a_core) * count + k * piece, piece)]

    def line_block(step, a_core, a_level, k):
        return line[step].at[pl.ds((a_core * depth + a_level) * count + k * piece, piece)]

    def near_copy(step, up, right, k, source, a_chip, target):
        at = up * width + right - 1
        return remote(
            source,
            near_block(step, a_chip, core, k),
            near_send.at[step, at, k],
            near_recv.at[step, at, k],
            chip_id(target),
        )

    def near_got(step, up, right, k):
        a_chip = chip_at(-up, -right)
        block = near_block(step, a_chip, core, k)
        near_copy(step, up, right, k, block, a_chip, a_chip).wait_recv()
        for turn in range(1, pair):
            near_mate(step, a_chip, turn, k, block).start()
        return block, a_chip

    def near_mate(step, a_chip, turn, k, source):
        return remote(
            source,
            near_block(step, a_chip, core, k),
            near_pass.at[step, turn - 1, a_chip, k],
            near_take.at[step, turn - 1, a_chip, k],
            mate_id(turn),
        )

    def line_copy(step, way, hop, k, source):
        a_level = level - (hop - 1) if way == 0 else level + (hop - 1)
        return remote(
            source,
            line_block(step, core, a_level, k),
            line_send.at[step, way, hop - 1, k],
            line_recv.at[step, way, hop - 1, k],
            level_id(level + 1 if way == 0 else level - 1),
        )

    def line_mate(step, a_level, turn, k, source):
        return remote(
            source,
            line_block(step, core, a_level, k),
            line_pass.at[step, turn - 1, a_level, k],
            line_take.at[step, turn - 1, a_level, k],
            mate_id(turn),
        )

    def z_copy(step, way, a_level, k):
        return remote(
            zout.at[step, a_level, pl.ds(k * piece, piece)],
            zin.at[step, way, a_level, pl.ds(k * piece, piece)],
            z_send.at[step, a_level, k],
            z_recv.at[step, way, a_level, k],
            level_id(level + 1 if way == 0 else level - 1),
        )

    def row_copy(step, up, right):
        return remote(
            rout.at[step, chip_at(up, right), part(0)],
            row_in.at[step, right - 1, up],
            row_send.at[step, right - 1, up],
            row_recv.at[step, right - 1, up],
            chip_id(chip_at(0, right)),
        )

    def col_copy(step, up, right):
        return remote(
            rout.at[step, chip_at(up, right), part(1)],
            col_in.at[step, up - 1, right],
            col_send.at[step, up - 1, right],
            col_recv.at[step, up - 1, right],
            chip_id(chip_at(up, 0)),
        )

    def col_final(step, up):
        return remote(
            rout.at[step, chip_at(up, 0), part(0)],
            col_end.at[step, up - 1],
            col_last.at[step, up - 1],
            col_done.at[step, up - 1],
            chip_id(chip_at(up, 0)),
        )

    def row_final(step, right):
        return remote(
            rout.at[step, chip_at(0, right), part(1)],
            row_end.at[step, right - 1],
            row_last.at[step, right - 1],
            row_done.at[step, right - 1],
            chip_id(chip_at(0, right)),
        )

    def ladder_level(other):
        return remote(
            ladder, ladders.at[level], ladder_send.at[other], ladder_recv.at[level], level_id(other)
        )

    def ladder_chip(other):
        return remote(
            ladder,
            ladders.at[depth + chip],
            ladder_send.at[depth + other],
            ladder_recv.at[depth + chip],
            chip_id(other),
        )

    def each_ladder(act):
        def one_level(other, carry):
            @pl.when(other != level)
            def _():
                act(ladder_level(other))

            return carry

        def one_chip(other, carry):
            @pl.when(other != chip)
            def _():
                act(ladder_chip(other))

            return carry

        lax.fori_loop(0, depth, one_level, 0)
        lax.fori_loop(0, chips, one_chip, 0)

    def take_ladders():
        def one_level(other, carry):
            @pl.when(other != level)
            def _():
                remote(
                    ladder,
                    ladders.at[other],
                    ladder_send.at[other],
                    ladder_recv.at[other],
                    level_id(other),
                ).wait_recv()

            return carry

        def one_chip(other, carry):
            @pl.when(other != chip)
            def _():
                remote(
                    ladder,
                    ladders.at[depth + other],
                    ladder_send.at[depth + other],
                    ladder_recv.at[depth + other],
                    chip_id(other),
                ).wait_recv()

            return carry

        lax.fori_loop(0, depth, one_level, 0)
        lax.fori_loop(0, chips, one_chip, 0)

    def tabulate():
        for way in range(2):
            for mode in range(modes):
                for j in range(count):
                    value = ladder[way, mode, j]
                    ladders[level, way, mode, j] = value
                    ladders[depth + chip, way, mode, j] = value

        def locate(owner, carry):
            a_node, a_spot = split(owner, cores)
            a_level, a_column = split(a_spot, width)
            a_side, a_core = split(a_node, pair)
            home[0, owner] = ((a_side * width + a_column) * pair + a_core) * count
            home[1, owner] = (a_core * depth + a_level) * count
            inside[0, owner] = jnp.where(a_level == level, 1.0, 0.0)
            beside = jnp.logical_and(a_side == side, a_column == column)
            inside[1, owner] = jnp.where(beside, 1.0, 0.0)
            return carry

        lax.fori_loop(0, owners, locate, 0)

        def entry(at, along_z):
            index, j = split(at, count)
            if along_z:
                target, kind, row = node * cores + index * width + column, 0, index
            else:
                a_side, a_column = split(index, width)
                target = (a_side * pair + core) * cores + level * width + a_column
                kind, row = 1, depth + index
            for way in range(2):
                for mode in range(modes):
                    source, member = split((higher, lower)[way][mode, target * count + j], count)
                    value = ladders[row, way, mode, j].astype(F32) * rates[way, mode]
                    slot = (row * count + j) * slots + way * modes + mode
                    place[slot] = home[kind, source] + member
                    weight[slot] = inside[kind, source] * value

        def entry_z(at, carry):
            entry(at, True)
            return carry

        def entry_r(at, carry):
            entry(at, False)
            return carry

        lax.fori_loop(0, depth * count, entry_z, 0)
        lax.fori_loop(0, chips * count, entry_r, 0)

    def partial(blocks, row, put):
        operator = coupling[...]

        def some(pick, carry):
            plus, minus = [], []
            for i in range(2):
                sums = []
                for way in range(2):
                    total = None
                    for mode in range(modes):
                        at = (row * count + pick * 2 + i) * slots + way * modes + mode
                        scale = jnp.full((16, dim), weight[at], F32).astype(BF16)
                        term = blocks[place[at]].reshape(dim // 16, 16, dim) * scale
                        total = term if total is None else total + term
                    sums.append(total.reshape(dim, dim))
                plus.append(sums[0] + sums[1])
                minus.append(sums[0] - sums[1])
            left = dot(operator, jnp.concatenate(plus, axis=1))
            right = dot(jnp.concatenate(minus, axis=0), operator)
            for i in range(2):
                value = left[:, i * dim : (i + 1) * dim] - right[i * dim : (i + 1) * dim]
                put(pick * 2 + i, value.astype(BF16))
            return carry

        lax.fori_loop(0, count // 2, some, 0)

    def prepare():
        def one(at, carry):
            step, sub = at // subs, at % subs
            u_re = propagators[step, sub, 0]
            u_im = propagators[step, sub, 1]
            right_u[at, :dim, :dim] = u_re
            right_u[at, :dim, dim:] = u_im
            right_u[at, dim:, :dim] = -u_im
            right_u[at, dim:, dim:] = u_re
            t_re = u_re.T
            t_im = u_im.T
            left_u[at, :dim, :dim] = t_re
            left_u[at, :dim, dim:] = t_im
            left_u[at, dim:, :dim] = -t_im
            left_u[at, dim:, dim:] = t_re
            return carry

        lax.fori_loop(0, steps * subs, one, 0)

    def turn_saved(sub):
        for j in range(count):
            kept = saved[steps - 1, sub, j].reshape(2 * dim, dim)
            saved_t[sub, :, 2 * dim * j : 2 * dim * (j + 1)] = kept.T

    def project(step, sub):
        total = jnp.zeros((dim, 2 * dim), F32)
        for j in range(count):
            lam_re = hist[step, sub + 1, j, 0]
            lam_im = hist[step, sub + 1, j, 1]
            both = jnp.concatenate(
                [
                    jnp.concatenate([lam_re, lam_im], axis=1),
                    jnp.concatenate([lam_im, -lam_re], axis=1),
                ],
                axis=0,
            )
            if step == steps - 1:
                kept_t = saved_t[sub, :, 2 * dim * j : 2 * dim * (j + 1)]
                total = total + dot(kept_t, both)
            else:
                kept = saved[step, sub, j].reshape(2 * dim, dim)
                total = total + lax.dot_general(
                    kept, both, (((0,), (0,)), ((), ())), preferred_element_type=F32
                )
        terms[step * subs + sub] = total
        if step == steps - 1 and sub % batch == batch - 1:
            spread(step * halves + sub // batch)

    def spread(group):
        for target in range(owners):
            term_stage[group, target] = jnp.concatenate(
                [
                    terms[group * batch + i, target * rows : (target + 1) * rows]
                    for i in range(batch)
                ],
                axis=0,
            ).astype(BF16)

        def send(offset, carry):
            pltpu.make_async_remote_copy(
                src_ref=term_stage.at[group, lax.rem(own + offset, owners)],
                dst_ref=term_inbox.at[group, offset - 1],
                send_sem=term_send.at[group],
                recv_sem=term_recv.at[group],
                device_id=owner_id(offset),
                device_id_type=MESH,
            ).start()
            return carry

        lax.fori_loop(1, owners, send, 0)

    def finish(group):
        everything = term_inbox.at[group]
        pltpu.make_async_copy(everything, everything, term_recv.at[group]).wait()
        total = term_stage[group, own].astype(F32)
        for offset in range(1, owners):
            total = total + term_inbox[group, offset - 1].astype(F32)
        for i in range(batch):
            for row in range(rows):
                for part in range(2):
                    grad[row, group * batch + i, part : part + 1, :] = total[
                        i * rows + row : i * rows + row + 1, part * dim : (part + 1) * dim
                    ]
        pltpu.make_async_copy(everything, everything, term_send.at[group]).wait()

    def rotate(step, half):
        def one(sub, carry):
            at = step * subs + sub
            mult_r = right_u[at]
            mult_l = left_u[at]
            for j in range(0, count, 2):
                rows = jnp.concatenate(
                    [
                        jnp.concatenate(
                            [hist[step, sub, j + i, 0], hist[step, sub, j + i, 1]], axis=1
                        )
                        for i in range(2)
                    ],
                    axis=0,
                )
                middle = dot(rows, mult_r).astype(BF16)
                stacked = jnp.concatenate(
                    [
                        jnp.concatenate([middle[:dim, :dim], middle[dim:, :dim]], axis=1),
                        jnp.concatenate([middle[:dim, dim:], middle[dim:, dim:]], axis=1),
                    ],
                    axis=0,
                )
                result = dot(mult_l, stacked).astype(BF16)
                for i in range(2):
                    for part in range(2):
                        hist[step, sub + 1, j + i, part] = result[
                            part * dim : (part + 1) * dim, i * dim : (i + 1) * dim
                        ]
            return carry

        lax.fori_loop(half * batch, (half + 1) * batch, one, 0)

    def join(step, state):
        def one(j, carry):
            lam = decay[j] * state[j, 0].astype(F32) + zout[step, level, j].astype(F32)
            hist[step, 0, j, 0] = lam.astype(BF16)
            total = rout[step, chip, j].astype(F32)
            lam = decay[j] * state[j, 1].astype(F32) - total
            hist[step, 0, j, 1] = lam.astype(BF16)
            return carry

        lax.fori_loop(0, count, one, 0)

    def fold(target, sources):
        for j in range(piece):
            total = target[j].astype(F32)
            for source in sources:
                total = total + source[j].astype(F32)
            target[j] = total.astype(BF16)

    def arrives(way, hop):
        return level >= hop if way == 0 else level + hop < depth

    def goes_on(way, hop):
        if way == 0:
            return jnp.logical_and(level >= hop - 1, level < depth - 1)
        return jnp.logical_and(level + hop - 1 < depth, level > 0)

    def take_line(step, hop, k, chosen=None):
        for way in range(2):
            due = arrives(way, hop)
            if chosen is not None:
                onward = goes_on(way, hop + 1)
                due = jnp.logical_and(due, onward if chosen else jnp.logical_not(onward))

            @pl.when(due)
            def _(way=way):
                a_level = level - hop if way == 0 else level + hop
                block = line_block(step, core, a_level, k)
                remote(
                    block,
                    block,
                    line_send.at[step, way, hop - 1, k],
                    line_recv.at[step, way, hop - 1, k],
                    level_id(level),
                ).wait_recv()
                if hop + 1 < depth:

                    @pl.when(goes_on(way, hop + 1))
                    def _():
                        line_copy(step, way, hop + 1, k, block).start()

                for turn in range(1, pair):
                    line_mate(step, a_level, turn, k, block).start()

    def each(lo, hi, act):
        def one(i, carry):
            act(i)
            return carry

        lax.fori_loop(lo, hi, one, 0)

    def take_first(step):
        def along(right):
            block, a_chip = near_got(step, 0, right, 0)
            each(
                1,
                tall,
                lambda up: near_copy(
                    step, up, right, 0, block, a_chip, chip_at(up, 0)
                ).start(),
            )

        def across(up):
            block, a_chip = near_got(step, up, 0, 1)
            each(
                1,
                width,
                lambda right: near_copy(
                    step, up, right, 1, block, a_chip, chip_at(0, right)
                ).start(),
            )

        each(1, width, along)
        each(1, tall, across)

    def take_second(step):
        each(1, width, lambda right: near_got(step, 0, right, 1) and None)
        each(1, tall, lambda up: near_got(step, up, 0, 0) and None)

    def take_far(step):
        def one(up):
            def two(right):
                for k in range(pieces):
                    near_got(step, up, right, k)

            each(1, width, two)

        each(1, tall, one)
        for turn in range(1, pair):

            def two(a_chip, turn=turn):
                for k in range(pieces):
                    block = near_block(step, a_chip, lax.rem(core + pair - turn, pair), k)
                    near_mate(step, a_chip, turn, k, block).wait_recv()

            each(0, chips, two)

    def mates_line(step):
        for turn in range(1, pair):

            def two(a_level, turn=turn):
                for k in range(pieces):
                    block = line_block(step, lax.rem(core + pair - turn, pair), a_level, k)
                    line_mate(step, a_level, turn, k, block).wait_recv()

            each(0, depth, two)

    def reduce_start(step, lo, hi):
        def one(i, carry):
            a_level = jnp.where(level * 2 < depth, depth - 1 - i, i)

            def put(j, value):
                zout[step, a_level, j] = value

            partial(near[step], a_level, put)

            def send(way):
                for k in range(pieces):
                    z_copy(step, way, a_level, k).start()

            pl.when(jnp.logical_and(level == 0, a_level > 0))(lambda: send(0))
            pl.when(jnp.logical_and(level == depth - 1, a_level < depth - 1))(lambda: send(1))
            return carry

        lax.fori_loop(lo, hi, one, 0)

    def exchange(step):
        def one(i):
            up, right = split(chips - 1 - i, width)
            target = chip_at(up, right)

            def put(j, value):
                rout[step, target, j] = value

            partial(line[step], depth + target, put)

            @pl.when(right > 0)
            def _():
                row_copy(step, up, right).start()

            @pl.when(up > 0)
            def _():
                col_copy(step, up, right).start()

        each(0, chips, one)

    def exchange_on(step):
        def column(up):
            target = chip_at(up, 0)
            each(1, width, lambda right: row_copy(step, up, right).wait_recv())
            fold(
                rout.at[step, target, part(0)],
                [row_in.at[step, right - 1, up] for right in range(1, width)],
            )
            col_final(step, up).start()

        def line_of(right):
            target = chip_at(0, right)
            each(1, tall, lambda up: col_copy(step, up, right).wait_recv())
            fold(
                rout.at[step, target, part(1)],
                [col_in.at[step, up - 1, right] for up in range(1, tall)],
            )
            row_final(step, right).start()

        each(1, tall, column)
        each(1, width, line_of)

    def exchange_end(step):
        each(1, width, lambda right: row_copy(step, 0, right).wait_recv())
        each(1, tall, lambda up: col_copy(step, up, 0).wait_recv())
        each(1, tall, lambda up: col_final(step, up).wait_recv())
        each(1, width, lambda right: row_final(step, right).wait_recv())
        fold(
            rout.at[step, chip, part(0)],
            [row_in.at[step, right - 1, 0] for right in range(1, width)]
            + [col_end.at[step, up - 1] for up in range(1, tall)],
        )
        fold(
            rout.at[step, chip, part(1)],
            [col_in.at[step, up - 1, 0] for up in range(1, tall)]
            + [row_end.at[step, right - 1] for right in range(1, width)],
        )

    def reduce_on(step, ahead):
        for k in range(pieces):
            for way in range(2):
                if way == 0:
                    a_level = level + ahead
                    fits = jnp.logical_and(level > 0, a_level < depth)
                else:
                    a_level = level - ahead
                    fits = jnp.logical_and(level < depth - 1, a_level >= 0)

                @pl.when(fits)
                def _(way=way, k=k, a_level=a_level):
                    z_copy(step, way, a_level, k).wait_recv()
                    fold(
                        zout.at[step, a_level, part(k)], [zin.at[step, way, a_level, part(k)]]
                    )
                    if ahead > 0:
                        z_copy(step, way, a_level, k).start()

    prepare()
    pl.semaphore_wait(barrier, owners - 1)
    each_ladder(lambda copy: copy.start())
    for step in range(steps):
        state = adjoint if step == 0 else hist.at[step - 1, subs]
        for k in range(pieces):
            for way in range(2):

                @pl.when(goes_on(way, 1))
                def _(way=way, k=k):
                    line_copy(step, way, 1, k, state.at[part(k), 0]).start()

        def first(right, k, step=step, state=state):
            near_copy(step, 0, right, k, state.at[part(k), 1], chip, chip_at(0, right)).start()

        def other(up, k, step=step, state=state):
            near_copy(step, up, 0, k, state.at[part(k), 1], chip, chip_at(up, 0)).start()

        each(1, width, lambda right: first(right, 0))
        each(1, tall, lambda up: other(up, 1))
        each(1, width, lambda right: first(right, 1))
        each(1, tall, lambda up: other(up, 0))
        for k in range(pieces):
            for turn in range(1, pair):
                near_mate(step, chip, turn, k, state.at[part(k), 1]).start()
                line_mate(step, level, turn, k, state.at[part(k), 0]).start()
        keep_im = pltpu.make_async_copy(
            state.at[:, 1], near[step].at[pl.ds((chip * pair + core) * count, count)], local.at[2]
        )
        keep_re = pltpu.make_async_copy(
            state.at[:, 0], line[step].at[pl.ds((core * depth + level) * count, count)], local.at[3]
        )
        keep_im.start()
        keep_re.start()
        if step == 0:
            fetch.wait()
            for sub in range(subs):
                turn_saved(sub)
            take_ladders()
            tabulate()
        else:
            for sub in range(subs):
                project(step - 1, sub)
        if depth > 1:
            take_line(step, 1, 0)
        take_first(step)
        for k in range(1, pieces):
            if depth > 1:
                take_line(step, 1, k)
        take_second(step)
        keep_im.wait()
        keep_re.wait()
        take_far(step)
        reduce_start(step, 0, 1)
        if depth > 2:
            for k in range(pieces):
                take_line(step, 2, k, True)
        reduce_start(step, 1, depth)
        reduce_on(step, depth - 2)
        if depth > 2:
            for k in range(pieces):
                take_line(step, 2, k, False)
        for hop in range(3, depth):
            for k in range(pieces):
                take_line(step, hop, k)
        mates_line(step)
        exchange(step)
        for ahead in range(depth - 3, 0, -1):
            reduce_on(step, ahead)
        exchange_on(step)
        if depth != 2:
            reduce_on(step, 0)
        exchange_end(step)
        if step > 0:
            for half in range(halves):
                spread((step - 1) * halves + half)
        join(step, state)
        for half in range(halves):
            rotate(step, half)
            if step == steps - 1:
                for sub in range(half * batch, (half + 1) * batch):
                    project(step, sub)
                    if sub == subs - 1:
                        result = pltpu.make_async_copy(hist.at[step, subs], out, local.at[1])
                        result.start()

        for hop in range(1, depth):
            for k in range(pieces):
                for way in range(2):

                    @pl.when(goes_on(way, hop))
                    def _(way=way, hop=hop, k=k):
                        a_level = level - (hop - 1) if way == 0 else level + (hop - 1)
                        block = line_block(step, core, a_level, k)
                        line_copy(step, way, hop, k, block).wait_send()

        def done_near(up, right, step=step):
            for k in range(pieces):
                block = near_block(step, chip, core, k)
                near_copy(step, up, right, k, block, chip, chip).wait_send()

        def done_chip(at, step=step):
            up, right = split(at, width)
            done_near(up, right)

            @pl.when(right > 0)
            def _():
                row_copy(step, up, right).wait_send()

            @pl.when(up > 0)
            def _():
                col_copy(step, up, right).wait_send()

        each(1, chips, done_chip)
        each(1, tall, lambda up: col_final(step, up).wait_send())
        each(1, width, lambda right: row_final(step, right).wait_send())
        for turn in range(1, pair):

            def sent_near(a_chip, step=step, turn=turn):
                for k in range(pieces):
                    block = near_block(step, a_chip, core, k)
                    near_mate(step, a_chip, turn, k, block).wait_send()

            def sent_line(a_level, step=step, turn=turn):
                for k in range(pieces):
                    block = line_block(step, core, a_level, k)
                    line_mate(step, a_level, turn, k, block).wait_send()

            each(0, chips, sent_near)
            each(0, depth, sent_line)

        def done_z(a_level, carry, step=step):
            @pl.when(a_level != level)
            def _():
                for k in range(pieces):
                    z_copy(step, 0, a_level, k).wait_send()

            return carry

        lax.fori_loop(0, depth, done_z, 0)

    each_ladder(lambda copy: copy.wait_send())
    result.wait()
    for group in range(steps * halves):
        finish(group)


def body(adjoint, saved, propagators, coupling, higher, lower, ladder, rates, decay):
    nodes = lax.axis_size("node")
    cores = lax.axis_size("cores")
    owners = nodes * cores
    count = adjoint.shape[0]
    modes = higher.shape[1]
    steps, subs = propagators.shape[:2]
    dim = coupling.shape[0]
    depth = 1 << (cores.bit_length() // 2)
    width = cores // depth
    pair = 2 if nodes % 2 == 0 else 1
    chips = nodes // pair * width
    pieces = 2
    rows = dim // owners
    halves = 2 if subs % 2 == 0 else 1
    batch = subs // halves
    higher, lower, ladder = higher.T, lower.T, jnp.swapaxes(ladder, 1, 2)
    smem = pl.BlockSpec(memory_space=pltpu.SMEM)
    vmem = pl.BlockSpec(memory_space=pltpu.VMEM)
    block = adjoint.shape
    hbm = pl.BlockSpec(memory_space=pl.ANY)
    hops = max(depth - 1, 1)
    others = max(chips - 1, 1)
    mates = max(pair - 1, 1)
    half = (count,) + block[2:]
    bit = (count // pieces,) + block[2:]
    tall = nodes // pair
    table = (depth + chips) * count * 2 * modes
    dma = pltpu.SemaphoreType.DMA
    state, grad = pl.pallas_call(
        functools.partial(kernel, (nodes, depth, width, pair, count, modes, steps, subs, dim, halves, pieces)),
        out_shape=(
            jax.ShapeDtypeStruct(block, BF16),
            jax.ShapeDtypeStruct((rows, steps * subs, 2, dim), F32),
        ),
        in_specs=[smem] * 5 + [vmem, hbm, vmem, vmem],
        out_specs=(hbm, vmem),
        scratch_shapes=[
            pltpu.VMEM((steps * subs, 2 * dim, 2 * dim), BF16),
            pltpu.VMEM((steps * subs, 2 * dim, 2 * dim), BF16),
            pltpu.VMEM((steps, subs + 1) + block, BF16),
            pltpu.VMEM((steps, depth) + half, BF16),
            pltpu.VMEM((steps, 2, depth) + half, BF16),
            pltpu.VMEM((steps, chips) + half, BF16),
            pltpu.VMEM((steps, max(width - 1, 1), tall) + bit, BF16),
            pltpu.VMEM((steps, max(tall - 1, 1), width) + bit, BF16),
            pltpu.VMEM((steps, max(width - 1, 1)) + bit, BF16),
            pltpu.VMEM((steps, max(tall - 1, 1)) + bit, BF16),
            pltpu.VMEM((steps * subs, dim, 2 * dim), F32),
            pltpu.VMEM((steps * halves, owners, batch * rows, 2 * dim), BF16),
            pltpu.VMEM((steps * halves, owners - 1, batch * rows, 2 * dim), BF16),
            pltpu.VMEM(saved.shape, BF16),
            pltpu.VMEM((subs, dim, count * 2 * dim), BF16),
            pltpu.SMEM((table,), jnp.int32),
            pltpu.SMEM((table,), F32),
            pltpu.SMEM((2, owners), jnp.int32),
            pltpu.SMEM((2, owners), F32),
            pltpu.SMEM((depth + chips, 2, modes, count), jnp.int32),
            dma((steps, others, pieces)),
            dma((steps, others, pieces)),
            dma((steps, mates, chips, pieces)),
            dma((steps, mates, chips, pieces)),
            dma((steps, 2, hops, pieces)),
            dma((steps, 2, hops, pieces)),
            dma((steps, mates, depth, pieces)),
            dma((steps, mates, depth, pieces)),
            dma((steps, depth, pieces)),
            dma((steps, 2, depth, pieces)),
            dma((steps, max(width - 1, 1), tall)),
            dma((steps, max(width - 1, 1), tall)),
            dma((steps, max(tall - 1, 1), width)),
            dma((steps, max(tall - 1, 1), width)),
            dma((steps, max(width - 1, 1))),
            dma((steps, max(width - 1, 1))),
            dma((steps, max(tall - 1, 1))),
            dma((steps, max(tall - 1, 1))),
            dma((depth + chips,)),
            dma((depth + chips,)),
            dma((steps * halves,)),
            dma((steps * halves,)),
            dma((4,)),
            *[pltpu.VMEM((chips * pair * count, dim, dim), BF16)] * steps,
            *[pltpu.VMEM((depth * pair * count, dim, dim), BF16)] * steps,
        ],
        compiler_params=pltpu.CompilerParams(
            collective_id=0, has_side_effects=True, vmem_limit_bytes=63_000_000
        ),
    )(higher, lower, ladder, rates, decay, adjoint, saved, propagators, coupling)
    return state, grad


def solution(mesh):
    return jax.shard_map(
        body,
        mesh=mesh,
        in_specs=(
            P(("node", "cores"), None, None, None),
            P(None, None, ("node", "cores"), None, None, None),
            P(),
            P(),
            P(),
            P(),
            P(None, ("node", "cores"), None),
            P(),
            P(("node", "cores")),
        ),
        out_specs=(P(("node", "cores"), None, None, None), P(("node", "cores"), None, None, None)),
        check_vma=False,
    )
```

```python
import functools

import jax
import jax.numpy as jnp
from jax import lax
from jax.experimental import pallas as pl
from jax.experimental.pallas import tpu as pltpu
from jax.sharding import PartitionSpec as P

MESH = pl.DeviceIdType.MESH
F32 = jnp.float32
BF16 = jnp.bfloat16


def dot(a, b):
    return jnp.dot(a, b, preferred_element_type=F32)


def kernel(
    dims,
    higher,
    lower,
    ladder,
    rates,
    decay,
    adjoint,
    saved_in,
    propagators_in,
    coupling,
    out,
    grad,
    right_u,
    left_u,
    hist,
    zout,
    zin,
    rout,
    row_in,
    col_in,
    row_end,
    col_end,
    terms,
    term_stage,
    term_inbox,
    saved,
    saved_t,
    place,
    weight,
    home,
    inside,
    ladders,
    near_send,
    near_recv,
    near_pass,
    near_take,
    line_send,
    line_recv,
    line_pass,
    line_take,
    z_send,
    z_recv,
    row_send,
    row_recv,
    col_send,
    col_recv,
    row_last,
    row_done,
    col_last,
    col_done,
    ladder_send,
    ladder_recv,
    term_send,
    term_recv,
    hello,
    again,
    local,
    propagators,
    held,
    *gathered,
):
    nodes, depth, width, pair, count, modes, steps, subs, dim, halves, pieces = dims
    near, line = gathered[:steps], gathered[steps:]
    cores = depth * width
    owners = nodes * cores
    tall = nodes // pair
    chips = tall * width
    rows = dim // owners
    batch = subs // halves
    piece = count // pieces
    slots = 2 * modes
    node = lax.axis_index("node")
    spot = lax.axis_index("cores")
    level = spot // width
    column = spot % width
    side = node // pair
    core = node % pair
    chip = side * width + column

    def split(value, size):
        if size & (size - 1) == 0:
            return value >> (size.bit_length() - 1), value & (size - 1)
        return lax.div(value, size), lax.rem(value, size)

    def chip_id(other):
        return ((other // width) * pair + core, level * width + other % width)

    def chip_at(up, right):
        return lax.rem(side + up + tall, tall) * width + lax.rem(column + right + width, width)

    def mate_id(turn):
        return (side * pair + lax.rem(core + turn, pair), spot)

    def level_id(other):
        return (node, other * width + column)

    barrier = pltpu.get_barrier_semaphore()

    own = node * cores + spot

    def owner_id(offset):
        other = lax.rem(own + offset, owners)
        return (other // cores, lax.rem(other, cores))

    def each(lo, hi, act):
        def one(i, carry):
            act(i)
            return carry

        lax.fori_loop(lo, hi, one, 0)

    def signal(semaphore, device):
        pl.semaphore_signal(semaphore, inc=1, device_id=device, device_id_type=MESH)

    def greet_levels(semaphore):
        def greet(other):
            pl.when(other != level)(lambda: signal(semaphore, level_id(other)))

        each(0, depth, greet)

    def greet_mates(semaphore):
        for turn in range(1, pair):
            signal(semaphore, mate_id(turn))

    def greet_chips(semaphore):
        def greet(other):
            pl.when(other != chip)(lambda: signal(semaphore, chip_id(other)))

        each(0, chips, greet)

    greet_levels(barrier)
    greet_chips(barrier)
    greet_mates(barrier)
    load_u = pltpu.make_async_copy(propagators_in, propagators, local.at[4])
    load_u.start()
    load = pltpu.make_async_copy(adjoint, held, local.at[5])
    load.start()
    fetch = pltpu.make_async_copy(saved_in, saved, local.at[0])
    fetch.start()

    def remote(source, target, sent, arrived, device):
        return pltpu.make_async_remote_copy(
            src_ref=source,
            dst_ref=target,
            send_sem=sent,
            recv_sem=arrived,
            device_id=device,
            device_id_type=MESH,
        )

    def part(k):
        return pl.ds(k * piece, piece)

    def near_block(step, a_chip, a_core, k):
        return near[step].at[pl.ds((a_chip * pair + a_core) * count + k * piece, piece)]

    def line_block(step, a_core, a_level, k):
        return line[step].at[pl.ds((a_core * depth + a_level) * count + k * piece, piece)]

    def near_copy(step, up, right, k, source, a_chip, target):
        at = up * width + right - 1
        return remote(
            source,
            near_block(step, a_chip, core, k),
            near_send.at[step, at, k],
            near_recv.at[step, at, k],
            chip_id(target),
        )

    def near_got(step, up, right, k):
        a_chip = chip_at(-up, -right)
        block = near_block(step, a_chip, core, k)
        near_copy(step, up, right, k, block, a_chip, a_chip).wait_recv()
        for turn in range(1, pair):
            near_mate(step, a_chip, turn, k, block).start()
        return block, a_chip

    def near_mate(step, a_chip, turn, k, source):
        return remote(
            source,
            near_block(step, a_chip, core, k),
            near_pass.at[step, turn - 1, a_chip, k],
            near_take.at[step, turn - 1, a_chip, k],
            mate_id(turn),
        )

    def line_copy(step, way, hop, k, source):
        a_level = level - (hop - 1) if way == 0 else level + (hop - 1)
        return remote(
            source,
            line_block(step, core, a_level, k),
            line_send.at[step, way, hop - 1, k],
            line_recv.at[step, way, hop - 1, k],
            level_id(level + 1 if way == 0 else level - 1),
        )

    def line_mate(step, a_level, turn, k, source):
        return remote(
            source,
            line_block(step, core, a_level, k),
            line_pass.at[step, turn - 1, a_level, k],
            line_take.at[step, turn - 1, a_level, k],
            mate_id(turn),
        )

    def z_copy(step, way, a_level, k):
        return remote(
            zout.at[step, a_level, pl.ds(k * piece, piece)],
            zin.at[step, way, a_level, pl.ds(k * piece, piece)],
            z_send.at[step, a_level, k],
            z_recv.at[step, way, a_level, k],
            level_id(level + 1 if way == 0 else level - 1),
        )

    def row_copy(step, up, right):
        return remote(
            rout.at[step, chip_at(up, right), part(0)],
            row_in.at[step, right - 1, up],
            row_send.at[step, right - 1, up],
            row_recv.at[step, right - 1, up],
            chip_id(chip_at(0, right)),
        )

    def col_copy(step, up, right):
        return remote(
            rout.at[step, chip_at(up, right), part(1)],
            col_in.at[step, up - 1, right],
            col_send.at[step, up - 1, right],
            col_recv.at[step, up - 1, right],
            chip_id(chip_at(up, 0)),
        )

    def col_final(step, up):
        return remote(
            rout.at[step, chip_at(up, 0), part(0)],
            col_end.at[step, up - 1],
            col_last.at[step, up - 1],
            col_done.at[step, up - 1],
            chip_id(chip_at(up, 0)),
        )

    def row_final(step, right):
        return remote(
            rout.at[step, chip_at(0, right), part(1)],
            row_end.at[step, right - 1],
            row_last.at[step, right - 1],
            row_done.at[step, right - 1],
            chip_id(chip_at(0, right)),
        )

    def ladder_level(other):
        return remote(
            ladder, ladders.at[level], ladder_send.at[other], ladder_recv.at[level], level_id(other)
        )

    def ladder_chip(other):
        return remote(
            ladder,
            ladders.at[depth + chip],
            ladder_send.at[depth + other],
            ladder_recv.at[depth + chip],
            chip_id(other),
        )

    def each_ladder(act):
        def one_level(other, carry):
            @pl.when(other != level)
            def _():
                act(ladder_level(other))

            return carry

        def one_chip(other, carry):
            @pl.when(other != chip)
            def _():
                act(ladder_chip(other))

            return carry

        lax.fori_loop(0, depth, one_level, 0)
        lax.fori_loop(0, chips, one_chip, 0)

    def take_ladders():
        def one_level(other, carry):
            @pl.when(other != level)
            def _():
                remote(
                    ladder,
                    ladders.at[other],
                    ladder_send.at[other],
                    ladder_recv.at[other],
                    level_id(other),
                ).wait_recv()

            return carry

        def one_chip(other, carry):
            @pl.when(other != chip)
            def _():
                remote(
                    ladder,
                    ladders.at[depth + other],
                    ladder_send.at[depth + other],
                    ladder_recv.at[depth + other],
                    chip_id(other),
                ).wait_recv()

            return carry

        lax.fori_loop(0, depth, one_level, 0)
        lax.fori_loop(0, chips, one_chip, 0)

    def note_own():
        for way in range(2):
            for mode in range(modes):
                for j in range(count):
                    value = ladder[way, mode, j]
                    ladders[level, way, mode, j] = value
                    ladders[depth + chip, way, mode, j] = value

        def locate(owner, carry):
            a_node, a_spot = split(owner, cores)
            a_level, a_column = split(a_spot, width)
            a_side, a_core = split(a_node, pair)
            home[0, owner] = ((a_side * width + a_column) * pair + a_core) * count
            home[1, owner] = (a_core * depth + a_level) * count
            inside[0, owner] = jnp.where(a_level == level, 1.0, 0.0)
            beside = jnp.logical_and(a_side == side, a_column == column)
            inside[1, owner] = jnp.where(beside, 1.0, 0.0)
            return carry

        lax.fori_loop(0, owners, locate, 0)

    def tabulate(along_z):
        def entry(at):
            index, j = split(at, count)
            if along_z:
                target, kind, row = node * cores + index * width + column, 0, index
            else:
                a_side, a_column = split(index, width)
                target = (a_side * pair + core) * cores + level * width + a_column
                kind, row = 1, depth + index
            for way in range(2):
                for mode in range(modes):
                    source, member = split((higher, lower)[way][mode, target * count + j], count)
                    value = ladders[row, way, mode, j].astype(F32) * rates[way, mode]
                    slot = (row * count + j) * slots + way * modes + mode
                    place[slot] = home[kind, source] + member
                    weight[slot] = inside[kind, source] * value

        each(0, (depth if along_z else chips) * count, entry)

    def partial(blocks, row, k, put):
        operator = coupling[...]

        def some(pick, carry):
            plus, minus = [], []
            for i in range(2):
                sums = []
                for way in range(2):
                    total = None
                    for mode in range(modes):
                        at = (row * count + pick * 2 + i) * slots + way * modes + mode
                        scale = jnp.full((16, dim), weight[at], F32).astype(BF16)
                        term = blocks[place[at]].reshape(dim // 16, 16, dim) * scale
                        total = term if total is None else total + term
                    sums.append(total.reshape(dim, dim))
                plus.append(sums[0] + sums[1])
                minus.append(sums[0] - sums[1])
            left = dot(operator, jnp.concatenate(plus, axis=1))
            right = dot(jnp.concatenate(minus, axis=0), operator)
            for i in range(2):
                value = left[:, i * dim : (i + 1) * dim] - right[i * dim : (i + 1) * dim]
                put(pick * 2 + i, value.astype(BF16))
            return carry

        lax.fori_loop(k * piece // 2, (k + 1) * piece // 2, some, 0)

    def prepare():
        def one(at, carry):
            step, sub = at // subs, at % subs
            u_re = propagators[step, sub, 0]
            u_im = propagators[step, sub, 1]
            right_u[at, :dim, :dim] = u_re
            right_u[at, :dim, dim:] = u_im
            right_u[at, dim:, :dim] = -u_im
            right_u[at, dim:, dim:] = u_re
            t_re = u_re.T
            t_im = u_im.T
            left_u[at, :dim, :dim] = t_re
            left_u[at, :dim, dim:] = t_im
            left_u[at, dim:, :dim] = -t_im
            left_u[at, dim:, dim:] = t_re
            return carry

        lax.fori_loop(0, steps * subs, one, 0)

    def turn_saved(sub):
        for j in range(count):
            kept = saved[steps - 1, sub, j].reshape(2 * dim, dim)
            saved_t[sub, :, 2 * dim * j : 2 * dim * (j + 1)] = kept.T

    def project(step, sub):
        total = jnp.zeros((dim, 2 * dim), F32)
        for j in range(count):
            lam_re = hist[step, sub + 1, j, 0]
            lam_im = hist[step, sub + 1, j, 1]
            both = jnp.concatenate(
                [
                    jnp.concatenate([lam_re, lam_im], axis=1),
                    jnp.concatenate([lam_im, -lam_re], axis=1),
                ],
                axis=0,
            )
            if step == steps - 1:
                kept_t = saved_t[sub, :, 2 * dim * j : 2 * dim * (j + 1)]
                total = total + dot(kept_t, both)
            else:
                kept = saved[step, sub, j].reshape(2 * dim, dim)
                total = total + lax.dot_general(
                    kept, both, (((0,), (0,)), ((), ())), preferred_element_type=F32
                )
        terms[step * subs + sub] = total
        if step == steps - 1 and sub % batch == batch - 1:
            stage(step * halves + sub // batch)
            spread(step * halves + sub // batch)

    def stage(group):
        for target in range(owners):
            term_stage[group, target] = jnp.concatenate(
                [
                    terms[group * batch + i, target * rows : (target + 1) * rows]
                    for i in range(batch)
                ],
                axis=0,
            ).astype(BF16)

    def spread(group):
        def send(offset, carry):
            pltpu.make_async_remote_copy(
                src_ref=term_stage.at[group, lax.rem(own + offset, owners)],
                dst_ref=term_inbox.at[group, offset - 1],
                send_sem=term_send.at[group],
                recv_sem=term_recv.at[group],
                device_id=owner_id(offset),
                device_id_type=MESH,
            ).start()
            return carry

        lax.fori_loop(1, owners, send, 0)

    def finish(group):
        everything = term_inbox.at[group]
        pltpu.make_async_copy(everything, everything, term_recv.at[group]).wait()
        total = term_stage[group, own].astype(F32)
        for offset in range(1, owners):
            total = total + term_inbox[group, offset - 1].astype(F32)
        for i in range(batch):
            for row in range(rows):
                for part in range(2):
                    grad[row, group * batch + i, part : part + 1, :] = total[
                        i * rows + row : i * rows + row + 1, part * dim : (part + 1) * dim
                    ]
        pltpu.make_async_copy(everything, everything, term_send.at[group]).wait()

    def rotate(step, half):
        def one(sub, carry):
            at = step * subs + sub
            mult_r = right_u[at]
            mult_l = left_u[at]
            for j in range(0, count, 2):
                rows = jnp.concatenate(
                    [
                        jnp.concatenate(
                            [hist[step, sub, j + i, 0], hist[step, sub, j + i, 1]], axis=1
                        )
                        for i in range(2)
                    ],
                    axis=0,
                )
                middle = dot(rows, mult_r).astype(BF16)
                stacked = jnp.concatenate(
                    [
                        jnp.concatenate([middle[:dim, :dim], middle[dim:, :dim]], axis=1),
                        jnp.concatenate([middle[:dim, dim:], middle[dim:, dim:]], axis=1),
                    ],
                    axis=0,
                )
                result = dot(mult_l, stacked).astype(BF16)
                for i in range(2):
                    for part in range(2):
                        hist[step, sub + 1, j + i, part] = result[
                            part * dim : (part + 1) * dim, i * dim : (i + 1) * dim
                        ]
            return carry

        lax.fori_loop(half * batch, (half + 1) * batch, one, 0)

    def join(step, state):
        def one(j, carry):
            lam = decay[j] * state[j, 0].astype(F32) + zout[step, level, j].astype(F32)
            hist[step, 0, j, 0] = lam.astype(BF16)
            total = rout[step, chip, j].astype(F32)
            lam = decay[j] * state[j, 1].astype(F32) - total
            hist[step, 0, j, 1] = lam.astype(BF16)
            return carry

        lax.fori_loop(0, count, one, 0)

    def fold(target, sources):
        for j in range(piece):
            total = target[j].astype(F32)
            for source in sources:
                total = total + source[j].astype(F32)
            target[j] = total.astype(BF16)

    def arrives(way, hop):
        return level >= hop if way == 0 else level + hop < depth

    def goes_on(way, hop):
        if way == 0:
            return jnp.logical_and(level >= hop - 1, level < depth - 1)
        return jnp.logical_and(level + hop - 1 < depth, level > 0)

    def take_line(step, hop, k, chosen=None):
        for way in range(2):
            due = arrives(way, hop)
            if chosen is not None:
                onward = goes_on(way, hop + 1)
                due = jnp.logical_and(due, onward if chosen else jnp.logical_not(onward))

            @pl.when(due)
            def _(way=way):
                a_level = level - hop if way == 0 else level + hop
                block = line_block(step, core, a_level, k)
                remote(
                    block,
                    block,
                    line_send.at[step, way, hop - 1, k],
                    line_recv.at[step, way, hop - 1, k],
                    level_id(level),
                ).wait_recv()
                if hop + 1 < depth:

                    @pl.when(goes_on(way, hop + 1))
                    def _():
                        line_copy(step, way, hop + 1, k, block).start()

                for turn in range(1, pair):
                    line_mate(step, a_level, turn, k, block).start()

    def take_first(step):
        def along(right):
            block, a_chip = near_got(step, 0, right, 0)
            each(
                1,
                tall,
                lambda up: near_copy(
                    step, up, right, 0, block, a_chip, chip_at(up, 0)
                ).start(),
            )

        def across(up):
            block, a_chip = near_got(step, up, 0, 1)
            each(
                1,
                width,
                lambda right: near_copy(
                    step, up, right, 1, block, a_chip, chip_at(0, right)
                ).start(),
            )

        each(1, width, along)
        each(1, tall, across)

    def take_second(step):
        each(1, width, lambda right: near_got(step, 0, right, 1) and None)
        each(1, tall, lambda up: near_got(step, up, 0, 0) and None)

    def take_far(step):
        def one(up):
            def two(right):
                for k in range(pieces):
                    near_got(step, up, right, k)

            each(1, width, two)

        each(1, tall, one)
        for turn in range(1, pair):

            def two(a_chip, turn=turn):
                for k in range(pieces):
                    block = near_block(step, a_chip, lax.rem(core + pair - turn, pair), k)
                    near_mate(step, a_chip, turn, k, block).wait_recv()

            each(0, chips, two)

    def mates_line(step):
        for turn in range(1, pair):

            def two(a_level, turn=turn):
                for k in range(pieces):
                    block = line_block(step, lax.rem(core + pair - turn, pair), a_level, k)
                    line_mate(step, a_level, turn, k, block).wait_recv()

            each(0, depth, two)

    def reduce_start(step, lo, hi):
        def one(i, carry):
            a_level = jnp.where(level * 2 < depth, depth - 1 - i, i)

            def put(j, value):
                zout[step, a_level, j] = value

            for k in range(pieces):
                partial(near[step], a_level, k, put)

                @pl.when(jnp.logical_and(level == 0, a_level > 0))
                def _(k=k):
                    z_copy(step, 0, a_level, k).start()

                @pl.when(jnp.logical_and(level == depth - 1, a_level < depth - 1))
                def _(k=k):
                    z_copy(step, 1, a_level, k).start()

            return carry

        lax.fori_loop(lo, hi, one, 0)

    def exchange(step):
        def one(i):
            up, right = split(chips - 1 - i, width)
            target = chip_at(up, right)

            def put(j, value):
                rout[step, target, j] = value

            partial(line[step], depth + target, 0, put)

            @pl.when(right > 0)
            def _():
                row_copy(step, up, right).start()

            for k in range(1, pieces):
                partial(line[step], depth + target, k, put)

            @pl.when(up > 0)
            def _():
                col_copy(step, up, right).start()

        each(0, chips, one)

    def exchange_on(step):
        def column(up):
            target = chip_at(up, 0)
            each(1, width, lambda right: row_copy(step, up, right).wait_recv())
            fold(
                rout.at[step, target, part(0)],
                [row_in.at[step, right - 1, up] for right in range(1, width)],
            )
            col_final(step, up).start()

        def line_of(right):
            target = chip_at(0, right)
            each(1, tall, lambda up: col_copy(step, up, right).wait_recv())
            fold(
                rout.at[step, target, part(1)],
                [col_in.at[step, up - 1, right] for up in range(1, tall)],
            )
            row_final(step, right).start()

        each(1, tall, column)
        each(1, width, line_of)

    def exchange_end(step):
        each(1, width, lambda right: row_copy(step, 0, right).wait_recv())
        each(1, tall, lambda up: col_copy(step, up, 0).wait_recv())
        each(1, tall, lambda up: col_final(step, up).wait_recv())
        each(1, width, lambda right: row_final(step, right).wait_recv())
        fold(
            rout.at[step, chip, part(0)],
            [row_in.at[step, right - 1, 0] for right in range(1, width)]
            + [col_end.at[step, up - 1] for up in range(1, tall)],
        )
        fold(
            rout.at[step, chip, part(1)],
            [col_in.at[step, up - 1, 0] for up in range(1, tall)]
            + [row_end.at[step, right - 1] for right in range(1, width)],
        )

    def reduce_on(step, ahead):
        for k in range(pieces):
            for way in range(2):
                if way == 0:
                    a_level = level + ahead
                    fits = jnp.logical_and(level > 0, a_level < depth)
                else:
                    a_level = level - ahead
                    fits = jnp.logical_and(level < depth - 1, a_level >= 0)

                @pl.when(fits)
                def _(way=way, k=k, a_level=a_level):
                    z_copy(step, way, a_level, k).wait_recv()
                    fold(
                        zout.at[step, a_level, part(k)], [zin.at[step, way, a_level, part(k)]]
                    )
                    if ahead > 0:
                        z_copy(step, way, a_level, k).start()

    pl.semaphore_wait(barrier, depth + chips + pair - 3)
    each_ladder(lambda copy: copy.start())
    for step in range(steps):
        state = adjoint if step == 0 else hist.at[step - 1, subs]
        for k in range(pieces):
            for way in range(2):

                @pl.when(goes_on(way, 1))
                def _(way=way, k=k):
                    line_copy(step, way, 1, k, state.at[part(k), 0]).start()

        def first(right, k, step=step, state=state):
            near_copy(step, 0, right, k, state.at[part(k), 1], chip, chip_at(0, right)).start()

        def other(up, k, step=step, state=state):
            near_copy(step, up, 0, k, state.at[part(k), 1], chip, chip_at(up, 0)).start()

        each(1, width, lambda right: first(right, 0))
        each(1, tall, lambda up: other(up, 1))
        each(1, width, lambda right: first(right, 1))
        each(1, tall, lambda up: other(up, 0))
        for k in range(pieces):
            for turn in range(1, pair):
                near_mate(step, chip, turn, k, state.at[part(k), 1]).start()
                line_mate(step, level, turn, k, state.at[part(k), 0]).start()
        keep_im = pltpu.make_async_copy(
            state.at[:, 1], near[step].at[pl.ds((chip * pair + core) * count, count)], local.at[2]
        )
        keep_re = pltpu.make_async_copy(
            state.at[:, 0], line[step].at[pl.ds((core * depth + level) * count, count)], local.at[3]
        )
        keep_im.start()
        keep_re.start()
        if step == 0:
            greet_levels(hello)
            load_u.wait()
            prepare()
            fetch.wait()
            for sub in range(subs):
                turn_saved(sub)
            note_own()
            take_ladders()
            tabulate(True)
        else:
            for sub in range(subs):
                project(step - 1, sub)
        if depth > 1:
            take_line(step, 1, 0)
        take_first(step)
        if step == 0:
            tabulate(False)
            pl.semaphore_wait(hello, depth - 1)
            greet_mates(again)
        else:
            for half in range(halves):
                stage((step - 1) * halves + half)
        for k in range(1, pieces):
            if depth > 1:
                take_line(step, 1, k)
        take_second(step)
        keep_im.wait()
        keep_re.wait()
        take_far(step)
        reduce_start(step, 0, 1)
        if depth > 2:
            for k in range(pieces):
                take_line(step, 2, k, True)
        reduce_start(step, 1, depth)
        reduce_on(step, depth - 2)
        if depth > 2:
            for k in range(pieces):
                take_line(step, 2, k, False)
        for hop in range(3, depth):
            for k in range(pieces):
                take_line(step, hop, k)
        mates_line(step)
        exchange(step)
        for ahead in range(depth - 3, 0, -1):
            reduce_on(step, ahead)
        exchange_on(step)
        if depth != 2:
            reduce_on(step, 0)
        exchange_end(step)
        if step == 1:
            pl.semaphore_wait(again, pair - 1)
        if step > 0:
            for half in range(halves):
                spread((step - 1) * halves + half)
        if step == 0:
            load.wait()
        join(step, held if step == 0 else state)
        for half in range(halves):
            rotate(step, half)
            if step == steps - 1:
                for sub in range(half * batch, (half + 1) * batch):
                    project(step, sub)
                    if sub == subs - 1:
                        result = pltpu.make_async_copy(hist.at[step, subs], out, local.at[1])
                        result.start()

        for hop in range(1, depth):
            for k in range(pieces):
                for way in range(2):

                    @pl.when(goes_on(way, hop))
                    def _(way=way, hop=hop, k=k):
                        a_level = level - (hop - 1) if way == 0 else level + (hop - 1)
                        block = line_block(step, core, a_level, k)
                        line_copy(step, way, hop, k, block).wait_send()

        def done_near(up, right, step=step):
            for k in range(pieces):
                block = near_block(step, chip, core, k)
                near_copy(step, up, right, k, block, chip, chip).wait_send()

        def done_chip(at, step=step):
            up, right = split(at, width)
            done_near(up, right)

            @pl.when(right > 0)
            def _():
                row_copy(step, up, right).wait_send()

            @pl.when(up > 0)
            def _():
                col_copy(step, up, right).wait_send()

        each(1, chips, done_chip)
        each(1, tall, lambda up: col_final(step, up).wait_send())
        each(1, width, lambda right: row_final(step, right).wait_send())
        for turn in range(1, pair):

            def sent_near(a_chip, step=step, turn=turn):
                for k in range(pieces):
                    block = near_block(step, a_chip, core, k)
                    near_mate(step, a_chip, turn, k, block).wait_send()

            def sent_line(a_level, step=step, turn=turn):
                for k in range(pieces):
                    block = line_block(step, core, a_level, k)
                    line_mate(step, a_level, turn, k, block).wait_send()

            each(0, chips, sent_near)
            each(0, depth, sent_line)

        def done_z(a_level, carry, step=step):
            @pl.when(a_level != level)
            def _():
                for k in range(pieces):
                    z_copy(step, 0, a_level, k).wait_send()

            return carry

        lax.fori_loop(0, depth, done_z, 0)

    each_ladder(lambda copy: copy.wait_send())
    result.wait()
    for group in range(steps * halves):
        finish(group)


def body(adjoint, saved, propagators, coupling, higher, lower, ladder, rates, decay):
    nodes = lax.axis_size("node")
    cores = lax.axis_size("cores")
    owners = nodes * cores
    count = adjoint.shape[0]
    modes = higher.shape[1]
    steps, subs = propagators.shape[:2]
    dim = coupling.shape[0]
    depth = 1 << (cores.bit_length() // 2)
    width = cores // depth
    pair = 2 if nodes % 2 == 0 else 1
    chips = nodes // pair * width
    pieces = 2
    rows = dim // owners
    halves = 2 if subs % 2 == 0 else 1
    batch = subs // halves
    higher, lower, ladder = higher.T, lower.T, jnp.swapaxes(ladder, 1, 2)
    smem = pl.BlockSpec(memory_space=pltpu.SMEM)
    vmem = pl.BlockSpec(memory_space=pltpu.VMEM)
    block = adjoint.shape
    hbm = pl.BlockSpec(memory_space=pl.ANY)
    hops = max(depth - 1, 1)
    others = max(chips - 1, 1)
    mates = max(pair - 1, 1)
    half = (count,) + block[2:]
    bit = (count // pieces,) + block[2:]
    tall = nodes // pair
    table = (depth + chips) * count * 2 * modes
    dma = pltpu.SemaphoreType.DMA
    state, grad = pl.pallas_call(
        functools.partial(kernel, (nodes, depth, width, pair, count, modes, steps, subs, dim, halves, pieces)),
        out_shape=(
            jax.ShapeDtypeStruct(block, BF16),
            jax.ShapeDtypeStruct((rows, steps * subs, 2, dim), F32),
        ),
        in_specs=[smem] * 5 + [hbm, hbm, hbm, vmem],
        out_specs=(hbm, vmem),
        scratch_shapes=[
            pltpu.VMEM((steps * subs, 2 * dim, 2 * dim), BF16),
            pltpu.VMEM((steps * subs, 2 * dim, 2 * dim), BF16),
            pltpu.VMEM((steps, subs + 1) + block, BF16),
            pltpu.VMEM((steps, depth) + half, BF16),
            pltpu.VMEM((steps, 2, depth) + half, BF16),
            pltpu.VMEM((steps, chips) + half, BF16),
            pltpu.VMEM((steps, max(width - 1, 1), tall) + bit, BF16),
            pltpu.VMEM((steps, max(tall - 1, 1), width) + bit, BF16),
            pltpu.VMEM((steps, max(width - 1, 1)) + bit, BF16),
            pltpu.VMEM((steps, max(tall - 1, 1)) + bit, BF16),
            pltpu.VMEM((steps * subs, dim, 2 * dim), F32),
            pltpu.VMEM((steps * halves, owners, batch * rows, 2 * dim), BF16),
            pltpu.VMEM((steps * halves, owners - 1, batch * rows, 2 * dim), BF16),
            pltpu.VMEM(saved.shape, BF16),
            pltpu.VMEM((subs, dim, count * 2 * dim), BF16),
            pltpu.SMEM((table,), jnp.int32),
            pltpu.SMEM((table,), F32),
            pltpu.SMEM((2, owners), jnp.int32),
            pltpu.SMEM((2, owners), F32),
            pltpu.SMEM((depth + chips, 2, modes, count), jnp.int32),
            dma((steps, others, pieces)),
            dma((steps, others, pieces)),
            dma((steps, mates, chips, pieces)),
            dma((steps, mates, chips, pieces)),
            dma((steps, 2, hops, pieces)),
            dma((steps, 2, hops, pieces)),
            dma((steps, mates, depth, pieces)),
            dma((steps, mates, depth, pieces)),
            dma((steps, depth, pieces)),
            dma((steps, 2, depth, pieces)),
            dma((steps, max(width - 1, 1), tall)),
            dma((steps, max(width - 1, 1), tall)),
            dma((steps, max(tall - 1, 1), width)),
            dma((steps, max(tall - 1, 1), width)),
            dma((steps, max(width - 1, 1))),
            dma((steps, max(width - 1, 1))),
            dma((steps, max(tall - 1, 1))),
            dma((steps, max(tall - 1, 1))),
            dma((depth + chips,)),
            dma((depth + chips,)),
            dma((steps * halves,)),
            dma((steps * halves,)),
            pltpu.SemaphoreType.REGULAR,
            pltpu.SemaphoreType.REGULAR,
            dma((6,)),
            pltpu.VMEM(propagators.shape, BF16),
            pltpu.VMEM(block, BF16),
            *[pltpu.VMEM((chips * pair * count, dim, dim), BF16)] * steps,
            *[pltpu.VMEM((depth * pair * count, dim, dim), BF16)] * steps,
        ],
        compiler_params=pltpu.CompilerParams(
            collective_id=0, has_side_effects=True, vmem_limit_bytes=63_000_000
        ),
    )(higher, lower, ladder, rates, decay, adjoint, saved, propagators, coupling)
    return state, grad


def solution(mesh):
    return jax.shard_map(
        body,
        mesh=mesh,
        in_specs=(
            P(("node", "cores"), None, None, None),
            P(None, None, ("node", "cores"), None, None, None),
            P(),
            P(),
            P(),
            P(),
            P(None, ("node", "cores"), None),
            P(),
            P(("node", "cores")),
        ),
        out_specs=(P(("node", "cores"), None, None, None), P(("node", "cores"), None, None, None)),
        check_vma=False,
    )
```

```python
import functools

import jax
import jax.numpy as jnp
from jax import lax
from jax.experimental import pallas as pl
from jax.experimental.pallas import tpu as pltpu
from jax.sharding import PartitionSpec as P

MESH = pl.DeviceIdType.MESH
F32 = jnp.float32
BF16 = jnp.bfloat16


def dot(a, b):
    return jnp.dot(a, b, preferred_element_type=F32)


def kernel(
    dims,
    higher_in,
    lower_in,
    ladder_in,
    rates_in,
    decay_in,
    adjoint,
    saved_in,
    propagators_in,
    coupling_in,
    out,
    grad,
    right_u,
    left_u,
    hist,
    zout,
    zin,
    rout,
    row_in,
    col_in,
    row_end,
    col_end,
    terms,
    term_stage,
    term_inbox,
    saved,
    saved_t,
    place,
    weight,
    home,
    inside,
    ladders,
    near_send,
    near_recv,
    near_pass,
    near_take,
    line_send,
    line_recv,
    line_pass,
    line_take,
    z_send,
    z_recv,
    r_send,
    row_recv,
    col_recv,
    row_done,
    col_done,
    ladder_send,
    ladder_recv,
    term_send,
    term_recv,
    hello,
    again,
    local,
    propagators,
    held,
    coupling,
    higher,
    lower,
    ladder,
    rates,
    decay,
    table_sem,
    early,
    early_core,
    early_row,
    early_col,
    early_z,
    early_sent,
    early_got,
    early_z_got,
    *gathered,
):
    nodes, depth, width, pair, count, modes, steps, subs, dim, halves, pieces = dims
    near, line = gathered[:steps], gathered[steps:]
    cores = depth * width
    owners = nodes * cores
    tall = nodes // pair
    chips = tall * width
    rows = dim // owners
    batch = subs // halves
    piece = count // pieces
    slots = 2 * modes
    node = lax.axis_index("node")
    spot = lax.axis_index("cores")
    level = spot // width
    column = spot % width
    side = node // pair
    core = node % pair
    chip = side * width + column

    def split(value, size):
        if size & (size - 1) == 0:
            return value >> (size.bit_length() - 1), value & (size - 1)
        return lax.div(value, size), lax.rem(value, size)

    def chip_id(other):
        return ((other // width) * pair + core, level * width + other % width)

    def chip_at(up, right):
        return lax.rem(side + up + tall, tall) * width + lax.rem(column + right + width, width)

    def mate_id(turn):
        return (side * pair + lax.rem(core + turn, pair), spot)

    def level_id(other):
        return (node, other * width + column)

    barrier = pltpu.get_barrier_semaphore()

    own = node * cores + spot

    def owner_id(offset):
        return split(split(own + offset, owners)[1], cores)

    def each(lo, hi, act):
        def one(i, carry):
            act(i)
            return carry

        lax.fori_loop(lo, hi, one, 0)

    def signal(semaphore, device):
        pl.semaphore_signal(semaphore, inc=1, device_id=device, device_id_type=MESH)

    def greet_levels(semaphore):
        def greet(other):
            pl.when(other != level)(lambda: signal(semaphore, level_id(other)))

        each(0, depth, greet)

    def greet_mates(semaphore):
        for turn in range(1, pair):
            signal(semaphore, mate_id(turn))

    def greet_chips(semaphore):
        def greet(other):
            pl.when(other != chip)(lambda: signal(semaphore, chip_id(other)))

        each(0, chips, greet)

    greet_levels(barrier)
    greet_chips(barrier)
    greet_mates(barrier)
    tables = [
        pltpu.make_async_copy(source, target, table_sem.at[at])
        for at, (source, target) in enumerate(
            (
                (ladder_in, ladder),
                (higher_in, higher),
                (lower_in, lower),
                (rates_in, rates),
                (decay_in, decay),
                (coupling_in, coupling),
            )
        )
    ]
    for copy in tables:
        copy.start()
    load_u = pltpu.make_async_copy(propagators_in, propagators, local.at[4])
    load_u.start()
    load = pltpu.make_async_copy(adjoint, held, local.at[5])
    load.start()
    fetch = pltpu.make_async_copy(saved_in, saved, local.at[0])
    fetch.start()

    def remote(source, target, sent, arrived, device):
        return pltpu.make_async_remote_copy(
            src_ref=source,
            dst_ref=target,
            send_sem=sent,
            recv_sem=arrived,
            device_id=device,
            device_id_type=MESH,
        )

    def part(k):
        return pl.ds(k * piece, piece)

    def near_block(step, a_chip, a_core, k):
        return near[step].at[pl.ds((a_chip * pair + a_core) * count + k * piece, piece)]

    def line_block(step, a_core, a_level, k):
        return line[step].at[pl.ds((a_core * depth + a_level) * count + k * piece, piece)]

    def near_copy(step, up, right, k, source, a_chip, target):
        at = up * width + right - 1
        return remote(
            source,
            near_block(step, a_chip, core, k),
            near_send.at[step],
            near_recv.at[step, at, k],
            chip_id(target),
        )

    def near_got(step, up, right, k):
        a_chip = chip_at(-up, -right)
        block = near_block(step, a_chip, core, k)
        near_copy(step, up, right, k, block, a_chip, a_chip).wait_recv()
        for turn in range(1, pair):
            near_mate(step, a_chip, turn, k, block).start()
        return block, a_chip

    def near_mate(step, a_chip, turn, k, source):
        return remote(
            source,
            near_block(step, a_chip, core, k),
            near_pass.at[step],
            near_take.at[step],
            mate_id(turn),
        )

    def line_copy(step, way, hop, k, source):
        a_level = level - (hop - 1) if way == 0 else level + (hop - 1)
        return remote(
            source,
            line_block(step, core, a_level, k),
            line_send.at[step],
            line_recv.at[step, way, hop - 1, k],
            level_id(level + 1 if way == 0 else level - 1),
        )

    def line_mate(step, a_level, turn, k, source):
        return remote(
            source,
            line_block(step, core, a_level, k),
            line_pass.at[step],
            line_take.at[step],
            mate_id(turn),
        )

    def z_copy(step, way, a_level, k):
        return remote(
            zout.at[step, a_level, pl.ds(k * piece, piece)],
            zin.at[step, way, a_level, pl.ds(k * piece, piece)],
            z_send.at[step],
            z_recv.at[step, way, a_level, k],
            level_id(level + 1 if way == 0 else level - 1),
        )

    def row_copy(step, up, right):
        return remote(
            rout.at[step, chip_at(up, right), part(0)],
            row_in.at[step, right - 1, up],
            r_send.at[step],
            row_recv.at[step, right - 1, up],
            chip_id(chip_at(0, right)),
        )

    def col_copy(step, up, right):
        return remote(
            rout.at[step, chip_at(up, right), part(1)],
            col_in.at[step, up - 1, right],
            r_send.at[step],
            col_recv.at[step, up - 1, right],
            chip_id(chip_at(up, 0)),
        )

    def col_final(step, up):
        return remote(
            rout.at[step, chip_at(up, 0), part(0)],
            col_end.at[step, up - 1],
            r_send.at[step],
            col_done.at[step, up - 1],
            chip_id(chip_at(up, 0)),
        )

    def row_final(step, right):
        return remote(
            rout.at[step, chip_at(0, right), part(1)],
            row_end.at[step, right - 1],
            r_send.at[step],
            row_done.at[step, right - 1],
            chip_id(chip_at(0, right)),
        )

    def ladder_level(other):
        return remote(
            ladder, ladders.at[level], ladder_send, ladder_recv, level_id(other)
        )

    def ladder_chip(other):
        return remote(
            ladder,
            ladders.at[depth + chip],
            ladder_send,
            ladder_recv,
            chip_id(other),
        )

    def each_ladder(act):
        def one_level(other, carry):
            @pl.when(other != level)
            def _():
                act(ladder_level(other))

            return carry

        def one_chip(other, carry):
            @pl.when(other != chip)
            def _():
                act(ladder_chip(other))

            return carry

        lax.fori_loop(0, depth, one_level, 0)
        lax.fori_loop(0, chips, one_chip, 0)

    def passed_ladders(semaphore):
        if depth + chips > 2:
            passed = ladders.at[pl.ds(0, depth + chips - 2)]
            pltpu.make_async_copy(passed, passed, semaphore).wait()

    def note_own():
        for way in range(2):
            for mode in range(modes):
                for j in range(count):
                    value = ladder[way, mode, j]
                    ladders[level, way, mode, j] = value
                    ladders[depth + chip, way, mode, j] = value

        def locate(owner, carry):
            a_node, a_spot = split(owner, cores)
            a_level, a_column = split(a_spot, width)
            a_side, a_core = split(a_node, pair)
            home[0, owner] = ((a_side * width + a_column) * pair + a_core) * count
            home[1, owner] = (a_core * depth + a_level) * count
            inside[0, owner] = jnp.where(a_level == level, 1.0, 0.0)
            beside = jnp.logical_and(a_side == side, a_column == column)
            inside[1, owner] = jnp.where(beside, 1.0, 0.0)
            return carry

        lax.fori_loop(0, owners, locate, 0)

    def tabulate(along_z):
        def entry(at):
            index, j = split(at, count)
            if along_z:
                target, kind, row = node * cores + index * width + column, 0, index
            else:
                a_side, a_column = split(index, width)
                target = (a_side * pair + core) * cores + level * width + a_column
                kind, row = 1, depth + index
            for way in range(2):
                for mode in range(modes):
                    source, member = split((higher, lower)[way][mode, target * count + j], count)
                    value = ladders[row, way, mode, j].astype(F32) * rates[way, mode]
                    slot = (row * count + j) * slots + way * modes + mode
                    place[slot] = home[kind, source] + member
                    weight[slot] = inside[kind, source] * value

        each(0, (depth if along_z else chips) * count, entry)

    def partial(blocks, row, k, put):
        operator = coupling[...]

        def some(pick, carry):
            plus, minus = [], []
            for i in range(2):
                sums = []
                for way in range(2):
                    total = None
                    for mode in range(modes):
                        at = (row * count + pick * 2 + i) * slots + way * modes + mode
                        scale = jnp.full((16, dim), weight[at], F32).astype(BF16)
                        term = blocks[place[at]].reshape(dim // 16, 16, dim) * scale
                        total = term if total is None else total + term
                    sums.append(total.reshape(dim, dim))
                plus.append(sums[0] + sums[1])
                minus.append(sums[0] - sums[1])
            left = dot(operator, jnp.concatenate(plus, axis=1))
            right = dot(jnp.concatenate(minus, axis=0), operator)
            for i in range(2):
                value = left[:, i * dim : (i + 1) * dim] - right[i * dim : (i + 1) * dim]
                put(pick * 2 + i, value.astype(BF16))
            return carry

        lax.fori_loop(k * piece // 2, (k + 1) * piece // 2, some, 0)

    def prepare():
        def one(at, carry):
            step, sub = at // subs, at % subs
            u_re = propagators[step, sub, 0]
            u_im = propagators[step, sub, 1]
            right_u[at, :dim, :dim] = u_re
            right_u[at, :dim, dim:] = u_im
            right_u[at, dim:, :dim] = -u_im
            right_u[at, dim:, dim:] = u_re
            t_re = u_re.T
            t_im = u_im.T
            left_u[at, :dim, :dim] = t_re
            left_u[at, :dim, dim:] = t_im
            left_u[at, dim:, :dim] = -t_im
            left_u[at, dim:, dim:] = t_re
            return carry

        lax.fori_loop(0, steps * subs, one, 0)

    def turn_saved(step, sub):
        for j in range(0, count, 2):
            for i in range(2):
                for part in range(2):
                    saved_t[step, sub, j // 2, part * dim : (part + 1) * dim, i * dim : (i + 1) * dim] = (
                        saved[step, sub, j + i, part].T
                    )

    def beside(step, sub, j):
        return jnp.concatenate(
            [
                jnp.concatenate([hist[step, sub, j + i, 0], hist[step, sub, j + i, 1]], axis=1)
                for i in range(2)
            ],
            axis=0,
        )

    def project(step, sub):
        total = jnp.zeros((2 * dim, 2 * dim), F32)
        for j in range(0, count, 2):
            total = total + dot(saved_t[step, sub, j // 2], beside(step, sub + 1, j))
        at = step * subs + sub
        terms[at, :, :dim] = total[:dim, :dim] + total[dim:, dim:]
        terms[at, :, dim:] = total[:dim, dim:] - total[dim:, :dim]
        if step == steps - 1 and sub % batch == batch - 1:
            stage(sub // batch)
            spread(sub // batch)

    def stage(group):
        for target in range(owners):
            term_stage[group, target] = jnp.concatenate(
                [
                    terms[(steps - 1) * subs + group * batch + i, target * rows : (target + 1) * rows]
                    for i in range(batch)
                ],
                axis=0,
            ).astype(BF16)

    def spread(group):
        def send(offset, carry):
            pltpu.make_async_remote_copy(
                src_ref=term_stage.at[group, lax.rem(own + offset, owners)],
                dst_ref=term_inbox.at[group, offset - 1],
                send_sem=term_send.at[group],
                recv_sem=term_recv.at[group],
                device_id=owner_id(offset),
                device_id_type=MESH,
            ).start()
            return carry

        lax.fori_loop(1, owners, send, 0)

    def finish(group):
        everything = term_inbox.at[group]
        pltpu.make_async_copy(everything, everything, term_recv.at[group]).wait()
        total = term_stage[group, own].astype(F32)
        for offset in range(1, owners):
            total = total + term_inbox[group, offset - 1].astype(F32)
        for i in range(batch):
            for row in range(rows):
                for part in range(2):
                    grad[row, (steps - 1) * subs + group * batch + i, part : part + 1, :] = total[
                        i * rows + row : i * rows + row + 1, part * dim : (part + 1) * dim
                    ]
        pltpu.make_async_copy(everything, everything, term_send.at[group]).wait()

    def rotate_one(step, sub):
        at = step * subs + sub
        mult_l = left_u[at]
        rows = jnp.concatenate([beside(step, sub, j) for j in range(0, count, 2)], axis=0)
        middles = dot(rows, right_u[at]).astype(BF16)
        for j in range(0, count, 2):
            middle = middles[j * dim : (j + 2) * dim]
            stacked = jnp.concatenate(
                [
                    jnp.concatenate([middle[:dim, :dim], middle[dim:, :dim]], axis=1),
                    jnp.concatenate([middle[:dim, dim:], middle[dim:, dim:]], axis=1),
                ],
                axis=0,
            )
            result = dot(mult_l, stacked).astype(BF16)
            for i in range(2):
                for part in range(2):
                    hist[step, sub + 1, j + i, part] = result[
                        part * dim : (part + 1) * dim, i * dim : (i + 1) * dim
                    ]

    def rotate(step):
        each(0, subs, lambda sub: rotate_one(step, sub))

    def add_to(target, sources):
        total = target[...].astype(F32)
        for source in sources:
            total = total + source[...].astype(F32)
        target[...] = total.astype(BF16)

    def early_copy(step, kind, at, source, target, device):
        return remote(
            source, target, early_sent.at[step, kind], early_got.at[step, kind, at], device
        )

    def early_mate(step, turn):
        return early_copy(
            step,
            0,
            turn - 1,
            early.at[step, lax.rem(core + turn, pair)],
            early_core.at[step],
            mate_id(turn),
        )

    def early_along(step, right):
        a_column = lax.rem(column + right, width)
        return early_copy(
            step,
            1,
            right - 1,
            early.at[step, core, a_column],
            early_row.at[step, right - 1],
            chip_id(chip_at(0, right)),
        )

    def early_across(step, up):
        a_side = lax.rem(side + up, tall)
        return early_copy(
            step,
            2,
            up - 1,
            early.at[step, core, column, a_side],
            early_col.at[step, up - 1],
            chip_id(chip_at(up, 0)),
        )

    def early_level(step, other, sender):
        return remote(
            early.at[step, core, column, side, other],
            early_z.at[step, sender],
            early_sent.at[step, 3],
            early_z_got.at[step],
            level_id(other),
        )

    def early_start(step):
        for target in range(owners):
            a_node, a_spot = target // cores, target % cores
            early[step, a_node % pair, a_spot % width, a_node // pair, a_spot // width] = (
                jnp.concatenate(
                    [
                        terms[step * subs + sub, target * rows : (target + 1) * rows]
                        for sub in range(subs)
                    ],
                    axis=0,
                ).astype(BF16)
            )
        for turn in range(1, pair):
            early_mate(step, turn).start()

    def early_rows(step):
        for turn in range(1, pair):
            early_mate(step, turn).wait_recv()
            add_to(early.at[step, core], [early_core.at[step]])
        for right in range(1, width):
            early_along(step, right).start()

    def early_cols(step):
        for right in range(1, width):
            early_along(step, right).wait_recv()
        add_to(
            early.at[step, core, column],
            [early_row.at[step, right - 1] for right in range(1, width)],
        )
        for up in range(1, tall):
            early_across(step, up).start()

    def early_levels(step):
        for up in range(1, tall):
            early_across(step, up).wait_recv()
        add_to(
            early.at[step, core, column, side],
            [early_col.at[step, up - 1] for up in range(1, tall)],
        )

        def send(other):
            pl.when(other != level)(lambda: early_level(step, other, level).start())

        each(0, depth, send)

    def early_finish(step):
        early_z[step, level] = early[step, core, column, side, level]

        if depth > 1:
            passed = early_z.at[step, pl.ds(0, depth - 1)]
            pltpu.make_async_copy(passed, passed, early_z_got.at[step]).wait()
        total = early_z[step, 0].astype(F32)
        for other in range(1, depth):
            total = total + early_z[step, other].astype(F32)
        for sub in range(subs):
            for row in range(rows):
                at = sub * rows + row
                for part in range(2):
                    grad[row, step * subs + sub, part : part + 1, :] = total[
                        at : at + 1, part * dim : (part + 1) * dim
                    ]
        if pair > 1:
            pltpu.make_async_copy(
                early_core.at[step], early_core.at[step], early_sent.at[step, 0]
            ).wait()
        if width > 1:
            pltpu.make_async_copy(
                early_row.at[step], early_row.at[step], early_sent.at[step, 1]
            ).wait()
        if tall > 1:
            pltpu.make_async_copy(
                early_col.at[step], early_col.at[step], early_sent.at[step, 2]
            ).wait()
        if depth > 1:
            passed = early_z.at[step, pl.ds(0, depth - 1)]
            pltpu.make_async_copy(passed, passed, early_sent.at[step, 3]).wait()

    def join(step, state):
        def one(j, carry):
            lam = decay[j] * state[j, 0].astype(F32) + zout[step, level, j].astype(F32)
            hist[step, 0, j, 0] = lam.astype(BF16)
            total = rout[step, chip, j].astype(F32)
            lam = decay[j] * state[j, 1].astype(F32) - total
            hist[step, 0, j, 1] = lam.astype(BF16)
            return carry

        lax.fori_loop(0, count, one, 0)

    def fold(target, sources):
        for j in range(piece):
            total = target[j].astype(F32)
            for source in sources:
                total = total + source[j].astype(F32)
            target[j] = total.astype(BF16)

    def arrives(way, hop):
        return level >= hop if way == 0 else level + hop < depth

    def goes_on(way, hop):
        if way == 0:
            return jnp.logical_and(level >= hop - 1, level < depth - 1)
        return jnp.logical_and(level + hop - 1 < depth, level > 0)

    def take_line(step, hop, k, chosen=None):
        for way in range(2):
            due = arrives(way, hop)
            if chosen is not None:
                onward = goes_on(way, hop + 1)
                due = jnp.logical_and(due, onward if chosen else jnp.logical_not(onward))

            @pl.when(due)
            def _(way=way):
                a_level = level - hop if way == 0 else level + hop
                block = line_block(step, core, a_level, k)
                remote(
                    block,
                    block,
                    line_send.at[step],
                    line_recv.at[step, way, hop - 1, k],
                    level_id(level),
                ).wait_recv()
                if hop + 1 < depth:

                    @pl.when(goes_on(way, hop + 1))
                    def _():
                        line_copy(step, way, hop + 1, k, block).start()

                for turn in range(1, pair):
                    line_mate(step, a_level, turn, k, block).start()

    def take_first(step):
        def along(right):
            block, a_chip = near_got(step, 0, right, 0)
            each(
                1,
                tall,
                lambda up: near_copy(
                    step, up, right, 0, block, a_chip, chip_at(up, 0)
                ).start(),
            )

        def across(up):
            block, a_chip = near_got(step, up, 0, 1)
            each(
                1,
                width,
                lambda right: near_copy(
                    step, up, right, 1, block, a_chip, chip_at(0, right)
                ).start(),
            )

        each(1, width, along)
        each(1, tall, across)

    def take_second(step):
        each(1, width, lambda right: near_got(step, 0, right, 1) and None)
        each(1, tall, lambda up: near_got(step, up, 0, 0) and None)

    def take_far(step):
        def one(up):
            def two(right):
                for k in range(pieces):
                    near_got(step, up, right, k)

            each(1, width, two)

        each(1, tall, one)
        for turn in range(1, pair):

            passed = near[step].at[pl.ds(0, chips * count)]
            pltpu.make_async_copy(passed, passed, near_take.at[step]).wait()

    def mates_line(step):
        for turn in range(1, pair):

            passed = line[step].at[pl.ds(0, depth * count)]
            pltpu.make_async_copy(passed, passed, line_take.at[step]).wait()

    def reduce_start(step, lo, hi):
        def one(i, carry):
            a_level = jnp.where(level * 2 < depth, depth - 1 - i, i)

            def put(j, value):
                zout[step, a_level, j] = value

            for k in range(pieces):
                partial(near[step], a_level, k, put)

                @pl.when(jnp.logical_and(level == 0, a_level > 0))
                def _(k=k):
                    z_copy(step, 0, a_level, k).start()

                @pl.when(jnp.logical_and(level == depth - 1, a_level < depth - 1))
                def _(k=k):
                    z_copy(step, 1, a_level, k).start()

            return carry

        lax.fori_loop(lo, hi, one, 0)

    def exchange(step):
        def one(i):
            up, right = split(chips - 1 - i, width)
            target = chip_at(up, right)

            def put(j, value):
                rout[step, target, j] = value

            partial(line[step], depth + target, 0, put)

            @pl.when(right > 0)
            def _():
                row_copy(step, up, right).start()

            for k in range(1, pieces):
                partial(line[step], depth + target, k, put)

            @pl.when(up > 0)
            def _():
                col_copy(step, up, right).start()

        each(0, chips, one)

    def exchange_on(step):
        def column(up):
            target = chip_at(up, 0)
            each(1, width, lambda right: row_copy(step, up, right).wait_recv())
            fold(
                rout.at[step, target, part(0)],
                [row_in.at[step, right - 1, up] for right in range(1, width)],
            )
            col_final(step, up).start()

        def line_of(right):
            target = chip_at(0, right)
            each(1, tall, lambda up: col_copy(step, up, right).wait_recv())
            fold(
                rout.at[step, target, part(1)],
                [col_in.at[step, up - 1, right] for up in range(1, tall)],
            )
            row_final(step, right).start()

        each(1, tall, column)
        each(1, width, line_of)

    def exchange_end(step):
        each(1, width, lambda right: row_copy(step, 0, right).wait_recv())
        each(1, tall, lambda up: col_copy(step, up, 0).wait_recv())
        each(1, tall, lambda up: col_final(step, up).wait_recv())
        each(1, width, lambda right: row_final(step, right).wait_recv())
        fold(
            rout.at[step, chip, part(0)],
            [row_in.at[step, right - 1, 0] for right in range(1, width)]
            + [col_end.at[step, up - 1] for up in range(1, tall)],
        )
        fold(
            rout.at[step, chip, part(1)],
            [col_in.at[step, up - 1, 0] for up in range(1, tall)]
            + [row_end.at[step, right - 1] for right in range(1, width)],
        )

    def reduce_on(step, ahead):
        for k in range(pieces):
            for way in range(2):
                if way == 0:
                    a_level = level + ahead
                    fits = jnp.logical_and(level > 0, a_level < depth)
                else:
                    a_level = level - ahead
                    fits = jnp.logical_and(level < depth - 1, a_level >= 0)

                @pl.when(fits)
                def _(way=way, k=k, a_level=a_level):
                    z_copy(step, way, a_level, k).wait_recv()
                    fold(
                        zout.at[step, a_level, part(k)], [zin.at[step, way, a_level, part(k)]]
                    )
                    if ahead > 0:
                        z_copy(step, way, a_level, k).start()

    pl.semaphore_wait(barrier, depth + chips + pair - 3)
    tables[0].wait()
    each_ladder(lambda copy: copy.start())
    for step in range(steps):
        state = adjoint if step == 0 else hist.at[step - 1, subs]
        for k in range(pieces):
            for way in range(2):

                @pl.when(goes_on(way, 1))
                def _(way=way, k=k):
                    line_copy(step, way, 1, k, state.at[part(k), 0]).start()

        def first(right, k, step=step, state=state):
            near_copy(step, 0, right, k, state.at[part(k), 1], chip, chip_at(0, right)).start()

        def other(up, k, step=step, state=state):
            near_copy(step, up, 0, k, state.at[part(k), 1], chip, chip_at(up, 0)).start()

        each(1, width, lambda right: first(right, 0))
        each(1, tall, lambda up: other(up, 1))
        each(1, width, lambda right: first(right, 1))
        each(1, tall, lambda up: other(up, 0))
        for k in range(pieces):
            for turn in range(1, pair):
                near_mate(step, chip, turn, k, state.at[part(k), 1]).start()
                line_mate(step, level, turn, k, state.at[part(k), 0]).start()
        keep_im = pltpu.make_async_copy(
            state.at[:, 1], near[step].at[pl.ds((chip * pair + core) * count, count)], local.at[2]
        )
        keep_re = pltpu.make_async_copy(
            state.at[:, 0], line[step].at[pl.ds((core * depth + level) * count, count)], local.at[3]
        )
        keep_im.start()
        keep_re.start()
        if step == 0:
            greet_levels(hello)
            load_u.wait()
            prepare()
            for copy in tables[1:]:
                copy.wait()
            fetch.wait()
            for sub in range(subs):
                for a_step in range(steps):
                    turn_saved(a_step, sub)
            note_own()
            passed_ladders(ladder_recv)
            tabulate(True)
        else:
            for sub in range(subs):
                project(step - 1, sub)
        if depth > 1:
            take_line(step, 1, 0)
        take_first(step)
        if step == 0:
            tabulate(False)
            pl.semaphore_wait(hello, depth - 1)
            greet_mates(again)
        else:
            early_start(step - 1)
        for k in range(1, pieces):
            if depth > 1:
                take_line(step, 1, k)
        take_second(step)
        if step > 0:
            early_rows(step - 1)
        keep_im.wait()
        keep_re.wait()
        take_far(step)
        reduce_start(step, 0, 1)
        if depth > 2:
            for k in range(pieces):
                take_line(step, 2, k, True)
        reduce_start(step, 1, depth)
        if step > 0:
            early_cols(step - 1)
        reduce_on(step, depth - 2)
        if depth > 2:
            for k in range(pieces):
                take_line(step, 2, k, False)
        for hop in range(3, depth):
            for k in range(pieces):
                take_line(step, hop, k)
        mates_line(step)
        exchange(step)
        if step > 0:
            early_levels(step - 1)
        for ahead in range(depth - 3, 0, -1):
            reduce_on(step, ahead)
        exchange_on(step)
        if depth != 2:
            reduce_on(step, 0)
        exchange_end(step)
        if step == steps - 1:
            pl.semaphore_wait(again, pair - 1)
        if step == 0:
            load.wait()
        join(step, held if step == 0 else state)
        if step < steps - 1:
            rotate(step)
        else:
            for half in range(halves):
                each(half * batch, (half + 1) * batch, lambda sub: rotate_one(step, sub))
                for sub in range(half * batch, (half + 1) * batch):
                    if sub == subs - 1:
                        result = pltpu.make_async_copy(hist.at[step, subs], out, local.at[1])
                        result.start()
                    project(step, sub)

    def sent(source, amount, semaphore):
        if amount > 0:
            passed = source.at[pl.ds(0, amount)]
            pltpu.make_async_copy(passed, passed, semaphore).wait()

    for step in range(steps):
        sent(near[step], (chips - 1) * count, near_send.at[step])
        sent(near[step], (pair - 1) * chips * count, near_pass.at[step])
        sent(line[step], (pair - 1) * depth * count, line_pass.at[step])
        crossings = (width - 1) * (tall + 1) + (tall - 1) * (width + 1)
        sent(near[step], crossings * piece, r_send.at[step])
        sent(zout.at[step], depth - 1, z_send.at[step])
        for a_level in range(depth):
            ups = a_level + 1 if a_level < depth - 1 else 0
            downs = depth - a_level if a_level > 0 else 0

            @pl.when(level == a_level)
            def _(step=step, blocks=ups + downs):
                sent(line[step], blocks * count, line_send.at[step])

    passed_ladders(ladder_send)
    result.wait()
    for step in range(steps - 1):
        early_finish(step)
    for half in range(halves):
        finish(half)


def deliver(state, grad, state_out, grad_out, state_kept, grad_kept, sems):
    into = [
        pltpu.make_async_copy(state, state_kept, sems.at[0]),
        pltpu.make_async_copy(grad, grad_kept, sems.at[1]),
    ]
    back = [
        pltpu.make_async_copy(state_kept, state_out, sems.at[2]),
        pltpu.make_async_copy(grad_kept, grad_out, sems.at[3]),
    ]
    for copy in into:
        copy.start()
    for arrival, leave in zip(into, back):
        arrival.wait()
        leave.start()
    for copy in back:
        copy.wait()


def body(adjoint, saved, propagators, coupling, higher, lower, ladder, rates, decay):
    nodes = lax.axis_size("node")
    cores = lax.axis_size("cores")
    owners = nodes * cores
    count = adjoint.shape[0]
    modes = higher.shape[1]
    steps, subs = propagators.shape[:2]
    dim = coupling.shape[0]
    depth = 1 << (cores.bit_length() // 2)
    width = cores // depth
    pair = 2 if nodes % 2 == 0 else 1
    chips = nodes // pair * width
    pieces = 2
    rows = dim // owners
    halves = 2 if subs % 2 == 0 else 1
    batch = subs // halves
    higher, lower, ladder = higher.T, lower.T, jnp.swapaxes(ladder, 1, 2)
    vmem = pl.BlockSpec(memory_space=pltpu.VMEM)
    block = adjoint.shape
    hbm = pl.BlockSpec(memory_space=pl.ANY)
    hops = max(depth - 1, 1)
    others = max(chips - 1, 1)
    mates = max(pair - 1, 1)
    half = (count,) + block[2:]
    bit = (count // pieces,) + block[2:]
    tall = nodes // pair
    before = max(steps - 1, 1)
    slab = (subs * rows, 2 * dim)
    table = (depth + chips) * count * 2 * modes
    dma = pltpu.SemaphoreType.DMA
    state, grad = pl.pallas_call(
        functools.partial(kernel, (nodes, depth, width, pair, count, modes, steps, subs, dim, halves, pieces)),
        out_shape=(
            jax.ShapeDtypeStruct(block, BF16),
            jax.ShapeDtypeStruct((rows, steps * subs, 2, dim), F32),
        ),
        in_specs=[hbm] * 9,
        out_specs=(hbm, vmem),
        scratch_shapes=[
            pltpu.VMEM((steps * subs, 2 * dim, 2 * dim), BF16),
            pltpu.VMEM((steps * subs, 2 * dim, 2 * dim), BF16),
            pltpu.VMEM((steps, subs + 1) + block, BF16),
            pltpu.VMEM((steps, depth) + half, BF16),
            pltpu.VMEM((steps, 2, depth) + half, BF16),
            pltpu.VMEM((steps, chips) + half, BF16),
            pltpu.VMEM((steps, max(width - 1, 1), tall) + bit, BF16),
            pltpu.VMEM((steps, max(tall - 1, 1), width) + bit, BF16),
            pltpu.VMEM((steps, max(width - 1, 1)) + bit, BF16),
            pltpu.VMEM((steps, max(tall - 1, 1)) + bit, BF16),
            pltpu.VMEM((steps * subs, dim, 2 * dim), F32),
            pltpu.VMEM((halves, owners, batch * rows, 2 * dim), BF16),
            pltpu.VMEM((halves, owners - 1, batch * rows, 2 * dim), BF16),
            pltpu.VMEM(saved.shape, BF16),
            pltpu.VMEM((steps, subs, count // 2, 2 * dim, 2 * dim), BF16),
            pltpu.SMEM((table,), jnp.int32),
            pltpu.SMEM((table,), F32),
            pltpu.SMEM((2, owners), jnp.int32),
            pltpu.SMEM((2, owners), F32),
            pltpu.SMEM((depth + chips, 2, modes, count), jnp.int32),
            dma((steps,)),
            dma((steps, others, pieces)),
            dma((steps,)),
            dma((steps,)),
            dma((steps,)),
            dma((steps, 2, hops, pieces)),
            dma((steps,)),
            dma((steps,)),
            dma((steps,)),
            dma((steps, 2, depth, pieces)),
            dma((steps,)),
            dma((steps, max(width - 1, 1), tall)),
            dma((steps, max(tall - 1, 1), width)),
            dma((steps, max(width - 1, 1))),
            dma((steps, max(tall - 1, 1))),
            dma(()),
            dma(()),
            dma((halves,)),
            dma((halves,)),
            pltpu.SemaphoreType.REGULAR,
            pltpu.SemaphoreType.REGULAR,
            dma((6,)),
            pltpu.VMEM(propagators.shape, BF16),
            pltpu.VMEM(block, BF16),
            pltpu.VMEM(coupling.shape, BF16),
            pltpu.SMEM(higher.shape, jnp.int32),
            pltpu.SMEM(lower.shape, jnp.int32),
            pltpu.SMEM(ladder.shape, jnp.int32),
            pltpu.SMEM(rates.shape, F32),
            pltpu.SMEM(decay.shape, F32),
            dma((6,)),
            pltpu.VMEM((before, pair, width, tall, depth) + slab, BF16),
            pltpu.VMEM((before, width, tall, depth) + slab, BF16),
            pltpu.VMEM((before, max(width - 1, 1), tall, depth) + slab, BF16),
            pltpu.VMEM((before, max(tall - 1, 1), depth) + slab, BF16),
            pltpu.VMEM((before, depth) + slab, BF16),
            dma((before, 4)),
            dma((before, 3, max(width - 1, tall - 1, 1))),
            dma((before,)),
            *[pltpu.VMEM((chips * pair * count, dim, dim), BF16)] * steps,
            *[pltpu.VMEM((depth * pair * count, dim, dim), BF16)] * steps,
        ],
        compiler_params=pltpu.CompilerParams(
            collective_id=0, has_side_effects=True, vmem_limit_bytes=63_000_000
        ),
    )(higher, lower, ladder, rates, decay, adjoint, saved, propagators, coupling)
    return pl.pallas_call(
        deliver,
        out_shape=(
            jax.ShapeDtypeStruct(state.shape, state.dtype),
            jax.ShapeDtypeStruct(grad.shape, grad.dtype),
        ),
        in_specs=[hbm, hbm],
        out_specs=(hbm, hbm),
        scratch_shapes=[
            pltpu.VMEM(state.shape, state.dtype),
            pltpu.VMEM(grad.shape, grad.dtype),
            dma((4,)),
        ],
    )(state, grad)


def solution(mesh):
    return jax.shard_map(
        body,
        mesh=mesh,
        in_specs=(
            P(("node", "cores"), None, None, None),
            P(None, None, ("node", "cores"), None, None, None),
            P(),
            P(),
            P(),
            P(),
            P(None, ("node", "cores"), None),
            P(),
            P(("node", "cores")),
        ),
        out_specs=(P(("node", "cores"), None, None, None), P(("node", "cores"), None, None, None)),
        check_vma=False,
    )
```

```python
import functools

import jax
import jax.numpy as jnp
from jax import lax
from jax.experimental import pallas as pl
from jax.experimental.pallas import tpu as pltpu
from jax.sharding import PartitionSpec as P

MESH = pl.DeviceIdType.MESH
F32 = jnp.float32
BF16 = jnp.bfloat16


def dot(a, b):
    return jnp.dot(a, b, preferred_element_type=F32)


def kernel(
    dims,
    higher_in,
    lower_in,
    ladder_in,
    rates_in,
    decay_in,
    adjoint,
    saved_in,
    propagators_in,
    coupling_in,
    out,
    grad,
    right_u,
    left_u,
    hist,
    zout,
    zin,
    rout,
    row_in,
    col_in,
    row_end,
    col_end,
    terms,
    term_stage,
    term_inbox,
    saved,
    saved_t,
    place,
    weight,
    home,
    inside,
    ladders,
    near_send,
    near_recv,
    near_pass,
    near_take,
    line_send,
    line_recv,
    line_pass,
    line_take,
    z_send,
    z_recv,
    r_send,
    row_recv,
    col_recv,
    row_done,
    col_done,
    ladder_send,
    ladder_recv,
    term_send,
    term_recv,
    hello,
    again,
    local,
    propagators,
    held,
    coupling,
    higher,
    lower,
    ladder,
    rates,
    decay,
    table_sem,
    early,
    early_core,
    early_row,
    early_col,
    early_z,
    early_sent,
    early_got,
    early_z_got,
    *gathered,
):
    nodes, depth, width, pair, count, modes, steps, subs, dim, halves, pieces = dims
    near, line = gathered[:steps], gathered[steps:]
    cores = depth * width
    owners = nodes * cores
    tall = nodes // pair
    chips = tall * width
    rows = dim // owners
    batch = subs // halves
    piece = count // pieces
    slots = 2 * modes
    node = lax.axis_index("node")
    spot = lax.axis_index("cores")
    level = spot // width
    column = spot % width
    side = node // pair
    core = node % pair
    chip = side * width + column

    def split(value, size):
        if size & (size - 1) == 0:
            return value >> (size.bit_length() - 1), value & (size - 1)
        return lax.div(value, size), lax.rem(value, size)

    def chip_id(other):
        return ((other // width) * pair + core, level * width + other % width)

    def chip_at(up, right):
        return lax.rem(side + up + tall, tall) * width + lax.rem(column + right + width, width)

    def mate_id(turn):
        return (side * pair + lax.rem(core + turn, pair), spot)

    def level_id(other):
        return (node, other * width + column)

    barrier = pltpu.get_barrier_semaphore()

    own = node * cores + spot

    def owner_id(offset):
        return split(split(own + offset, owners)[1], cores)

    def each(lo, hi, act):
        def one(i, carry):
            act(i)
            return carry

        lax.fori_loop(lo, hi, one, 0)

    def signal(semaphore, device):
        pl.semaphore_signal(semaphore, inc=1, device_id=device, device_id_type=MESH)

    def greet_levels(semaphore):
        def greet(other):
            pl.when(other != level)(lambda: signal(semaphore, level_id(other)))

        each(0, depth, greet)

    def greet_mates(semaphore):
        for turn in range(1, pair):
            signal(semaphore, mate_id(turn))

    def greet_chips(semaphore):
        def greet(other):
            pl.when(other != chip)(lambda: signal(semaphore, chip_id(other)))

        each(0, chips, greet)

    greet_levels(barrier)
    greet_chips(barrier)
    greet_mates(barrier)
    tables = [
        pltpu.make_async_copy(source, target, table_sem.at[at])
        for at, (source, target) in enumerate(
            (
                (ladder_in, ladder),
                (higher_in, higher),
                (lower_in, lower),
                (rates_in, rates),
                (decay_in, decay),
                (coupling_in, coupling),
            )
        )
    ]
    for copy in tables:
        copy.start()
    load_u = pltpu.make_async_copy(propagators_in, propagators, local.at[4])
    load_u.start()
    load = pltpu.make_async_copy(adjoint, held, local.at[5])
    load.start()
    fetch = pltpu.make_async_copy(saved_in, saved, local.at[0])
    fetch.start()

    def remote(source, target, sent, arrived, device):
        return pltpu.make_async_remote_copy(
            src_ref=source,
            dst_ref=target,
            send_sem=sent,
            recv_sem=arrived,
            device_id=device,
            device_id_type=MESH,
        )

    def part(k):
        return pl.ds(k * piece, piece)

    def near_block(step, a_chip, a_core, k):
        return near[step].at[pl.ds((a_chip * pair + a_core) * count + k * piece, piece)]

    def line_block(step, a_core, a_level, k):
        return line[step].at[pl.ds((a_core * depth + a_level) * count + k * piece, piece)]

    def near_copy(step, up, right, k, source, a_chip, target):
        at = up * width + right - 1
        return remote(
            source,
            near_block(step, a_chip, core, k),
            near_send.at[step],
            near_recv.at[step, at, k],
            chip_id(target),
        )

    def near_got(step, up, right, k):
        a_chip = chip_at(-up, -right)
        block = near_block(step, a_chip, core, k)
        near_copy(step, up, right, k, block, a_chip, a_chip).wait_recv()
        for turn in range(1, pair):
            near_mate(step, a_chip, turn, k, block).start()
        return block, a_chip

    def near_mate(step, a_chip, turn, k, source):
        return remote(
            source,
            near_block(step, a_chip, core, k),
            near_pass.at[step],
            near_take.at[step],
            mate_id(turn),
        )

    def line_copy(step, way, hop, k, source):
        a_level = level - (hop - 1) if way == 0 else level + (hop - 1)
        return remote(
            source,
            line_block(step, core, a_level, k),
            line_send.at[step],
            line_recv.at[step, way, hop - 1, k],
            level_id(level + 1 if way == 0 else level - 1),
        )

    def line_mate(step, a_level, turn, k, source):
        return remote(
            source,
            line_block(step, core, a_level, k),
            line_pass.at[step],
            line_take.at[step],
            mate_id(turn),
        )

    def z_copy(step, way, a_level, k):
        return remote(
            zout.at[step, a_level, pl.ds(k * piece, piece)],
            zin.at[step, way, a_level, pl.ds(k * piece, piece)],
            z_send.at[step],
            z_recv.at[step, way, a_level, k],
            level_id(level + 1 if way == 0 else level - 1),
        )

    def row_copy(step, up, right):
        return remote(
            rout.at[step, chip_at(up, right), part(0)],
            row_in.at[step, right - 1, up],
            r_send.at[step],
            row_recv.at[step, right - 1, up],
            chip_id(chip_at(0, right)),
        )

    def col_copy(step, up, right):
        return remote(
            rout.at[step, chip_at(up, right), part(1)],
            col_in.at[step, up - 1, right],
            r_send.at[step],
            col_recv.at[step, up - 1, right],
            chip_id(chip_at(up, 0)),
        )

    def col_final(step, up):
        return remote(
            rout.at[step, chip_at(up, 0), part(0)],
            col_end.at[step, up - 1],
            r_send.at[step],
            col_done.at[step, up - 1],
            chip_id(chip_at(up, 0)),
        )

    def row_final(step, right):
        return remote(
            rout.at[step, chip_at(0, right), part(1)],
            row_end.at[step, right - 1],
            r_send.at[step],
            row_done.at[step, right - 1],
            chip_id(chip_at(0, right)),
        )

    def ladder_level(other):
        return remote(
            ladder, ladders.at[level], ladder_send, ladder_recv, level_id(other)
        )

    def ladder_chip(other):
        return remote(
            ladder,
            ladders.at[depth + chip],
            ladder_send,
            ladder_recv,
            chip_id(other),
        )

    def each_ladder(act):
        def one_level(other, carry):
            @pl.when(other != level)
            def _():
                act(ladder_level(other))

            return carry

        def one_chip(other, carry):
            @pl.when(other != chip)
            def _():
                act(ladder_chip(other))

            return carry

        lax.fori_loop(0, depth, one_level, 0)
        lax.fori_loop(0, chips, one_chip, 0)

    def passed_ladders(semaphore):
        if depth + chips > 2:
            passed = ladders.at[pl.ds(0, depth + chips - 2)]
            pltpu.make_async_copy(passed, passed, semaphore).wait()

    def note_own():
        for way in range(2):
            for mode in range(modes):
                for j in range(count):
                    value = ladder[way, mode, j]
                    ladders[level, way, mode, j] = value
                    ladders[depth + chip, way, mode, j] = value

        def locate(owner, carry):
            a_node, a_spot = split(owner, cores)
            a_level, a_column = split(a_spot, width)
            a_side, a_core = split(a_node, pair)
            home[0, owner] = ((a_side * width + a_column) * pair + a_core) * count
            home[1, owner] = (a_core * depth + a_level) * count
            inside[0, owner] = jnp.where(a_level == level, 1.0, 0.0)
            beside = jnp.logical_and(a_side == side, a_column == column)
            inside[1, owner] = jnp.where(beside, 1.0, 0.0)
            return carry

        lax.fori_loop(0, owners, locate, 0)

    def tabulate(along_z):
        def entry(at):
            index, j = split(at, count)
            if along_z:
                target, kind, row = node * cores + index * width + column, 0, index
            else:
                a_side, a_column = split(index, width)
                target = (a_side * pair + core) * cores + level * width + a_column
                kind, row = 1, depth + index
            for way in range(2):
                for mode in range(modes):
                    source, member = split((higher, lower)[way][mode, target * count + j], count)
                    value = ladders[row, way, mode, j].astype(F32) * rates[way, mode]
                    slot = (row * count + j) * slots + way * modes + mode
                    place[slot] = home[kind, source] + member
                    weight[slot] = inside[kind, source] * value

        each(0, (depth if along_z else chips) * count, entry)

    def partial(blocks, row, k, put):
        operator = coupling[...]

        def some(pick, carry):
            plus, minus = [], []
            for i in range(2):
                sums = []
                for way in range(2):
                    total = None
                    for mode in range(modes):
                        at = (row * count + pick * 2 + i) * slots + way * modes + mode
                        scale = jnp.full((16, dim), weight[at], F32).astype(BF16)
                        term = blocks[place[at]].reshape(dim // 16, 16, dim) * scale
                        total = term if total is None else total + term
                    sums.append(total.reshape(dim, dim))
                plus.append(sums[0] + sums[1])
                minus.append(sums[0] - sums[1])
            left = dot(operator, jnp.concatenate(plus, axis=1))
            right = dot(jnp.concatenate(minus, axis=0), operator)
            for i in range(2):
                value = left[:, i * dim : (i + 1) * dim] - right[i * dim : (i + 1) * dim]
                put(pick * 2 + i, value.astype(BF16))
            return carry

        lax.fori_loop(k * piece // 2, (k + 1) * piece // 2, some, 0)

    def prepare():
        def one(at, carry):
            step, sub = at // subs, at % subs
            u_re = propagators[step, sub, 0]
            u_im = propagators[step, sub, 1]
            right_u[at, :dim, :dim] = u_re
            right_u[at, :dim, dim:] = u_im
            right_u[at, dim:, :dim] = -u_im
            right_u[at, dim:, dim:] = u_re
            t_re = u_re.T
            t_im = u_im.T
            left_u[at, :dim, :dim] = t_re
            left_u[at, :dim, dim:] = t_im
            left_u[at, dim:, :dim] = -t_im
            left_u[at, dim:, dim:] = t_re
            return carry

        lax.fori_loop(0, steps * subs, one, 0)

        def accumulate(sub):
            for step in range(steps):
                at = step * subs + sub
                right_u[at] = dot(right_u[at - 1], right_u[at]).astype(BF16)
                left_u[at] = dot(left_u[at], left_u[at - 1]).astype(BF16)

        each(1, subs, accumulate)

    def turn_saved(step, sub):
        flat = jnp.concatenate(
            [
                jnp.concatenate([saved[step, sub, j, part].T for part in range(2)], axis=1)
                for j in range(count)
            ],
            axis=0,
        )
        turned = dot(flat, left_u[step * subs + sub]).astype(BF16)
        for j in range(count):
            for part in range(2):
                saved_t[step, sub, part * dim : (part + 1) * dim, j * dim : (j + 1) * dim] = turned[
                    j * dim : (j + 1) * dim, part * dim : (part + 1) * dim
                ]

    def flatten(step):
        return jnp.concatenate(
            [
                jnp.concatenate([hist[step, 0, j, part] for part in range(2)], axis=1)
                for j in range(count)
            ],
            axis=0,
        )

    def project(step, lo, hi):
        total = dot(
            saved_t[step, lo:hi].reshape((hi - lo) * 2 * dim, count * dim), flatten(step)
        )
        for sub in range(lo, hi):
            at = step * subs + sub
            top = total[(sub - lo) * 2 * dim : (sub - lo) * 2 * dim + dim]
            low = total[(sub - lo) * 2 * dim + dim : (sub - lo + 1) * 2 * dim]
            re = top[:, :dim] + low[:, dim:]
            im = top[:, dim:] - low[:, :dim]
            terms[at] = dot(jnp.concatenate([re, im], axis=1).astype(BF16), right_u[at])

    def stage(group):
        for target in range(owners):
            term_stage[group, target] = jnp.concatenate(
                [
                    terms[(steps - 1) * subs + group * batch + i, target * rows : (target + 1) * rows]
                    for i in range(batch)
                ],
                axis=0,
            ).astype(BF16)

    def spread(group):
        def send(offset, carry):
            pltpu.make_async_remote_copy(
                src_ref=term_stage.at[group, lax.rem(own + offset, owners)],
                dst_ref=term_inbox.at[group, offset - 1],
                send_sem=term_send.at[group],
                recv_sem=term_recv.at[group],
                device_id=owner_id(offset),
                device_id_type=MESH,
            ).start()
            return carry

        lax.fori_loop(1, owners, send, 0)

    def finish(group):
        everything = term_inbox.at[group]
        pltpu.make_async_copy(everything, everything, term_recv.at[group]).wait()
        total = term_stage[group, own].astype(F32)
        for offset in range(1, owners):
            total = total + term_inbox[group, offset - 1].astype(F32)
        for i in range(batch):
            for row in range(rows):
                for part in range(2):
                    grad[row, (steps - 1) * subs + group * batch + i, part : part + 1, :] = total[
                        i * rows + row : i * rows + row + 1, part * dim : (part + 1) * dim
                    ]
        pltpu.make_async_copy(everything, everything, term_send.at[group]).wait()

    def rotate(step):
        at = step * subs + subs - 1
        mult_l = left_u[at]
        middles = dot(flatten(step), right_u[at]).astype(BF16)
        for j in range(0, count, 2):
            middle = middles[j * dim : (j + 2) * dim]
            stacked = jnp.concatenate(
                [
                    jnp.concatenate([middle[:dim, :dim], middle[dim:, :dim]], axis=1),
                    jnp.concatenate([middle[:dim, dim:], middle[dim:, dim:]], axis=1),
                ],
                axis=0,
            )
            result = dot(mult_l, stacked).astype(BF16)
            for i in range(2):
                for part in range(2):
                    hist[step, 1, j + i, part] = result[
                        part * dim : (part + 1) * dim, i * dim : (i + 1) * dim
                    ]

    def add_to(target, sources):
        total = target[...].astype(F32)
        for source in sources:
            total = total + source[...].astype(F32)
        target[...] = total.astype(BF16)

    def early_copy(step, kind, at, source, target, device):
        return remote(
            source, target, early_sent.at[step, kind], early_got.at[step, kind, at], device
        )

    def early_mate(step, turn):
        return early_copy(
            step,
            0,
            turn - 1,
            early.at[step, lax.rem(core + turn, pair)],
            early_core.at[step],
            mate_id(turn),
        )

    def early_along(step, right):
        a_column = lax.rem(column + right, width)
        return early_copy(
            step,
            1,
            right - 1,
            early.at[step, core, a_column],
            early_row.at[step, right - 1],
            chip_id(chip_at(0, right)),
        )

    def early_across(step, up):
        a_side = lax.rem(side + up, tall)
        return early_copy(
            step,
            2,
            up - 1,
            early.at[step, core, column, a_side],
            early_col.at[step, up - 1],
            chip_id(chip_at(up, 0)),
        )

    def early_level(step, other, sender):
        return remote(
            early.at[step, core, column, side, other],
            early_z.at[step, sender],
            early_sent.at[step, 3],
            early_z_got.at[step],
            level_id(other),
        )

    def early_start(step):
        for target in range(owners):
            a_node, a_spot = target // cores, target % cores
            early[step, a_node % pair, a_spot % width, a_node // pair, a_spot // width] = (
                jnp.concatenate(
                    [
                        terms[step * subs + sub, target * rows : (target + 1) * rows]
                        for sub in range(subs)
                    ],
                    axis=0,
                ).astype(BF16)
            )
        for turn in range(1, pair):
            early_mate(step, turn).start()

    def early_rows(step):
        for turn in range(1, pair):
            early_mate(step, turn).wait_recv()
            add_to(early.at[step, core], [early_core.at[step]])
        for right in range(1, width):
            early_along(step, right).start()

    def early_cols(step):
        for right in range(1, width):
            early_along(step, right).wait_recv()
        add_to(
            early.at[step, core, column],
            [early_row.at[step, right - 1] for right in range(1, width)],
        )
        for up in range(1, tall):
            early_across(step, up).start()

    def early_levels(step):
        for up in range(1, tall):
            early_across(step, up).wait_recv()
        add_to(
            early.at[step, core, column, side],
            [early_col.at[step, up - 1] for up in range(1, tall)],
        )

        def send(other):
            pl.when(other != level)(lambda: early_level(step, other, level).start())

        each(0, depth, send)

    def early_finish(step):
        early_z[step, level] = early[step, core, column, side, level]

        if depth > 1:
            passed = early_z.at[step, pl.ds(0, depth - 1)]
            pltpu.make_async_copy(passed, passed, early_z_got.at[step]).wait()
        total = early_z[step, 0].astype(F32)
        for other in range(1, depth):
            total = total + early_z[step, other].astype(F32)
        for sub in range(subs):
            for row in range(rows):
                at = sub * rows + row
                for part in range(2):
                    grad[row, step * subs + sub, part : part + 1, :] = total[
                        at : at + 1, part * dim : (part + 1) * dim
                    ]
        if pair > 1:
            pltpu.make_async_copy(
                early_core.at[step], early_core.at[step], early_sent.at[step, 0]
            ).wait()
        if width > 1:
            pltpu.make_async_copy(
                early_row.at[step], early_row.at[step], early_sent.at[step, 1]
            ).wait()
        if tall > 1:
            pltpu.make_async_copy(
                early_col.at[step], early_col.at[step], early_sent.at[step, 2]
            ).wait()
        if depth > 1:
            passed = early_z.at[step, pl.ds(0, depth - 1)]
            pltpu.make_async_copy(passed, passed, early_sent.at[step, 3]).wait()

    def join(step, state):
        def one(j, carry):
            lam = decay[j] * state[j, 0].astype(F32) + zout[step, level, j].astype(F32)
            hist[step, 0, j, 0] = lam.astype(BF16)
            total = rout[step, chip, j].astype(F32)
            lam = decay[j] * state[j, 1].astype(F32) - total
            hist[step, 0, j, 1] = lam.astype(BF16)
            return carry

        lax.fori_loop(0, count, one, 0)

    def fold(target, sources):
        for j in range(piece):
            total = target[j].astype(F32)
            for source in sources:
                total = total + source[j].astype(F32)
            target[j] = total.astype(BF16)

    def arrives(way, hop):
        return level >= hop if way == 0 else level + hop < depth

    def goes_on(way, hop):
        if way == 0:
            return jnp.logical_and(level >= hop - 1, level < depth - 1)
        return jnp.logical_and(level + hop - 1 < depth, level > 0)

    def take_line(step, hop, k, chosen=None):
        for way in range(2):
            due = arrives(way, hop)
            if chosen is not None:
                onward = goes_on(way, hop + 1)
                due = jnp.logical_and(due, onward if chosen else jnp.logical_not(onward))

            @pl.when(due)
            def _(way=way):
                a_level = level - hop if way == 0 else level + hop
                block = line_block(step, core, a_level, k)
                remote(
                    block,
                    block,
                    line_send.at[step],
                    line_recv.at[step, way, hop - 1, k],
                    level_id(level),
                ).wait_recv()
                if hop + 1 < depth:

                    @pl.when(goes_on(way, hop + 1))
                    def _():
                        line_copy(step, way, hop + 1, k, block).start()

                for turn in range(1, pair):
                    line_mate(step, a_level, turn, k, block).start()

    def take_first(step):
        def along(right):
            block, a_chip = near_got(step, 0, right, 0)
            each(
                1,
                tall,
                lambda up: near_copy(
                    step, up, right, 0, block, a_chip, chip_at(up, 0)
                ).start(),
            )

        def across(up):
            block, a_chip = near_got(step, up, 0, 1)
            each(
                1,
                width,
                lambda right: near_copy(
                    step, up, right, 1, block, a_chip, chip_at(0, right)
                ).start(),
            )

        each(1, width, along)
        each(1, tall, across)

    def take_second(step):
        each(1, width, lambda right: near_got(step, 0, right, 1) and None)
        each(1, tall, lambda up: near_got(step, up, 0, 0) and None)

    def take_far(step):
        def one(up):
            def two(right):
                for k in range(pieces):
                    near_got(step, up, right, k)

            each(1, width, two)

        each(1, tall, one)
        for turn in range(1, pair):

            passed = near[step].at[pl.ds(0, chips * count)]
            pltpu.make_async_copy(passed, passed, near_take.at[step]).wait()

    def mates_line(step):
        for turn in range(1, pair):

            passed = line[step].at[pl.ds(0, depth * count)]
            pltpu.make_async_copy(passed, passed, line_take.at[step]).wait()

    def reduce_start(step, lo, hi):
        def one(i, carry):
            a_level = jnp.where(level * 2 < depth, depth - 1 - i, i)

            def put(j, value):
                zout[step, a_level, j] = value

            for k in range(pieces):
                partial(near[step], a_level, k, put)

                @pl.when(jnp.logical_and(level == 0, a_level > 0))
                def _(k=k):
                    z_copy(step, 0, a_level, k).start()

                @pl.when(jnp.logical_and(level == depth - 1, a_level < depth - 1))
                def _(k=k):
                    z_copy(step, 1, a_level, k).start()

            return carry

        lax.fori_loop(lo, hi, one, 0)

    def exchange(step):
        def one(i):
            up, right = split(chips - 1 - i, width)
            target = chip_at(up, right)

            def put(j, value):
                rout[step, target, j] = value

            partial(line[step], depth + target, 0, put)

            @pl.when(right > 0)
            def _():
                row_copy(step, up, right).start()

            for k in range(1, pieces):
                partial(line[step], depth + target, k, put)

            @pl.when(up > 0)
            def _():
                col_copy(step, up, right).start()

        each(0, chips, one)

    def exchange_on(step):
        def column(up):
            target = chip_at(up, 0)
            each(1, width, lambda right: row_copy(step, up, right).wait_recv())
            fold(
                rout.at[step, target, part(0)],
                [row_in.at[step, right - 1, up] for right in range(1, width)],
            )
            col_final(step, up).start()

        def line_of(right):
            target = chip_at(0, right)
            each(1, tall, lambda up: col_copy(step, up, right).wait_recv())
            fold(
                rout.at[step, target, part(1)],
                [col_in.at[step, up - 1, right] for up in range(1, tall)],
            )
            row_final(step, right).start()

        each(1, tall, column)
        each(1, width, line_of)

    def exchange_end(step):
        each(1, width, lambda right: row_copy(step, 0, right).wait_recv())
        each(1, tall, lambda up: col_copy(step, up, 0).wait_recv())
        each(1, tall, lambda up: col_final(step, up).wait_recv())
        each(1, width, lambda right: row_final(step, right).wait_recv())
        fold(
            rout.at[step, chip, part(0)],
            [row_in.at[step, right - 1, 0] for right in range(1, width)]
            + [col_end.at[step, up - 1] for up in range(1, tall)],
        )
        fold(
            rout.at[step, chip, part(1)],
            [col_in.at[step, up - 1, 0] for up in range(1, tall)]
            + [row_end.at[step, right - 1] for right in range(1, width)],
        )

    def reduce_on(step, ahead):
        for k in range(pieces):
            for way in range(2):
                if way == 0:
                    a_level = level + ahead
                    fits = jnp.logical_and(level > 0, a_level < depth)
                else:
                    a_level = level - ahead
                    fits = jnp.logical_and(level < depth - 1, a_level >= 0)

                @pl.when(fits)
                def _(way=way, k=k, a_level=a_level):
                    z_copy(step, way, a_level, k).wait_recv()
                    fold(
                        zout.at[step, a_level, part(k)], [zin.at[step, way, a_level, part(k)]]
                    )
                    if ahead > 0:
                        z_copy(step, way, a_level, k).start()

    pl.semaphore_wait(barrier, depth + chips + pair - 3)
    tables[0].wait()
    each_ladder(lambda copy: copy.start())
    for step in range(steps):
        state = adjoint if step == 0 else hist.at[step - 1, 1]
        for k in range(pieces):
            for way in range(2):

                @pl.when(goes_on(way, 1))
                def _(way=way, k=k):
                    line_copy(step, way, 1, k, state.at[part(k), 0]).start()

        def first(right, k, step=step, state=state):
            near_copy(step, 0, right, k, state.at[part(k), 1], chip, chip_at(0, right)).start()

        def other(up, k, step=step, state=state):
            near_copy(step, up, 0, k, state.at[part(k), 1], chip, chip_at(up, 0)).start()

        each(1, width, lambda right: first(right, 0))
        each(1, tall, lambda up: other(up, 1))
        each(1, width, lambda right: first(right, 1))
        each(1, tall, lambda up: other(up, 0))
        for k in range(pieces):
            for turn in range(1, pair):
                near_mate(step, chip, turn, k, state.at[part(k), 1]).start()
                line_mate(step, level, turn, k, state.at[part(k), 0]).start()
        keep_im = pltpu.make_async_copy(
            state.at[:, 1], near[step].at[pl.ds((chip * pair + core) * count, count)], local.at[2]
        )
        keep_re = pltpu.make_async_copy(
            state.at[:, 0], line[step].at[pl.ds((core * depth + level) * count, count)], local.at[3]
        )
        keep_im.start()
        keep_re.start()
        if step == 0:
            greet_levels(hello)
            for copy in tables[1:]:
                copy.wait()
            note_own()
            passed_ladders(ladder_recv)
            tabulate(True)
        else:
            for sub in range(subs):
                turn_saved(step - 1, sub)
            for half in range(halves):
                project(step - 1, half * batch, (half + 1) * batch)
        if depth > 1:
            take_line(step, 1, 0)
        take_first(step)
        if step == 0:
            tabulate(False)
            pl.semaphore_wait(hello, depth - 1)
            greet_mates(again)
        else:
            early_start(step - 1)
        for k in range(1, pieces):
            if depth > 1:
                take_line(step, 1, k)
        take_second(step)
        if step > 0:
            early_rows(step - 1)
        keep_im.wait()
        keep_re.wait()
        take_far(step)
        reduce_start(step, 0, 1)
        if depth > 2:
            for k in range(pieces):
                take_line(step, 2, k, True)
        reduce_start(step, 1, depth)
        if step > 0:
            early_cols(step - 1)
        reduce_on(step, depth - 2)
        if depth > 2:
            for k in range(pieces):
                take_line(step, 2, k, False)
        for hop in range(3, depth):
            for k in range(pieces):
                take_line(step, hop, k)
        mates_line(step)
        exchange(step)
        if step > 0:
            early_levels(step - 1)
        for ahead in range(depth - 3, 0, -1):
            reduce_on(step, ahead)
        exchange_on(step)
        if step == 0:
            load_u.wait()
            prepare()
            fetch.wait()
        if step == steps - 1:
            for sub in range(subs):
                turn_saved(step, sub)
        if depth != 2:
            reduce_on(step, 0)
        exchange_end(step)
        if step == steps - 1:
            pl.semaphore_wait(again, pair - 1)
        if step == 0:
            load.wait()
        join(step, held if step == 0 else state)
        if step == steps - 1:
            for half in range(halves):
                project(step, half * batch, (half + 1) * batch)
                stage(half)
                spread(half)
        rotate(step)
    result = pltpu.make_async_copy(hist.at[steps - 1, 1], out, local.at[1])
    result.start()

    def sent(source, amount, semaphore):
        if amount > 0:
            passed = source.at[pl.ds(0, amount)]
            pltpu.make_async_copy(passed, passed, semaphore).wait()

    for step in range(steps):
        sent(near[step], (chips - 1) * count, near_send.at[step])
        sent(near[step], (pair - 1) * chips * count, near_pass.at[step])
        sent(line[step], (pair - 1) * depth * count, line_pass.at[step])
        crossings = (width - 1) * (tall + 1) + (tall - 1) * (width + 1)
        sent(near[step], crossings * piece, r_send.at[step])
        sent(zout.at[step], depth - 1, z_send.at[step])
        for a_level in range(depth):
            ups = a_level + 1 if a_level < depth - 1 else 0
            downs = depth - a_level if a_level > 0 else 0

            @pl.when(level == a_level)
            def _(step=step, blocks=ups + downs):
                sent(line[step], blocks * count, line_send.at[step])

    passed_ladders(ladder_send)
    result.wait()
    for step in range(steps - 1):
        early_finish(step)
    for half in range(halves):
        finish(half)


def deliver(state, grad, state_out, grad_out, state_kept, grad_kept, sems):
    into = [
        pltpu.make_async_copy(state, state_kept, sems.at[0]),
        pltpu.make_async_copy(grad, grad_kept, sems.at[1]),
    ]
    back = [
        pltpu.make_async_copy(state_kept, state_out, sems.at[2]),
        pltpu.make_async_copy(grad_kept, grad_out, sems.at[3]),
    ]
    for copy in into:
        copy.start()
    for arrival, leave in zip(into, back):
        arrival.wait()
        leave.start()
    for copy in back:
        copy.wait()


def body(adjoint, saved, propagators, coupling, higher, lower, ladder, rates, decay):
    nodes = lax.axis_size("node")
    cores = lax.axis_size("cores")
    owners = nodes * cores
    count = adjoint.shape[0]
    modes = higher.shape[1]
    steps, subs = propagators.shape[:2]
    dim = coupling.shape[0]
    depth = 1 << (cores.bit_length() // 2)
    width = cores // depth
    pair = 2 if nodes % 2 == 0 else 1
    chips = nodes // pair * width
    pieces = 2
    rows = dim // owners
    halves = 2 if subs % 2 == 0 else 1
    batch = subs // halves
    higher, lower, ladder = higher.T, lower.T, jnp.swapaxes(ladder, 1, 2)
    vmem = pl.BlockSpec(memory_space=pltpu.VMEM)
    block = adjoint.shape
    hbm = pl.BlockSpec(memory_space=pl.ANY)
    hops = max(depth - 1, 1)
    others = max(chips - 1, 1)
    mates = max(pair - 1, 1)
    half = (count,) + block[2:]
    bit = (count // pieces,) + block[2:]
    tall = nodes // pair
    before = max(steps - 1, 1)
    slab = (subs * rows, 2 * dim)
    table = (depth + chips) * count * 2 * modes
    dma = pltpu.SemaphoreType.DMA
    state, grad = pl.pallas_call(
        functools.partial(kernel, (nodes, depth, width, pair, count, modes, steps, subs, dim, halves, pieces)),
        out_shape=(
            jax.ShapeDtypeStruct(block, BF16),
            jax.ShapeDtypeStruct((rows, steps * subs, 2, dim), F32),
        ),
        in_specs=[hbm] * 9,
        out_specs=(hbm, vmem),
        scratch_shapes=[
            pltpu.VMEM((steps * subs, 2 * dim, 2 * dim), BF16),
            pltpu.VMEM((steps * subs, 2 * dim, 2 * dim), BF16),
            pltpu.VMEM((steps, 2) + block, BF16),
            pltpu.VMEM((steps, depth) + half, BF16),
            pltpu.VMEM((steps, 2, depth) + half, BF16),
            pltpu.VMEM((steps, chips) + half, BF16),
            pltpu.VMEM((steps, max(width - 1, 1), tall) + bit, BF16),
            pltpu.VMEM((steps, max(tall - 1, 1), width) + bit, BF16),
            pltpu.VMEM((steps, max(width - 1, 1)) + bit, BF16),
            pltpu.VMEM((steps, max(tall - 1, 1)) + bit, BF16),
            pltpu.VMEM((steps * subs, dim, 2 * dim), F32),
            pltpu.VMEM((halves, owners, batch * rows, 2 * dim), BF16),
            pltpu.VMEM((halves, owners - 1, batch * rows, 2 * dim), BF16),
            pltpu.VMEM(saved.shape, BF16),
            pltpu.VMEM((steps, subs, 2 * dim, count * dim), BF16),
            pltpu.SMEM((table,), jnp.int32),
            pltpu.SMEM((table,), F32),
            pltpu.SMEM((2, owners), jnp.int32),
            pltpu.SMEM((2, owners), F32),
            pltpu.SMEM((depth + chips, 2, modes, count), jnp.int32),
            dma((steps,)),
            dma((steps, others, pieces)),
            dma((steps,)),
            dma((steps,)),
            dma((steps,)),
            dma((steps, 2, hops, pieces)),
            dma((steps,)),
            dma((steps,)),
            dma((steps,)),
            dma((steps, 2, depth, pieces)),
            dma((steps,)),
            dma((steps, max(width - 1, 1), tall)),
            dma((steps, max(tall - 1, 1), width)),
            dma((steps, max(width - 1, 1))),
            dma((steps, max(tall - 1, 1))),
            dma(()),
            dma(()),
            dma((halves,)),
            dma((halves,)),
            pltpu.SemaphoreType.REGULAR,
            pltpu.SemaphoreType.REGULAR,
            dma((6,)),
            pltpu.VMEM(propagators.shape, BF16),
            pltpu.VMEM(block, BF16),
            pltpu.VMEM(coupling.shape, BF16),
            pltpu.SMEM(higher.shape, jnp.int32),
            pltpu.SMEM(lower.shape, jnp.int32),
            pltpu.SMEM(ladder.shape, jnp.int32),
            pltpu.SMEM(rates.shape, F32),
            pltpu.SMEM(decay.shape, F32),
            dma((6,)),
            pltpu.VMEM((before, pair, width, tall, depth) + slab, BF16),
            pltpu.VMEM((before, width, tall, depth) + slab, BF16),
            pltpu.VMEM((before, max(width - 1, 1), tall, depth) + slab, BF16),
            pltpu.VMEM((before, max(tall - 1, 1), depth) + slab, BF16),
            pltpu.VMEM((before, depth) + slab, BF16),
            dma((before, 4)),
            dma((before, 3, max(width - 1, tall - 1, 1))),
            dma((before,)),
            *[pltpu.VMEM((chips * pair * count, dim, dim), BF16)] * steps,
            *[pltpu.VMEM((depth * pair * count, dim, dim), BF16)] * steps,
        ],
        compiler_params=pltpu.CompilerParams(
            collective_id=0, has_side_effects=True, vmem_limit_bytes=63_000_000
        ),
    )(higher, lower, ladder, rates, decay, adjoint, saved, propagators, coupling)
    return pl.pallas_call(
        deliver,
        out_shape=(
            jax.ShapeDtypeStruct(state.shape, state.dtype),
            jax.ShapeDtypeStruct(grad.shape, grad.dtype),
        ),
        in_specs=[hbm, hbm],
        out_specs=(hbm, hbm),
        scratch_shapes=[
            pltpu.VMEM(state.shape, state.dtype),
            pltpu.VMEM(grad.shape, grad.dtype),
            dma((4,)),
        ],
    )(state, grad)


def solution(mesh):
    return jax.shard_map(
        body,
        mesh=mesh,
        in_specs=(
            P(("node", "cores"), None, None, None),
            P(None, None, ("node", "cores"), None, None, None),
            P(),
            P(),
            P(),
            P(),
            P(None, ("node", "cores"), None),
            P(),
            P(("node", "cores")),
        ),
        out_specs=(P(("node", "cores"), None, None, None), P(("node", "cores"), None, None, None)),
        check_vma=False,
    )
```

```python
import functools

import jax
import jax.numpy as jnp
from jax import lax
from jax.experimental import pallas as pl
from jax.experimental.pallas import tpu as pltpu
from jax.sharding import PartitionSpec as P

MESH = pl.DeviceIdType.MESH
F32 = jnp.float32
BF16 = jnp.bfloat16


def dot(a, b):
    return jnp.dot(a, b, preferred_element_type=F32)


def kernel(
    dims,
    higher_in,
    lower_in,
    ladder_in,
    rates_in,
    decay_in,
    adjoint,
    saved_in,
    propagators_in,
    coupling_in,
    out,
    grad,
    right_u,
    left_u,
    hist,
    zout,
    zin,
    rout,
    row_in,
    col_in,
    row_end,
    col_end,
    terms,
    term_stage,
    term_inbox,
    saved,
    saved_t,
    place,
    weight,
    home,
    inside,
    ladders,
    near_send,
    near_recv,
    near_pass,
    near_take,
    line_send,
    line_recv,
    line_pass,
    line_take,
    z_send,
    z_recv,
    r_send,
    row_recv,
    col_recv,
    row_done,
    col_done,
    ladder_send,
    ladder_recv,
    term_send,
    term_recv,
    hello,
    again,
    local,
    propagators,
    held,
    coupling,
    higher,
    lower,
    ladder,
    rates,
    decay,
    table_sem,
    early,
    early_core,
    early_row,
    early_col,
    early_z,
    early_sent,
    early_got,
    early_z_got,
    *gathered,
):
    nodes, depth, width, pair, count, modes, steps, subs, dim, halves, pieces = dims
    near, line = gathered[:steps], gathered[steps:]
    cores = depth * width
    owners = nodes * cores
    tall = nodes // pair
    chips = tall * width
    rows = dim // owners
    batch = subs // halves
    piece = count // pieces
    slots = 2 * modes
    node = lax.axis_index("node")
    spot = lax.axis_index("cores")
    level = spot // width
    column = spot % width
    side = node // pair
    core = node % pair
    chip = side * width + column

    def split(value, size):
        if size & (size - 1) == 0:
            return value >> (size.bit_length() - 1), value & (size - 1)
        return lax.div(value, size), lax.rem(value, size)

    def chip_id(other):
        return ((other // width) * pair + core, level * width + other % width)

    def chip_at(up, right):
        return lax.rem(side + up + tall, tall) * width + lax.rem(column + right + width, width)

    def mate_id(turn):
        return (side * pair + lax.rem(core + turn, pair), spot)

    def level_id(other):
        return (node, other * width + column)

    barrier = pltpu.get_barrier_semaphore()

    own = node * cores + spot

    def owner_id(offset):
        return split(split(own + offset, owners)[1], cores)

    def each(lo, hi, act):
        def one(i, carry):
            act(i)
            return carry

        lax.fori_loop(lo, hi, one, 0)

    def signal(semaphore, device):
        pl.semaphore_signal(semaphore, inc=1, device_id=device, device_id_type=MESH)

    def greet_levels(semaphore):
        def greet(other):
            pl.when(other != level)(lambda: signal(semaphore, level_id(other)))

        each(0, depth, greet)

    def greet_mates(semaphore):
        for turn in range(1, pair):
            signal(semaphore, mate_id(turn))

    def greet_chips(semaphore):
        def greet(other):
            pl.when(other != chip)(lambda: signal(semaphore, chip_id(other)))

        each(0, chips, greet)

    greet_levels(barrier)
    greet_chips(barrier)
    greet_mates(barrier)
    tables = [
        pltpu.make_async_copy(source, target, table_sem.at[at])
        for at, (source, target) in enumerate(
            (
                (ladder_in, ladder),
                (higher_in, higher),
                (lower_in, lower),
                (rates_in, rates),
                (decay_in, decay),
                (coupling_in, coupling),
            )
        )
    ]
    for copy in tables:
        copy.start()
    load_u = pltpu.make_async_copy(propagators_in, propagators, local.at[4])
    load_u.start()
    load = pltpu.make_async_copy(adjoint, held, local.at[5])
    load.start()
    fetch = pltpu.make_async_copy(saved_in, saved, local.at[0])
    fetch.start()

    def remote(source, target, sent, arrived, device):
        return pltpu.make_async_remote_copy(
            src_ref=source,
            dst_ref=target,
            send_sem=sent,
            recv_sem=arrived,
            device_id=device,
            device_id_type=MESH,
        )

    def part(k):
        return pl.ds(k * piece, piece)

    def near_block(step, a_chip, a_core, k):
        return near[step].at[pl.ds((a_chip * pair + a_core) * count + k * piece, piece)]

    def line_block(step, a_core, a_level, k):
        return line[step].at[pl.ds((a_core * depth + a_level) * count + k * piece, piece)]

    def near_copy(step, up, right, k, source, a_chip, target):
        at = up * width + right - 1
        return remote(
            source,
            near_block(step, a_chip, core, k),
            near_send.at[step],
            near_recv.at[step, at, k],
            chip_id(target),
        )

    def near_got(step, up, right, k):
        a_chip = chip_at(-up, -right)
        block = near_block(step, a_chip, core, k)
        near_copy(step, up, right, k, block, a_chip, a_chip).wait_recv()
        for turn in range(1, pair):
            near_mate(step, a_chip, turn, k, block).start()
        return block, a_chip

    def near_mate(step, a_chip, turn, k, source):
        return remote(
            source,
            near_block(step, a_chip, core, k),
            near_pass.at[step],
            near_take.at[step],
            mate_id(turn),
        )

    def line_copy(step, way, hop, k, source):
        a_level = level - (hop - 1) if way == 0 else level + (hop - 1)
        return remote(
            source,
            line_block(step, core, a_level, k),
            line_send.at[step],
            line_recv.at[step, way, hop - 1, k],
            level_id(level + 1 if way == 0 else level - 1),
        )

    def line_mate(step, a_level, turn, k, source):
        return remote(
            source,
            line_block(step, core, a_level, k),
            line_pass.at[step],
            line_take.at[step],
            mate_id(turn),
        )

    def z_copy(step, way, a_level, k):
        return remote(
            zout.at[step, a_level, pl.ds(k * piece, piece)],
            zin.at[step, way, a_level, pl.ds(k * piece, piece)],
            z_send.at[step],
            z_recv.at[step, way, a_level, k],
            level_id(level + 1 if way == 0 else level - 1),
        )

    def row_copy(step, up, right):
        return remote(
            rout.at[step, chip_at(up, right), part(0)],
            row_in.at[step, right - 1, up],
            r_send.at[step],
            row_recv.at[step, right - 1, up],
            chip_id(chip_at(0, right)),
        )

    def col_copy(step, up, right):
        return remote(
            rout.at[step, chip_at(up, right), part(1)],
            col_in.at[step, up - 1, right],
            r_send.at[step],
            col_recv.at[step, up - 1, right],
            chip_id(chip_at(up, 0)),
        )

    def col_final(step, up):
        return remote(
            rout.at[step, chip_at(up, 0), part(0)],
            col_end.at[step, up - 1],
            r_send.at[step],
            col_done.at[step, up - 1],
            chip_id(chip_at(up, 0)),
        )

    def row_final(step, right):
        return remote(
            rout.at[step, chip_at(0, right), part(1)],
            row_end.at[step, right - 1],
            r_send.at[step],
            row_done.at[step, right - 1],
            chip_id(chip_at(0, right)),
        )

    def ladder_level(other):
        return remote(
            ladder, ladders.at[level], ladder_send, ladder_recv, level_id(other)
        )

    def ladder_chip(other):
        return remote(
            ladder,
            ladders.at[depth + chip],
            ladder_send,
            ladder_recv,
            chip_id(other),
        )

    def each_ladder(act):
        def one_level(other, carry):
            @pl.when(other != level)
            def _():
                act(ladder_level(other))

            return carry

        def one_chip(other, carry):
            @pl.when(other != chip)
            def _():
                act(ladder_chip(other))

            return carry

        lax.fori_loop(0, depth, one_level, 0)
        lax.fori_loop(0, chips, one_chip, 0)

    def passed_ladders(semaphore):
        if depth + chips > 2:
            passed = ladders.at[pl.ds(0, depth + chips - 2)]
            pltpu.make_async_copy(passed, passed, semaphore).wait()

    def note_own():
        for way in range(2):
            for mode in range(modes):
                for j in range(count):
                    value = ladder[way, mode, j]
                    ladders[level, way, mode, j] = value
                    ladders[depth + chip, way, mode, j] = value

        def locate(owner, carry):
            a_node, a_spot = split(owner, cores)
            a_level, a_column = split(a_spot, width)
            a_side, a_core = split(a_node, pair)
            home[0, owner] = ((a_side * width + a_column) * pair + a_core) * count
            home[1, owner] = (a_core * depth + a_level) * count
            inside[0, owner] = jnp.where(a_level == level, 1.0, 0.0)
            beside = jnp.logical_and(a_side == side, a_column == column)
            inside[1, owner] = jnp.where(beside, 1.0, 0.0)
            return carry

        lax.fori_loop(0, owners, locate, 0)

    def tabulate(along_z):
        def entry(at):
            index, j = split(at, count)
            if along_z:
                target, kind, row = node * cores + index * width + column, 0, index
            else:
                a_side, a_column = split(index, width)
                target = (a_side * pair + core) * cores + level * width + a_column
                kind, row = 1, depth + index
            for way in range(2):
                for mode in range(modes):
                    source, member = split((higher, lower)[way][mode, target * count + j], count)
                    value = ladders[row, way, mode, j].astype(F32) * rates[way, mode]
                    slot = (row * count + j) * slots + way * modes + mode
                    place[slot] = home[kind, source] + member
                    weight[slot] = inside[kind, source] * value

        each(0, (depth if along_z else chips) * count, entry)

    def partial(blocks, row, k, put):
        operator = coupling[...]

        def some(pick, carry):
            plus, minus = [], []
            for i in range(2):
                sums = []
                for way in range(2):
                    total = None
                    for mode in range(modes):
                        at = (row * count + pick * 2 + i) * slots + way * modes + mode
                        scale = jnp.full((16, dim), weight[at], F32).astype(BF16)
                        term = blocks[place[at]].reshape(dim // 16, 16, dim) * scale
                        total = term if total is None else total + term
                    sums.append(total.reshape(dim, dim))
                plus.append(sums[0] + sums[1])
                minus.append(sums[0] - sums[1])
            left = dot(operator, jnp.concatenate(plus, axis=1))
            right = dot(jnp.concatenate(minus, axis=0), operator)
            for i in range(2):
                value = left[:, i * dim : (i + 1) * dim] - right[i * dim : (i + 1) * dim]
                put(pick * 2 + i, value.astype(BF16))
            return carry

        lax.fori_loop(k * piece // 2, (k + 1) * piece // 2, some, 0)

    def prepare():
        def one(at, carry):
            step, sub = at // subs, at % subs
            u_re = propagators[step, sub, 0]
            u_im = propagators[step, sub, 1]
            right_u[at, :dim, :dim] = u_re
            right_u[at, :dim, dim:] = u_im
            right_u[at, dim:, :dim] = -u_im
            right_u[at, dim:, dim:] = u_re
            t_re = u_re.T
            t_im = u_im.T
            left_u[at, :dim, :dim] = t_re
            left_u[at, :dim, dim:] = t_im
            left_u[at, dim:, :dim] = -t_im
            left_u[at, dim:, dim:] = t_re
            return carry

        lax.fori_loop(0, steps * subs, one, 0)

        def accumulate(sub):
            for step in range(steps):
                at = step * subs + sub
                right_u[at] = dot(right_u[at - 1], right_u[at]).astype(BF16)
                left_u[at] = dot(left_u[at], left_u[at - 1]).astype(BF16)

        each(1, subs, accumulate)

    def turn_saved(step, sub):
        flat = jnp.concatenate(
            [
                jnp.concatenate([saved[step, sub, j, part].T for part in range(2)], axis=1)
                for j in range(count)
            ],
            axis=0,
        )
        turned = dot(flat, left_u[step * subs + sub]).astype(BF16)
        for j in range(count):
            for part in range(2):
                saved_t[step, sub, part * dim : (part + 1) * dim, j * dim : (j + 1) * dim] = turned[
                    j * dim : (j + 1) * dim, part * dim : (part + 1) * dim
                ]

    def flatten(step):
        return jnp.concatenate(
            [
                jnp.concatenate([hist[step, 0, j, part] for part in range(2)], axis=1)
                for j in range(count)
            ],
            axis=0,
        )

    def project(step, lo, hi):
        total = dot(
            saved_t[step, lo:hi].reshape((hi - lo) * 2 * dim, count * dim), flatten(step)
        )
        for sub in range(lo, hi):
            at = step * subs + sub
            top = total[(sub - lo) * 2 * dim : (sub - lo) * 2 * dim + dim]
            low = total[(sub - lo) * 2 * dim + dim : (sub - lo + 1) * 2 * dim]
            re = top[:, :dim] + low[:, dim:]
            im = top[:, dim:] - low[:, :dim]
            terms[at] = dot(jnp.concatenate([re, im], axis=1).astype(BF16), right_u[at])

    def stage(group):
        for target in range(owners):
            term_stage[group, target] = jnp.concatenate(
                [
                    terms[(steps - 1) * subs + group * batch + i, target * rows : (target + 1) * rows]
                    for i in range(batch)
                ],
                axis=0,
            ).astype(BF16)

    def spread(group):
        def send(offset, carry):
            pltpu.make_async_remote_copy(
                src_ref=term_stage.at[group, lax.rem(own + offset, owners)],
                dst_ref=term_inbox.at[group, offset - 1],
                send_sem=term_send.at[group],
                recv_sem=term_recv.at[group],
                device_id=owner_id(offset),
                device_id_type=MESH,
            ).start()
            return carry

        lax.fori_loop(1, owners, send, 0)

    def finish(group):
        everything = term_inbox.at[group]
        pltpu.make_async_copy(everything, everything, term_recv.at[group]).wait()
        total = term_stage[group, own].astype(F32)
        for offset in range(1, owners):
            total = total + term_inbox[group, offset - 1].astype(F32)
        for i in range(batch):
            for row in range(rows):
                for part in range(2):
                    grad[row, (steps - 1) * subs + group * batch + i, part : part + 1, :] = total[
                        i * rows + row : i * rows + row + 1, part * dim : (part + 1) * dim
                    ]
        pltpu.make_async_copy(everything, everything, term_send.at[group]).wait()

    def rotate(step):
        at = step * subs + subs - 1
        mult_l = left_u[at]
        middles = dot(flatten(step), right_u[at]).astype(BF16)
        for j in range(0, count, 2):
            middle = middles[j * dim : (j + 2) * dim]
            stacked = jnp.concatenate(
                [
                    jnp.concatenate([middle[:dim, :dim], middle[dim:, :dim]], axis=1),
                    jnp.concatenate([middle[:dim, dim:], middle[dim:, dim:]], axis=1),
                ],
                axis=0,
            )
            result = dot(mult_l, stacked).astype(BF16)
            for i in range(2):
                for part in range(2):
                    hist[step, 1, j + i, part] = result[
                        part * dim : (part + 1) * dim, i * dim : (i + 1) * dim
                    ]

    def add_to(target, sources):
        total = target[...].astype(F32)
        for source in sources:
            total = total + source[...].astype(F32)
        target[...] = total.astype(BF16)

    def early_copy(step, kind, at, source, target, device):
        return remote(
            source, target, early_sent.at[step, kind], early_got.at[step, kind, at], device
        )

    def early_mate(step, turn):
        return early_copy(
            step,
            0,
            turn - 1,
            early.at[step, lax.rem(core + turn, pair)],
            early_core.at[step],
            mate_id(turn),
        )

    def early_along(step, right):
        a_column = lax.rem(column + right, width)
        return early_copy(
            step,
            1,
            right - 1,
            early.at[step, core, a_column],
            early_row.at[step, right - 1],
            chip_id(chip_at(0, right)),
        )

    def early_across(step, up):
        a_side = lax.rem(side + up, tall)
        return early_copy(
            step,
            2,
            up - 1,
            early.at[step, core, column, a_side],
            early_col.at[step, up - 1],
            chip_id(chip_at(up, 0)),
        )

    def early_level(step, other, sender):
        return remote(
            early.at[step, core, column, side, other],
            early_z.at[step, sender],
            early_sent.at[step, 3],
            early_z_got.at[step],
            level_id(other),
        )

    def early_start(step):
        for target in range(owners):
            a_node, a_spot = target // cores, target % cores
            early[step, a_node % pair, a_spot % width, a_node // pair, a_spot // width] = (
                jnp.concatenate(
                    [
                        terms[step * subs + sub, target * rows : (target + 1) * rows]
                        for sub in range(subs)
                    ],
                    axis=0,
                ).astype(BF16)
            )
        for turn in range(1, pair):
            early_mate(step, turn).start()

    def early_rows(step):
        for turn in range(1, pair):
            early_mate(step, turn).wait_recv()
            add_to(early.at[step, core], [early_core.at[step]])
        for right in range(1, width):
            early_along(step, right).start()

    def early_cols(step):
        for right in range(1, width):
            early_along(step, right).wait_recv()
        add_to(
            early.at[step, core, column],
            [early_row.at[step, right - 1] for right in range(1, width)],
        )
        for up in range(1, tall):
            early_across(step, up).start()

    def early_levels(step):
        for up in range(1, tall):
            early_across(step, up).wait_recv()
        add_to(
            early.at[step, core, column, side],
            [early_col.at[step, up - 1] for up in range(1, tall)],
        )

        def send(other):
            pl.when(other != level)(lambda: early_level(step, other, level).start())

        each(0, depth, send)

    def early_finish(step):
        early_z[step, level] = early[step, core, column, side, level]

        if depth > 1:
            passed = early_z.at[step, pl.ds(0, depth - 1)]
            pltpu.make_async_copy(passed, passed, early_z_got.at[step]).wait()
        total = early_z[step, 0].astype(F32)
        for other in range(1, depth):
            total = total + early_z[step, other].astype(F32)
        for sub in range(subs):
            for row in range(rows):
                at = sub * rows + row
                for part in range(2):
                    grad[row, step * subs + sub, part : part + 1, :] = total[
                        at : at + 1, part * dim : (part + 1) * dim
                    ]
        if pair > 1:
            pltpu.make_async_copy(
                early_core.at[step], early_core.at[step], early_sent.at[step, 0]
            ).wait()
        if width > 1:
            pltpu.make_async_copy(
                early_row.at[step], early_row.at[step], early_sent.at[step, 1]
            ).wait()
        if tall > 1:
            pltpu.make_async_copy(
                early_col.at[step], early_col.at[step], early_sent.at[step, 2]
            ).wait()
        if depth > 1:
            passed = early_z.at[step, pl.ds(0, depth - 1)]
            pltpu.make_async_copy(passed, passed, early_sent.at[step, 3]).wait()

    def join(step, state):
        def one(j, carry):
            lam = decay[j] * state[j, 0].astype(F32) + zout[step, level, j].astype(F32)
            hist[step, 0, j, 0] = lam.astype(BF16)
            total = rout[step, chip, j].astype(F32)
            lam = decay[j] * state[j, 1].astype(F32) - total
            hist[step, 0, j, 1] = lam.astype(BF16)
            return carry

        lax.fori_loop(0, count, one, 0)

    def fold(target, sources):
        for j in range(piece):
            total = target[j].astype(F32)
            for source in sources:
                total = total + source[j].astype(F32)
            target[j] = total.astype(BF16)

    def arrives(way, hop):
        return level >= hop if way == 0 else level + hop < depth

    def goes_on(way, hop):
        if way == 0:
            return jnp.logical_and(level >= hop - 1, level < depth - 1)
        return jnp.logical_and(level + hop - 1 < depth, level > 0)

    def take_line(step, hop, k, chosen=None):
        for way in range(2):
            due = arrives(way, hop)
            if chosen is not None:
                onward = goes_on(way, hop + 1)
                due = jnp.logical_and(due, onward if chosen else jnp.logical_not(onward))

            @pl.when(due)
            def _(way=way):
                a_level = level - hop if way == 0 else level + hop
                block = line_block(step, core, a_level, k)
                remote(
                    block,
                    block,
                    line_send.at[step],
                    line_recv.at[step, way, hop - 1, k],
                    level_id(level),
                ).wait_recv()
                if hop + 1 < depth:

                    @pl.when(goes_on(way, hop + 1))
                    def _():
                        line_copy(step, way, hop + 1, k, block).start()

                for turn in range(1, pair):
                    line_mate(step, a_level, turn, k, block).start()

    def take_first(step):
        def along(right):
            block, a_chip = near_got(step, 0, right, 0)
            each(
                1,
                tall,
                lambda up: near_copy(
                    step, up, right, 0, block, a_chip, chip_at(up, 0)
                ).start(),
            )

        def across(up):
            block, a_chip = near_got(step, up, 0, 1)
            each(
                1,
                width,
                lambda right: near_copy(
                    step, up, right, 1, block, a_chip, chip_at(0, right)
                ).start(),
            )

        each(1, width, along)
        each(1, tall, across)

    def take_second(step):
        each(1, width, lambda right: near_got(step, 0, right, 1) and None)
        each(1, tall, lambda up: near_got(step, up, 0, 0) and None)

    def take_far(step):
        def one(up):
            def two(right):
                for k in range(pieces):
                    near_got(step, up, right, k)

            each(1, width, two)

        each(1, tall, one)
        for turn in range(1, pair):

            passed = near[step].at[pl.ds(0, chips * count)]
            pltpu.make_async_copy(passed, passed, near_take.at[step]).wait()

    def mates_line(step):
        for turn in range(1, pair):

            passed = line[step].at[pl.ds(0, depth * count)]
            pltpu.make_async_copy(passed, passed, line_take.at[step]).wait()

    def reduce_start(step, lo, hi):
        def one(i, carry):
            a_level = jnp.where(level * 2 < depth, depth - 1 - i, i)

            def put(j, value):
                zout[step, a_level, j] = value

            for k in range(pieces):
                partial(near[step], a_level, k, put)

                @pl.when(jnp.logical_and(level == 0, a_level > 0))
                def _(k=k):
                    z_copy(step, 0, a_level, k).start()

                @pl.when(jnp.logical_and(level == depth - 1, a_level < depth - 1))
                def _(k=k):
                    z_copy(step, 1, a_level, k).start()

            return carry

        lax.fori_loop(lo, hi, one, 0)

    def exchange(step, lo, hi):
        def one(i):
            up, right = split(chips - 1 - i, width)
            target = chip_at(up, right)

            def put(j, value):
                rout[step, target, j] = value

            partial(line[step], depth + target, 0, put)

            @pl.when(right > 0)
            def _():
                row_copy(step, up, right).start()

            for k in range(1, pieces):
                partial(line[step], depth + target, k, put)

            @pl.when(up > 0)
            def _():
                col_copy(step, up, right).start()

        each(lo, hi, one)

    def exchange_on(step):
        def column(up):
            target = chip_at(up, 0)
            each(1, width, lambda right: row_copy(step, up, right).wait_recv())
            fold(
                rout.at[step, target, part(0)],
                [row_in.at[step, right - 1, up] for right in range(1, width)],
            )
            col_final(step, up).start()

        def line_of(right):
            target = chip_at(0, right)
            each(1, tall, lambda up: col_copy(step, up, right).wait_recv())
            fold(
                rout.at[step, target, part(1)],
                [col_in.at[step, up - 1, right] for up in range(1, tall)],
            )
            row_final(step, right).start()

        each(1, tall, column)
        each(1, width, line_of)

    def exchange_end(step):
        each(1, width, lambda right: row_copy(step, 0, right).wait_recv())
        each(1, tall, lambda up: col_copy(step, up, 0).wait_recv())
        each(1, tall, lambda up: col_final(step, up).wait_recv())
        each(1, width, lambda right: row_final(step, right).wait_recv())
        fold(
            rout.at[step, chip, part(0)],
            [row_in.at[step, right - 1, 0] for right in range(1, width)]
            + [col_end.at[step, up - 1] for up in range(1, tall)],
        )
        fold(
            rout.at[step, chip, part(1)],
            [col_in.at[step, up - 1, 0] for up in range(1, tall)]
            + [row_end.at[step, right - 1] for right in range(1, width)],
        )

    def reduce_on(step, ahead, some):
        for k in some:
            for way in range(2):
                if way == 0:
                    a_level = level + ahead
                    fits = jnp.logical_and(level > 0, a_level < depth)
                else:
                    a_level = level - ahead
                    fits = jnp.logical_and(level < depth - 1, a_level >= 0)

                @pl.when(fits)
                def _(way=way, k=k, a_level=a_level):
                    z_copy(step, way, a_level, k).wait_recv()
                    fold(
                        zout.at[step, a_level, part(k)], [zin.at[step, way, a_level, part(k)]]
                    )
                    if ahead > 0:
                        z_copy(step, way, a_level, k).start()

    pl.semaphore_wait(barrier, depth + chips + pair - 3)
    tables[0].wait()
    each_ladder(lambda copy: copy.start())
    for step in range(steps):
        state = adjoint if step == 0 else hist.at[step - 1, 1]
        for k in range(pieces):
            for way in range(2):

                @pl.when(goes_on(way, 1))
                def _(way=way, k=k):
                    line_copy(step, way, 1, k, state.at[part(k), 0]).start()

        def first(right, k, step=step, state=state):
            near_copy(step, 0, right, k, state.at[part(k), 1], chip, chip_at(0, right)).start()

        def other(up, k, step=step, state=state):
            near_copy(step, up, 0, k, state.at[part(k), 1], chip, chip_at(up, 0)).start()

        each(1, width, lambda right: first(right, 0))
        each(1, tall, lambda up: other(up, 1))
        each(1, width, lambda right: first(right, 1))
        each(1, tall, lambda up: other(up, 0))
        for k in range(pieces):
            for turn in range(1, pair):
                near_mate(step, chip, turn, k, state.at[part(k), 1]).start()
                line_mate(step, level, turn, k, state.at[part(k), 0]).start()
        keep_im = pltpu.make_async_copy(
            state.at[:, 1], near[step].at[pl.ds((chip * pair + core) * count, count)], local.at[2]
        )
        keep_re = pltpu.make_async_copy(
            state.at[:, 0], line[step].at[pl.ds((core * depth + level) * count, count)], local.at[3]
        )
        keep_im.start()
        keep_re.start()
        if step == 0:
            greet_levels(hello)
            for copy in tables[1:]:
                copy.wait()
            note_own()
        else:
            for sub in range(subs):
                turn_saved(step - 1, sub)
            for half in range(halves):
                project(step - 1, half * batch, (half + 1) * batch)
        if depth > 1:
            take_line(step, 1, 0)
        take_first(step)
        if step == 0:
            passed_ladders(ladder_recv)
            tabulate(True)
        else:
            early_start(step - 1)
        for k in range(1, pieces):
            if depth > 1:
                take_line(step, 1, k)
        take_second(step)
        if step == 0:
            pl.semaphore_wait(hello, depth - 1)
            greet_mates(again)
        else:
            early_rows(step - 1)
        keep_im.wait()
        keep_re.wait()
        take_far(step)
        reduce_start(step, 0, 1)
        if depth > 2:
            for k in range(pieces):
                take_line(step, 2, k, True)
        reduce_start(step, 1, depth)
        if step > 0:
            early_cols(step - 1)
        reduce_on(step, depth - 2, [0])
        if step == 0:
            tabulate(False)
            reduce_on(step, depth - 2, range(1, pieces))
        if depth > 2:
            for k in range(pieces):
                take_line(step, 2, k, False)
        for hop in range(3, depth):
            for k in range(pieces):
                take_line(step, hop, k)
        mates_line(step)
        exchange(step, 0, chips // 2)
        if step > 0:
            reduce_on(step, depth - 2, range(1, pieces))
        exchange(step, chips // 2, chips)
        if step > 0:
            early_levels(step - 1)
        for ahead in range(depth - 3, 0, -1):
            reduce_on(step, ahead, range(pieces))
        exchange_on(step)
        if step == 0:
            load_u.wait()
            prepare()
            fetch.wait()
        if step == steps - 1:
            for sub in range(subs):
                turn_saved(step, sub)
        if depth != 2:
            reduce_on(step, 0, range(pieces))
        exchange_end(step)
        if step == steps - 1:
            pl.semaphore_wait(again, pair - 1)
        if step == 0:
            load.wait()
        join(step, held if step == 0 else state)
        if step == steps - 1:
            for half in range(halves):
                project(step, half * batch, (half + 1) * batch)
                stage(half)
                spread(half)
        rotate(step)
    result = pltpu.make_async_copy(hist.at[steps - 1, 1], out, local.at[1])
    result.start()

    def sent(source, amount, semaphore):
        if amount > 0:
            passed = source.at[pl.ds(0, amount)]
            pltpu.make_async_copy(passed, passed, semaphore).wait()

    for step in range(steps):
        sent(near[step], (chips - 1) * count, near_send.at[step])
        sent(near[step], (pair - 1) * chips * count, near_pass.at[step])
        sent(line[step], (pair - 1) * depth * count, line_pass.at[step])
        crossings = (width - 1) * (tall + 1) + (tall - 1) * (width + 1)
        sent(near[step], crossings * piece, r_send.at[step])
        sent(zout.at[step], depth - 1, z_send.at[step])
        for a_level in range(depth):
            ups = a_level + 1 if a_level < depth - 1 else 0
            downs = depth - a_level if a_level > 0 else 0

            @pl.when(level == a_level)
            def _(step=step, blocks=ups + downs):
                sent(line[step], blocks * count, line_send.at[step])

    passed_ladders(ladder_send)
    result.wait()
    for step in range(steps - 1):
        early_finish(step)
    for half in range(halves):
        finish(half)


def deliver(state, grad, state_out, grad_out, state_kept, grad_kept, sems):
    into = [
        pltpu.make_async_copy(state, state_kept, sems.at[0]),
        pltpu.make_async_copy(grad, grad_kept, sems.at[1]),
    ]
    back = [
        pltpu.make_async_copy(state_kept, state_out, sems.at[2]),
        pltpu.make_async_copy(grad_kept, grad_out, sems.at[3]),
    ]
    for copy in into:
        copy.start()
    for arrival, leave in zip(into, back):
        arrival.wait()
        leave.start()
    for copy in back:
        copy.wait()


def body(adjoint, saved, propagators, coupling, higher, lower, ladder, rates, decay):
    nodes = lax.axis_size("node")
    cores = lax.axis_size("cores")
    owners = nodes * cores
    count = adjoint.shape[0]
    modes = higher.shape[1]
    steps, subs = propagators.shape[:2]
    dim = coupling.shape[0]
    depth = 1 << (cores.bit_length() // 2)
    width = cores // depth
    pair = 2 if nodes % 2 == 0 else 1
    chips = nodes // pair * width
    pieces = 2
    rows = dim // owners
    halves = 2 if subs % 2 == 0 else 1
    batch = subs // halves
    higher, lower, ladder = higher.T, lower.T, jnp.swapaxes(ladder, 1, 2)
    vmem = pl.BlockSpec(memory_space=pltpu.VMEM)
    block = adjoint.shape
    hbm = pl.BlockSpec(memory_space=pl.ANY)
    hops = max(depth - 1, 1)
    others = max(chips - 1, 1)
    mates = max(pair - 1, 1)
    half = (count,) + block[2:]
    bit = (count // pieces,) + block[2:]
    tall = nodes // pair
    before = max(steps - 1, 1)
    slab = (subs * rows, 2 * dim)
    table = (depth + chips) * count * 2 * modes
    dma = pltpu.SemaphoreType.DMA
    state, grad = pl.pallas_call(
        functools.partial(kernel, (nodes, depth, width, pair, count, modes, steps, subs, dim, halves, pieces)),
        out_shape=(
            jax.ShapeDtypeStruct(block, BF16),
            jax.ShapeDtypeStruct((rows, steps * subs, 2, dim), F32),
        ),
        in_specs=[hbm] * 9,
        out_specs=(hbm, vmem),
        scratch_shapes=[
            pltpu.VMEM((steps * subs, 2 * dim, 2 * dim), BF16),
            pltpu.VMEM((steps * subs, 2 * dim, 2 * dim), BF16),
            pltpu.VMEM((steps, 2) + block, BF16),
            pltpu.VMEM((steps, depth) + half, BF16),
            pltpu.VMEM((steps, 2, depth) + half, BF16),
            pltpu.VMEM((steps, chips) + half, BF16),
            pltpu.VMEM((steps, max(width - 1, 1), tall) + bit, BF16),
            pltpu.VMEM((steps, max(tall - 1, 1), width) + bit, BF16),
            pltpu.VMEM((steps, max(width - 1, 1)) + bit, BF16),
            pltpu.VMEM((steps, max(tall - 1, 1)) + bit, BF16),
            pltpu.VMEM((steps * subs, dim, 2 * dim), F32),
            pltpu.VMEM((halves, owners, batch * rows, 2 * dim), BF16),
            pltpu.VMEM((halves, owners - 1, batch * rows, 2 * dim), BF16),
            pltpu.VMEM(saved.shape, BF16),
            pltpu.VMEM((steps, subs, 2 * dim, count * dim), BF16),
            pltpu.SMEM((table,), jnp.int32),
            pltpu.SMEM((table,), F32),
            pltpu.SMEM((2, owners), jnp.int32),
            pltpu.SMEM((2, owners), F32),
            pltpu.SMEM((depth + chips, 2, modes, count), jnp.int32),
            dma((steps,)),
            dma((steps, others, pieces)),
            dma((steps,)),
            dma((steps,)),
            dma((steps,)),
            dma((steps, 2, hops, pieces)),
            dma((steps,)),
            dma((steps,)),
            dma((steps,)),
            dma((steps, 2, depth, pieces)),
            dma((steps,)),
            dma((steps, max(width - 1, 1), tall)),
            dma((steps, max(tall - 1, 1), width)),
            dma((steps, max(width - 1, 1))),
            dma((steps, max(tall - 1, 1))),
            dma(()),
            dma(()),
            dma((halves,)),
            dma((halves,)),
            pltpu.SemaphoreType.REGULAR,
            pltpu.SemaphoreType.REGULAR,
            dma((6,)),
            pltpu.VMEM(propagators.shape, BF16),
            pltpu.VMEM(block, BF16),
            pltpu.VMEM(coupling.shape, BF16),
            pltpu.SMEM(higher.shape, jnp.int32),
            pltpu.SMEM(lower.shape, jnp.int32),
            pltpu.SMEM(ladder.shape, jnp.int32),
            pltpu.SMEM(rates.shape, F32),
            pltpu.SMEM(decay.shape, F32),
            dma((6,)),
            pltpu.VMEM((before, pair, width, tall, depth) + slab, BF16),
            pltpu.VMEM((before, width, tall, depth) + slab, BF16),
            pltpu.VMEM((before, max(width - 1, 1), tall, depth) + slab, BF16),
            pltpu.VMEM((before, max(tall - 1, 1), depth) + slab, BF16),
            pltpu.VMEM((before, depth) + slab, BF16),
            dma((before, 4)),
            dma((before, 3, max(width - 1, tall - 1, 1))),
            dma((before,)),
            *[pltpu.VMEM((chips * pair * count, dim, dim), BF16)] * steps,
            *[pltpu.VMEM((depth * pair * count, dim, dim), BF16)] * steps,
        ],
        compiler_params=pltpu.CompilerParams(
            collective_id=0, has_side_effects=True, vmem_limit_bytes=63_000_000
        ),
    )(higher, lower, ladder, rates, decay, adjoint, saved, propagators, coupling)
    return pl.pallas_call(
        deliver,
        out_shape=(
            jax.ShapeDtypeStruct(state.shape, state.dtype),
            jax.ShapeDtypeStruct(grad.shape, grad.dtype),
        ),
        in_specs=[hbm, hbm],
        out_specs=(hbm, hbm),
        scratch_shapes=[
            pltpu.VMEM(state.shape, state.dtype),
            pltpu.VMEM(grad.shape, grad.dtype),
            dma((4,)),
        ],
    )(state, grad)


def solution(mesh):
    return jax.shard_map(
        body,
        mesh=mesh,
        in_specs=(
            P(("node", "cores"), None, None, None),
            P(None, None, ("node", "cores"), None, None, None),
            P(),
            P(),
            P(),
            P(),
            P(None, ("node", "cores"), None),
            P(),
            P(("node", "cores")),
        ),
        out_specs=(P(("node", "cores"), None, None, None), P(("node", "cores"), None, None, None)),
        check_vma=False,
    )
```

```python
import functools

import jax
import jax.numpy as jnp
from jax import lax
from jax.experimental import pallas as pl
from jax.experimental.pallas import tpu as pltpu
from jax.sharding import PartitionSpec as P

MESH = pl.DeviceIdType.MESH
F32 = jnp.float32
BF16 = jnp.bfloat16


def dot(a, b):
    return jnp.dot(a, b, preferred_element_type=F32)


def kernel(
    dims,
    higher_in,
    lower_in,
    ladder_in,
    rates_in,
    decay_in,
    adjoint,
    saved_in,
    propagators_in,
    coupling_in,
    out,
    grad,
    right_u,
    left_u,
    hist,
    zout,
    zin,
    rout,
    row_in,
    col_in,
    row_end,
    col_end,
    terms,
    term_stage,
    term_inbox,
    saved,
    saved_t,
    place,
    weight,
    home,
    inside,
    ladders,
    near_send,
    near_recv,
    near_pass,
    near_take,
    line_send,
    line_recv,
    line_pass,
    line_take,
    z_send,
    z_recv,
    r_send,
    row_recv,
    col_recv,
    row_done,
    col_done,
    ladder_send,
    ladder_recv,
    term_send,
    term_recv,
    hello,
    again,
    local,
    propagators,
    held,
    coupling,
    higher,
    lower,
    ladder,
    rates,
    decay,
    table_sem,
    early,
    early_core,
    early_row,
    early_col,
    early_z,
    early_sent,
    early_got,
    early_z_got,
    *gathered,
):
    nodes, depth, width, pair, count, modes, steps, subs, dim, halves, pieces = dims
    near, line = gathered[:steps], gathered[steps:]
    cores = depth * width
    owners = nodes * cores
    tall = nodes // pair
    chips = tall * width
    rows = dim // owners
    batch = subs // halves
    piece = count // pieces
    slots = 2 * modes
    node = lax.axis_index("node")
    spot = lax.axis_index("cores")
    level = spot // width
    column = spot % width
    side = node // pair
    core = node % pair
    chip = side * width + column

    def split(value, size):
        if size & (size - 1) == 0:
            return value >> (size.bit_length() - 1), value & (size - 1)
        return lax.div(value, size), lax.rem(value, size)

    def chip_id(other):
        return ((other // width) * pair + core, level * width + other % width)

    def chip_at(up, right):
        return lax.rem(side + up + tall, tall) * width + lax.rem(column + right + width, width)

    def mate_id(turn):
        return (side * pair + lax.rem(core + turn, pair), spot)

    def level_id(other):
        return (node, other * width + column)

    barrier = pltpu.get_barrier_semaphore()

    own = node * cores + spot

    def owner_id(offset):
        return split(split(own + offset, owners)[1], cores)

    def each(lo, hi, act):
        def one(i, carry):
            act(i)
            return carry

        lax.fori_loop(lo, hi, one, 0)

    def signal(semaphore, device):
        pl.semaphore_signal(semaphore, inc=1, device_id=device, device_id_type=MESH)

    def greet_levels(semaphore):
        def greet(other):
            pl.when(other != level)(lambda: signal(semaphore, level_id(other)))

        each(0, depth, greet)

    def greet_mates(semaphore):
        for turn in range(1, pair):
            signal(semaphore, mate_id(turn))

    def greet_chips(semaphore):
        def greet(other):
            pl.when(other != chip)(lambda: signal(semaphore, chip_id(other)))

        each(0, chips, greet)

    greet_levels(barrier)
    greet_chips(barrier)
    greet_mates(barrier)
    tables = [
        pltpu.make_async_copy(source, target, table_sem.at[at])
        for at, (source, target) in enumerate(
            (
                (ladder_in, ladder),
                (higher_in, higher),
                (lower_in, lower),
                (rates_in, rates),
                (decay_in, decay),
                (coupling_in, coupling),
            )
        )
    ]
    for copy in tables:
        copy.start()
    load_u = pltpu.make_async_copy(propagators_in, propagators, local.at[4])
    load_u.start()
    load = pltpu.make_async_copy(adjoint, held, local.at[5])
    load.start()
    fetch = pltpu.make_async_copy(saved_in, saved, local.at[0])
    fetch.start()

    def remote(source, target, sent, arrived, device):
        return pltpu.make_async_remote_copy(
            src_ref=source,
            dst_ref=target,
            send_sem=sent,
            recv_sem=arrived,
            device_id=device,
            device_id_type=MESH,
        )

    def part(k):
        return pl.ds(k * piece, piece)

    def near_block(step, a_chip, a_core, k):
        return near[step].at[pl.ds((a_chip * pair + a_core) * count + k * piece, piece)]

    def line_block(step, a_core, a_level, k):
        return line[step].at[pl.ds((a_core * depth + a_level) * count + k * piece, piece)]

    def near_copy(step, up, right, k, source, a_chip, target):
        at = up * width + right - 1
        return remote(
            source,
            near_block(step, a_chip, core, k),
            near_send.at[step],
            near_recv.at[step, at, k],
            chip_id(target),
        )

    def near_got(step, up, right, k):
        a_chip = chip_at(-up, -right)
        block = near_block(step, a_chip, core, k)
        near_copy(step, up, right, k, block, a_chip, a_chip).wait_recv()
        for turn in range(1, pair):
            near_mate(step, a_chip, turn, k, block).start()
        return block, a_chip

    def near_mate(step, a_chip, turn, k, source):
        return remote(
            source,
            near_block(step, a_chip, core, k),
            near_pass.at[step],
            near_take.at[step],
            mate_id(turn),
        )

    def line_copy(step, way, hop, k, source):
        a_level = level - (hop - 1) if way == 0 else level + (hop - 1)
        return remote(
            source,
            line_block(step, core, a_level, k),
            line_send.at[step],
            line_recv.at[step, a_level, k],
            level_id(level + 1 if way == 0 else level - 1),
        )

    def line_mate(step, a_level, turn, k, source):
        return remote(
            source,
            line_block(step, core, a_level, k),
            line_pass.at[step],
            line_take.at[step],
            mate_id(turn),
        )

    def z_copy(step, way, a_level, k):
        return remote(
            zout.at[step, a_level, pl.ds(k * piece, piece)],
            zin.at[step, way, a_level, pl.ds(k * piece, piece)],
            z_send.at[step],
            z_recv.at[step, a_level + (1 - way), k],
            level_id(level + 1 if way == 0 else level - 1),
        )

    def row_copy(step, up, right):
        return remote(
            rout.at[step, chip_at(up, right), part(0)],
            row_in.at[step, right - 1, up],
            r_send.at[step],
            row_recv.at[step, right - 1, up],
            chip_id(chip_at(0, right)),
        )

    def col_copy(step, up, right):
        return remote(
            rout.at[step, chip_at(up, right), part(1)],
            col_in.at[step, up - 1, right],
            r_send.at[step],
            col_recv.at[step, up - 1, right],
            chip_id(chip_at(up, 0)),
        )

    def col_final(step, up):
        return remote(
            rout.at[step, chip_at(up, 0), part(0)],
            col_end.at[step, up - 1],
            r_send.at[step],
            col_done.at[step, up - 1],
            chip_id(chip_at(up, 0)),
        )

    def row_final(step, right):
        return remote(
            rout.at[step, chip_at(0, right), part(1)],
            row_end.at[step, right - 1],
            r_send.at[step],
            row_done.at[step, right - 1],
            chip_id(chip_at(0, right)),
        )

    def ladder_level(other):
        return remote(
            ladder, ladders.at[level], ladder_send, ladder_recv, level_id(other)
        )

    def ladder_chip(other):
        return remote(
            ladder,
            ladders.at[depth + chip],
            ladder_send,
            ladder_recv,
            chip_id(other),
        )

    def each_ladder(act):
        def one_level(other, carry):
            @pl.when(other != level)
            def _():
                act(ladder_level(other))

            return carry

        def one_chip(other, carry):
            @pl.when(other != chip)
            def _():
                act(ladder_chip(other))

            return carry

        lax.fori_loop(0, depth, one_level, 0)
        lax.fori_loop(0, chips, one_chip, 0)

    def passed_ladders(semaphore):
        if depth + chips > 2:
            passed = ladders.at[pl.ds(0, depth + chips - 2)]
            pltpu.make_async_copy(passed, passed, semaphore).wait()

    def note_own():
        for way in range(2):
            for mode in range(modes):
                for j in range(count):
                    value = ladder[way, mode, j]
                    ladders[level, way, mode, j] = value
                    ladders[depth + chip, way, mode, j] = value

        def locate(owner, carry):
            a_node, a_spot = split(owner, cores)
            a_level, a_column = split(a_spot, width)
            a_side, a_core = split(a_node, pair)
            home[0, owner] = ((a_side * width + a_column) * pair + a_core) * count
            home[1, owner] = (a_core * depth + a_level) * count
            inside[0, owner] = jnp.where(a_level == level, 1.0, 0.0)
            beside = jnp.logical_and(a_side == side, a_column == column)
            inside[1, owner] = jnp.where(beside, 1.0, 0.0)
            return carry

        lax.fori_loop(0, owners, locate, 0)

    def tabulate(along_z):
        def entry(at):
            index, j = split(at, count)
            if along_z:
                target, kind, row = node * cores + index * width + column, 0, index
            else:
                a_side, a_column = split(index, width)
                target = (a_side * pair + core) * cores + level * width + a_column
                kind, row = 1, depth + index
            for way in range(2):
                for mode in range(modes):
                    source, member = split((higher, lower)[way][mode, target * count + j], count)
                    value = ladders[row, way, mode, j].astype(F32) * rates[way, mode]
                    slot = (row * count + j) * slots + way * modes + mode
                    place[slot] = home[kind, source] + member
                    weight[slot] = inside[kind, source] * value

        each(0, (depth if along_z else chips) * count, entry)

    def partial(blocks, row, k, put):
        operator = coupling[...]

        def some(pick, carry):
            plus, minus = [], []
            for i in range(2):
                sums = []
                for way in range(2):
                    total = None
                    for mode in range(modes):
                        at = (row * count + pick * 2 + i) * slots + way * modes + mode
                        scale = jnp.full((16, dim), weight[at], F32).astype(BF16)
                        term = blocks[place[at]].reshape(dim // 16, 16, dim) * scale
                        total = term if total is None else total + term
                    sums.append(total.reshape(dim, dim))
                plus.append(sums[0] + sums[1])
                minus.append(sums[0] - sums[1])
            left = dot(operator, jnp.concatenate(plus, axis=1))
            right = dot(jnp.concatenate(minus, axis=0), operator)
            for i in range(2):
                value = left[:, i * dim : (i + 1) * dim] - right[i * dim : (i + 1) * dim]
                put(pick * 2 + i, value.astype(BF16))
            return carry

        lax.fori_loop(k * piece // 2, (k + 1) * piece // 2, some, 0)

    def prepare():
        def one(at, carry):
            step, sub = at // subs, at % subs
            u_re = propagators[step, sub, 0]
            u_im = propagators[step, sub, 1]
            right_u[at, :dim, :dim] = u_re
            right_u[at, :dim, dim:] = u_im
            right_u[at, dim:, :dim] = -u_im
            right_u[at, dim:, dim:] = u_re
            t_re = u_re.T
            t_im = u_im.T
            left_u[at, :dim, :dim] = t_re
            left_u[at, :dim, dim:] = t_im
            left_u[at, dim:, :dim] = -t_im
            left_u[at, dim:, dim:] = t_re
            return carry

        lax.fori_loop(0, steps * subs, one, 0)

        def accumulate(sub):
            for step in range(steps):
                at = step * subs + sub
                right_u[at] = dot(right_u[at - 1], right_u[at]).astype(BF16)
                left_u[at] = dot(left_u[at], left_u[at - 1]).astype(BF16)

        each(1, subs, accumulate)

    def turn_saved(step, sub):
        flat = jnp.concatenate(
            [
                jnp.concatenate([saved[step, sub, j, part].T for part in range(2)], axis=1)
                for j in range(count)
            ],
            axis=0,
        )
        turned = dot(flat, left_u[step * subs + sub]).astype(BF16)
        for j in range(count):
            for part in range(2):
                saved_t[step, sub, part * dim : (part + 1) * dim, j * dim : (j + 1) * dim] = turned[
                    j * dim : (j + 1) * dim, part * dim : (part + 1) * dim
                ]

    def flatten(step):
        return jnp.concatenate(
            [
                jnp.concatenate([hist[step, 0, j, part] for part in range(2)], axis=1)
                for j in range(count)
            ],
            axis=0,
        )

    def project(step, lo, hi):
        total = dot(
            saved_t[step, lo:hi].reshape((hi - lo) * 2 * dim, count * dim), flatten(step)
        )
        for sub in range(lo, hi):
            at = step * subs + sub
            top = total[(sub - lo) * 2 * dim : (sub - lo) * 2 * dim + dim]
            low = total[(sub - lo) * 2 * dim + dim : (sub - lo + 1) * 2 * dim]
            re = top[:, :dim] + low[:, dim:]
            im = top[:, dim:] - low[:, :dim]
            terms[at] = dot(jnp.concatenate([re, im], axis=1).astype(BF16), right_u[at])

    def stage(group):
        for target in range(owners):
            term_stage[group, target] = jnp.concatenate(
                [
                    terms[(steps - 1) * subs + group * batch + i, target * rows : (target + 1) * rows]
                    for i in range(batch)
                ],
                axis=0,
            ).astype(BF16)

    def spread(group):
        def send(offset, carry):
            pltpu.make_async_remote_copy(
                src_ref=term_stage.at[group, split(own + offset, owners)[1]],
                dst_ref=term_inbox.at[group, offset - 1],
                send_sem=term_send.at[group],
                recv_sem=term_recv.at[group],
                device_id=owner_id(offset),
                device_id_type=MESH,
            ).start()
            return carry

        lax.fori_loop(1, owners, send, 0)

    def finish(group):
        everything = term_inbox.at[group]
        pltpu.make_async_copy(everything, everything, term_recv.at[group]).wait()
        total = term_stage[group, own].astype(F32)
        for offset in range(1, owners):
            total = total + term_inbox[group, offset - 1].astype(F32)
        for i in range(batch):
            for row in range(rows):
                for part in range(2):
                    grad[row, (steps - 1) * subs + group * batch + i, part : part + 1, :] = total[
                        i * rows + row : i * rows + row + 1, part * dim : (part + 1) * dim
                    ]
        pltpu.make_async_copy(everything, everything, term_send.at[group]).wait()

    def rotate(step):
        at = step * subs + subs - 1
        mult_l = left_u[at]
        middles = dot(flatten(step), right_u[at]).astype(BF16)
        for j in range(0, count, 2):
            middle = middles[j * dim : (j + 2) * dim]
            stacked = jnp.concatenate(
                [
                    jnp.concatenate([middle[:dim, :dim], middle[dim:, :dim]], axis=1),
                    jnp.concatenate([middle[:dim, dim:], middle[dim:, dim:]], axis=1),
                ],
                axis=0,
            )
            result = dot(mult_l, stacked).astype(BF16)
            for i in range(2):
                for part in range(2):
                    hist[step, 1, j + i, part] = result[
                        part * dim : (part + 1) * dim, i * dim : (i + 1) * dim
                    ]

    def add_to(target, sources):
        total = target[...].astype(F32)
        for source in sources:
            total = total + source[...].astype(F32)
        target[...] = total.astype(BF16)

    def early_copy(step, kind, at, source, target, device):
        return remote(
            source, target, early_sent.at[step, kind], early_got.at[step, kind, at], device
        )

    def early_mate(step, turn):
        return early_copy(
            step,
            0,
            turn - 1,
            early.at[step, lax.rem(core + turn, pair)],
            early_core.at[step],
            mate_id(turn),
        )

    def early_along(step, right):
        a_column = lax.rem(column + right, width)
        return early_copy(
            step,
            1,
            right - 1,
            early.at[step, core, a_column],
            early_row.at[step, right - 1],
            chip_id(chip_at(0, right)),
        )

    def early_across(step, up):
        a_side = lax.rem(side + up, tall)
        return early_copy(
            step,
            2,
            up - 1,
            early.at[step, core, column, a_side],
            early_col.at[step, up - 1],
            chip_id(chip_at(up, 0)),
        )

    def early_level(step, other, sender):
        return remote(
            early.at[step, core, column, side, other],
            early_z.at[step, sender],
            early_sent.at[step, 3],
            early_z_got.at[step],
            level_id(other),
        )

    def early_start(step):
        for target in range(owners):
            a_node, a_spot = target // cores, target % cores
            early[step, a_node % pair, a_spot % width, a_node // pair, a_spot // width] = (
                jnp.concatenate(
                    [
                        terms[step * subs + sub, target * rows : (target + 1) * rows]
                        for sub in range(subs)
                    ],
                    axis=0,
                ).astype(BF16)
            )
        for turn in range(1, pair):
            early_mate(step, turn).start()

    def early_rows(step):
        for turn in range(1, pair):
            early_mate(step, turn).wait_recv()
            add_to(early.at[step, core], [early_core.at[step]])
        for right in range(1, width):
            early_along(step, right).start()

    def early_cols(step):
        for right in range(1, width):
            early_along(step, right).wait_recv()
        add_to(
            early.at[step, core, column],
            [early_row.at[step, right - 1] for right in range(1, width)],
        )
        for up in range(1, tall):
            early_across(step, up).start()

    def early_levels(step):
        for up in range(1, tall):
            early_across(step, up).wait_recv()
        add_to(
            early.at[step, core, column, side],
            [early_col.at[step, up - 1] for up in range(1, tall)],
        )

        def send(other):
            pl.when(other != level)(lambda: early_level(step, other, level).start())

        each(0, depth, send)

    def early_finish(step):
        early_z[step, level] = early[step, core, column, side, level]

        if depth > 1:
            passed = early_z.at[step, pl.ds(0, depth - 1)]
            pltpu.make_async_copy(passed, passed, early_z_got.at[step]).wait()
        total = early_z[step, 0].astype(F32)
        for other in range(1, depth):
            total = total + early_z[step, other].astype(F32)
        for sub in range(subs):
            for row in range(rows):
                at = sub * rows + row
                for part in range(2):
                    grad[row, step * subs + sub, part : part + 1, :] = total[
                        at : at + 1, part * dim : (part + 1) * dim
                    ]
        if pair > 1:
            pltpu.make_async_copy(
                early_core.at[step], early_core.at[step], early_sent.at[step, 0]
            ).wait()
        if width > 1:
            pltpu.make_async_copy(
                early_row.at[step], early_row.at[step], early_sent.at[step, 1]
            ).wait()
        if tall > 1:
            pltpu.make_async_copy(
                early_col.at[step], early_col.at[step], early_sent.at[step, 2]
            ).wait()
        if depth > 1:
            passed = early_z.at[step, pl.ds(0, depth - 1)]
            pltpu.make_async_copy(passed, passed, early_sent.at[step, 3]).wait()

    def join(step, state):
        def one(j, carry):
            lam = decay[j] * state[j, 0].astype(F32) + zout[step, level, j].astype(F32)
            hist[step, 0, j, 0] = lam.astype(BF16)
            total = rout[step, chip, j].astype(F32)
            lam = decay[j] * state[j, 1].astype(F32) - total
            hist[step, 0, j, 1] = lam.astype(BF16)
            return carry

        lax.fori_loop(0, count, one, 0)

    def fold(target, sources):
        for j in range(piece):
            total = target[j].astype(F32)
            for source in sources:
                total = total + source[j].astype(F32)
            target[j] = total.astype(BF16)

    def arrives(way, hop):
        return level >= hop if way == 0 else level + hop < depth

    def goes_on(way, hop):
        if way == 0:
            return jnp.logical_and(level >= hop - 1, level < depth - 1)
        return jnp.logical_and(level + hop - 1 < depth, level > 0)

    def take_line(step, hop, k, chosen=None):
        for way in range(2):
            due = arrives(way, hop)
            if chosen is not None:
                onward = goes_on(way, hop + 1)
                due = jnp.logical_and(due, onward if chosen else jnp.logical_not(onward))

            @pl.when(due)
            def _(way=way):
                a_level = level - hop if way == 0 else level + hop
                block = line_block(step, core, a_level, k)
                remote(
                    block,
                    block,
                    line_send.at[step],
                    line_recv.at[step, a_level, k],
                    level_id(level),
                ).wait_recv()
                if hop + 1 < depth:

                    @pl.when(goes_on(way, hop + 1))
                    def _():
                        line_copy(step, way, hop + 1, k, block).start()

                for turn in range(1, pair):
                    line_mate(step, a_level, turn, k, block).start()

    def take_first(step):
        def along(right):
            block, a_chip = near_got(step, 0, right, 0)
            each(
                1,
                tall,
                lambda up: near_copy(
                    step, up, right, 0, block, a_chip, chip_at(up, 0)
                ).start(),
            )

        def across(up):
            block, a_chip = near_got(step, up, 0, 1)
            each(
                1,
                width,
                lambda right: near_copy(
                    step, up, right, 1, block, a_chip, chip_at(0, right)
                ).start(),
            )

        each(1, width, along)
        each(1, tall, across)

    def take_second(step):
        each(1, width, lambda right: near_got(step, 0, right, 1) and None)
        each(1, tall, lambda up: near_got(step, up, 0, 0) and None)

    def take_far(step):
        def one(up):
            def two(right):
                for k in range(pieces):
                    near_got(step, up, right, k)

            each(1, width, two)

        each(1, tall, one)
        for turn in range(1, pair):

            passed = near[step].at[pl.ds(0, chips * count)]
            pltpu.make_async_copy(passed, passed, near_take.at[step]).wait()

    def mates_line(step):
        for turn in range(1, pair):

            passed = line[step].at[pl.ds(0, depth * count)]
            pltpu.make_async_copy(passed, passed, line_take.at[step]).wait()

    def reduce_start(step, lo, hi):
        def one(i, carry):
            a_level = jnp.where(level * 2 < depth, depth - 1 - i, i)

            def put(j, value):
                zout[step, a_level, j] = value

            for k in range(pieces):
                partial(near[step], a_level, k, put)

                @pl.when(jnp.logical_and(level == 0, a_level > 0))
                def _(k=k):
                    z_copy(step, 0, a_level, k).start()

                @pl.when(jnp.logical_and(level == depth - 1, a_level < depth - 1))
                def _(k=k):
                    z_copy(step, 1, a_level, k).start()

            return carry

        lax.fori_loop(lo, hi, one, 0)

    def exchange(step, lo, hi):
        def one(i):
            up, right = split(chips - 1 - i, width)
            target = chip_at(up, right)

            def put(j, value):
                rout[step, target, j] = value

            partial(line[step], depth + target, 0, put)

            @pl.when(right > 0)
            def _():
                row_copy(step, up, right).start()

            for k in range(1, pieces):
                partial(line[step], depth + target, k, put)

            @pl.when(up > 0)
            def _():
                col_copy(step, up, right).start()

        each(lo, hi, one)

    def exchange_on(step):
        def column(up):
            target = chip_at(up, 0)
            each(1, width, lambda right: row_copy(step, up, right).wait_recv())
            fold(
                rout.at[step, target, part(0)],
                [row_in.at[step, right - 1, up] for right in range(1, width)],
            )
            col_final(step, up).start()

        def line_of(right):
            target = chip_at(0, right)
            each(1, tall, lambda up: col_copy(step, up, right).wait_recv())
            fold(
                rout.at[step, target, part(1)],
                [col_in.at[step, up - 1, right] for up in range(1, tall)],
            )
            row_final(step, right).start()

        each(1, tall, column)
        each(1, width, line_of)

    def exchange_end(step):
        each(1, width, lambda right: row_copy(step, 0, right).wait_recv())
        each(1, tall, lambda up: col_copy(step, up, 0).wait_recv())
        each(1, tall, lambda up: col_final(step, up).wait_recv())
        each(1, width, lambda right: row_final(step, right).wait_recv())
        fold(
            rout.at[step, chip, part(0)],
            [row_in.at[step, right - 1, 0] for right in range(1, width)]
            + [col_end.at[step, up - 1] for up in range(1, tall)],
        )
        fold(
            rout.at[step, chip, part(1)],
            [col_in.at[step, up - 1, 0] for up in range(1, tall)]
            + [row_end.at[step, right - 1] for right in range(1, width)],
        )

    def reduce_on(step, ahead, some):
        for k in some:
            for way in range(2):
                if way == 0:
                    a_level = level + ahead
                    fits = jnp.logical_and(level > 0, a_level < depth)
                else:
                    a_level = level - ahead
                    fits = jnp.logical_and(level < depth - 1, a_level >= 0)

                @pl.when(fits)
                def _(way=way, k=k, a_level=a_level):
                    z_copy(step, way, a_level, k).wait_recv()
                    fold(
                        zout.at[step, a_level, part(k)], [zin.at[step, way, a_level, part(k)]]
                    )
                    if ahead > 0:
                        z_copy(step, way, a_level, k).start()

    pl.semaphore_wait(barrier, depth + chips + pair - 3)
    tables[0].wait()
    each_ladder(lambda copy: copy.start())
    for step in range(steps):
        state = adjoint if step == 0 else hist.at[step - 1, 1]
        for k in range(pieces):
            for way in range(2):

                @pl.when(goes_on(way, 1))
                def _(way=way, k=k):
                    line_copy(step, way, 1, k, state.at[part(k), 0]).start()

        def first(right, k, step=step, state=state):
            near_copy(step, 0, right, k, state.at[part(k), 1], chip, chip_at(0, right)).start()

        def other(up, k, step=step, state=state):
            near_copy(step, up, 0, k, state.at[part(k), 1], chip, chip_at(up, 0)).start()

        each(1, width, lambda right: first(right, 0))
        each(1, tall, lambda up: other(up, 1))
        each(1, width, lambda right: first(right, 1))
        each(1, tall, lambda up: other(up, 0))
        for k in range(pieces):
            for turn in range(1, pair):
                near_mate(step, chip, turn, k, state.at[part(k), 1]).start()
                line_mate(step, level, turn, k, state.at[part(k), 0]).start()
        keep_im = pltpu.make_async_copy(
            state.at[:, 1], near[step].at[pl.ds((chip * pair + core) * count, count)], local.at[2]
        )
        keep_re = pltpu.make_async_copy(
            state.at[:, 0], line[step].at[pl.ds((core * depth + level) * count, count)], local.at[3]
        )
        keep_im.start()
        keep_re.start()
        if step == 0:
            greet_levels(hello)
            for copy in tables[1:]:
                copy.wait()
            note_own()
        else:
            for sub in range(subs):
                turn_saved(step - 1, sub)
            for half in range(halves):
                project(step - 1, half * batch, (half + 1) * batch)
        if depth > 1:
            take_line(step, 1, 0)
        take_first(step)
        if step == 0:
            passed_ladders(ladder_recv)
            tabulate(True)
        else:
            early_start(step - 1)
        for k in range(1, pieces):
            if depth > 1:
                take_line(step, 1, k)
        take_second(step)
        if step == 0:
            pl.semaphore_wait(hello, depth - 1)
            greet_mates(again)
        else:
            early_rows(step - 1)
        keep_im.wait()
        keep_re.wait()
        take_far(step)
        reduce_start(step, 0, 1)
        if depth > 2:
            for k in range(pieces):
                take_line(step, 2, k, True)
        reduce_start(step, 1, depth)
        if step > 0:
            early_cols(step - 1)
        reduce_on(step, depth - 2, [0])
        if step == 0:
            tabulate(False)
            reduce_on(step, depth - 2, range(1, pieces))
        if depth > 2:
            for k in range(pieces):
                take_line(step, 2, k, False)
        for hop in range(3, depth):
            for k in range(pieces):
                take_line(step, hop, k)
        mates_line(step)
        exchange(step, 0, chips // 2)
        if step > 0:
            reduce_on(step, depth - 2, range(1, pieces))
        exchange(step, chips // 2, chips)
        if step > 0:
            early_levels(step - 1)
        for ahead in range(depth - 3, 0, -1):
            reduce_on(step, ahead, range(pieces))
        exchange_on(step)
        if step == 0:
            load_u.wait()
            prepare()
            fetch.wait()
        if step == steps - 1:
            for sub in range(subs):
                turn_saved(step, sub)
        if depth != 2:
            reduce_on(step, 0, range(pieces))
        exchange_end(step)
        if step == steps - 1:
            pl.semaphore_wait(again, pair - 1)
        if step == 0:
            load.wait()
        join(step, held if step == 0 else state)
        if step == steps - 1:
            for half in range(halves):
                project(step, half * batch, (half + 1) * batch)
                stage(half)
                spread(half)
        rotate(step)
    result = pltpu.make_async_copy(hist.at[steps - 1, 1], out, local.at[1])
    result.start()

    def sent(source, amount, semaphore):
        if amount > 0:
            passed = source.at[pl.ds(0, amount)]
            pltpu.make_async_copy(passed, passed, semaphore).wait()

    for step in range(steps):
        sent(near[step], (chips - 1) * count, near_send.at[step])
        sent(near[step], (pair - 1) * chips * count, near_pass.at[step])
        sent(line[step], (pair - 1) * depth * count, line_pass.at[step])
        crossings = (width - 1) * (tall + 1) + (tall - 1) * (width + 1)
        sent(near[step], crossings * piece, r_send.at[step])
        sent(zout.at[step], depth - 1, z_send.at[step])
        for a_level in range(depth):
            ups = a_level + 1 if a_level < depth - 1 else 0
            downs = depth - a_level if a_level > 0 else 0

            @pl.when(level == a_level)
            def _(step=step, blocks=ups + downs):
                sent(line[step], blocks * count, line_send.at[step])

    passed_ladders(ladder_send)
    result.wait()
    for step in range(steps - 1):
        early_finish(step)
    for half in range(halves):
        finish(half)


def deliver(state, grad, state_out, grad_out, state_kept, grad_kept, sems):
    pieces = state.shape[0]
    into = [pltpu.make_async_copy(grad, grad_kept, sems.at[0])]
    back = [pltpu.make_async_copy(grad_kept, grad_out, sems.at[1])]
    for at in range(pieces):
        into.append(pltpu.make_async_copy(state.at[at], state_kept.at[at], sems.at[2 + 2 * at]))
        back.append(
            pltpu.make_async_copy(state_kept.at[at], state_out.at[at], sems.at[3 + 2 * at])
        )
    for copy in into:
        copy.start()
    for arrival, leave in zip(into, back):
        arrival.wait()
        leave.start()
    for copy in back:
        copy.wait()


def body(adjoint, saved, propagators, coupling, higher, lower, ladder, rates, decay):
    nodes = lax.axis_size("node")
    cores = lax.axis_size("cores")
    owners = nodes * cores
    count = adjoint.shape[0]
    modes = higher.shape[1]
    steps, subs = propagators.shape[:2]
    dim = coupling.shape[0]
    depth = 1 << (cores.bit_length() // 2)
    width = cores // depth
    pair = 2 if nodes % 2 == 0 else 1
    chips = nodes // pair * width
    pieces = 2
    rows = dim // owners
    halves = 2 if subs % 2 == 0 else 1
    batch = subs // halves
    higher, lower, ladder = higher.T, lower.T, jnp.swapaxes(ladder, 1, 2)
    vmem = pl.BlockSpec(memory_space=pltpu.VMEM)
    block = adjoint.shape
    hbm = pl.BlockSpec(memory_space=pl.ANY)
    hops = max(depth - 1, 1)
    others = max(chips - 1, 1)
    mates = max(pair - 1, 1)
    half = (count,) + block[2:]
    bit = (count // pieces,) + block[2:]
    tall = nodes // pair
    before = max(steps - 1, 1)
    slab = (subs * rows, 2 * dim)
    table = (depth + chips) * count * 2 * modes
    dma = pltpu.SemaphoreType.DMA
    state, grad = pl.pallas_call(
        functools.partial(kernel, (nodes, depth, width, pair, count, modes, steps, subs, dim, halves, pieces)),
        out_shape=(
            jax.ShapeDtypeStruct(block, BF16),
            jax.ShapeDtypeStruct((rows, steps * subs, 2, dim), F32),
        ),
        in_specs=[hbm] * 9,
        out_specs=(hbm, vmem),
        scratch_shapes=[
            pltpu.VMEM((steps * subs, 2 * dim, 2 * dim), BF16),
            pltpu.VMEM((steps * subs, 2 * dim, 2 * dim), BF16),
            pltpu.VMEM((steps, 2) + block, BF16),
            pltpu.VMEM((steps, depth) + half, BF16),
            pltpu.VMEM((steps, 2, depth) + half, BF16),
            pltpu.VMEM((steps, chips) + half, BF16),
            pltpu.VMEM((steps, max(width - 1, 1), tall) + bit, BF16),
            pltpu.VMEM((steps, max(tall - 1, 1), width) + bit, BF16),
            pltpu.VMEM((steps, max(width - 1, 1)) + bit, BF16),
            pltpu.VMEM((steps, max(tall - 1, 1)) + bit, BF16),
            pltpu.VMEM((steps * subs, dim, 2 * dim), F32),
            pltpu.VMEM((halves, owners, batch * rows, 2 * dim), BF16),
            pltpu.VMEM((halves, owners - 1, batch * rows, 2 * dim), BF16),
            pltpu.VMEM(saved.shape, BF16),
            pltpu.VMEM((steps, subs, 2 * dim, count * dim), BF16),
            pltpu.SMEM((table,), jnp.int32),
            pltpu.SMEM((table,), F32),
            pltpu.SMEM((2, owners), jnp.int32),
            pltpu.SMEM((2, owners), F32),
            pltpu.SMEM((depth + chips, 2, modes, count), jnp.int32),
            dma((steps,)),
            dma((steps, others, pieces)),
            dma((steps,)),
            dma((steps,)),
            dma((steps,)),
            dma((steps, depth, pieces)),
            dma((steps,)),
            dma((steps,)),
            dma((steps,)),
            dma((steps, depth + 1, pieces)),
            dma((steps,)),
            dma((steps, max(width - 1, 1), tall)),
            dma((steps, max(tall - 1, 1), width)),
            dma((steps, max(width - 1, 1))),
            dma((steps, max(tall - 1, 1))),
            dma(()),
            dma(()),
            dma((halves,)),
            dma((halves,)),
            pltpu.SemaphoreType.REGULAR,
            pltpu.SemaphoreType.REGULAR,
            dma((6,)),
            pltpu.VMEM(propagators.shape, BF16),
            pltpu.VMEM(block, BF16),
            pltpu.VMEM(coupling.shape, BF16),
            pltpu.SMEM(higher.shape, jnp.int32),
            pltpu.SMEM(lower.shape, jnp.int32),
            pltpu.SMEM(ladder.shape, jnp.int32),
            pltpu.SMEM(rates.shape, F32),
            pltpu.SMEM(decay.shape, F32),
            dma((6,)),
            pltpu.VMEM((before, pair, width, tall, depth) + slab, BF16),
            pltpu.VMEM((before, width, tall, depth) + slab, BF16),
            pltpu.VMEM((before, max(width - 1, 1), tall, depth) + slab, BF16),
            pltpu.VMEM((before, max(tall - 1, 1), depth) + slab, BF16),
            pltpu.VMEM((before, depth) + slab, BF16),
            dma((before, 4)),
            dma((before, 3, max(width - 1, tall - 1, 1))),
            dma((before,)),
            *[pltpu.VMEM((chips * pair * count, dim, dim), BF16)] * steps,
            *[pltpu.VMEM((depth * pair * count, dim, dim), BF16)] * steps,
        ],
        compiler_params=pltpu.CompilerParams(
            collective_id=0, has_side_effects=True, vmem_limit_bytes=63_000_000
        ),
    )(higher, lower, ladder, rates, decay, adjoint, saved, propagators, coupling)
    return pl.pallas_call(
        deliver,
        out_shape=(
            jax.ShapeDtypeStruct(state.shape, state.dtype),
            jax.ShapeDtypeStruct(grad.shape, grad.dtype),
        ),
        in_specs=[hbm, hbm],
        out_specs=(hbm, hbm),
        scratch_shapes=[
            pltpu.VMEM(state.shape, state.dtype),
            pltpu.VMEM(grad.shape, grad.dtype),
            dma((2 + 2 * state.shape[0],)),
        ],
    )(state, grad)


def solution(mesh):
    return jax.shard_map(
        body,
        mesh=mesh,
        in_specs=(
            P(("node", "cores"), None, None, None),
            P(None, None, ("node", "cores"), None, None, None),
            P(),
            P(),
            P(),
            P(),
            P(None, ("node", "cores"), None),
            P(),
            P(("node", "cores")),
        ),
        out_specs=(P(("node", "cores"), None, None, None), P(("node", "cores"), None, None, None)),
        check_vma=False,
    )
```
